32 devices in a mesh: rep: 4 (over z), shard: 8 (over y, x, core).
Axes of the slice: x: 2, y: 2, z: 4, core: 2. Of those that a mesh axis runs over, the one named last changes fastest.
Arguments:
- tokens: bfloat16 [4096, 2048], P(('rep', 'shard')), may hold values from -6 to 6
- segments: int32 [4096], P(('rep', 'shard')), may hold values from 0 to 127, never falling along the last dimension, each value on 1 to 128 neighbouring positions
- routes: int32 [4096, 8], P(('rep', 'shard')), may hold values from 0 to 9, as said below
- slot_ids: int32 [4096, 8], P(('rep', 'shard')), may hold values from 0 to 127, as said below
- attn_gain: float32 [2048], P('shard'), may hold values from 0.25 to 1.75
- w_query: float32 [2048, 2048], P('shard'), may hold values from -0.125 to 0.125
- w_key: float32 [2048, 2048], P('shard'), may hold values from -0.125 to 0.125
- w_value: float32 [2048, 2048], P('shard'), may hold values from -0.125 to 0.125
- w_out: float32 [2048, 2048], P('shard'), may hold values from -0.375 to 0.375
- query_gain: float32 [128], P('shard'), may hold values from 0.25 to 1.75
- key_gain: float32 [128], P('shard'), may hold values from 0.25 to 1.75
- ffn_gain: float32 [2048], P('shard'), may hold values from 0.25 to 1.75
- router: float32 [2048, 10], P('shard'), may hold values from -0.0625 to 0.0625
- w_gate: float32 [10, 2048, 1024], P(None, 'shard'), may hold values from -0.125 to 0.125
- w_up: float32 [10, 2048, 1024], P(None, 'shard'), may hold values from -0.125 to 0.125
- w_down: float32 [10, 1024, 2048], P(None, 'shard'), may hold values from -0.75 to 0.75
- cotangent: bfloat16 [4096, 2048], P(('rep', 'shard')), may hold values from -6 to 6
Outputs:
- output: bfloat16 [4096, 2048], P(('rep', 'shard'))
- grad_tokens: float32 [4096, 2048], P(('rep', 'shard'))
- grad_attn_gain: float32 [2048], P('shard')
- grad_w_query: float32 [2048, 2048], P('shard')
- grad_w_key: float32 [2048, 2048], P('shard')
- grad_w_value: float32 [2048, 2048], P('shard')
- grad_w_out: float32 [2048, 2048], P('shard')
- grad_query_gain: float32 [128], P('shard')
- grad_key_gain: float32 [128], P('shard')
- grad_ffn_gain: float32 [2048], P('shard')
- grad_router: float32 [2048, 10], P('shard')
- grad_w_gate: float32 [10, 2048, 1024], P(None, 'shard')
- grad_w_up: float32 [10, 2048, 1024], P(None, 'shard')
- grad_w_down: float32 [10, 1024, 2048], P(None, 'shard')
The draws below stay inside these ranges and needn't reach their ends.
Inputs may be any that keep to these rules, and one draw needn't show every extreme that they name: `routes`: each row names 8 different experts; in the rows of each sequence of 128 tokens one expert is named by every row. `slot_ids`: within one sequence of 128 tokens, the routes to one expert hold the slots 0 to their count - 1, each once. `segments`: segment numbers never fall along the tokens.
All inputs are finite; a program needn't handle non-finite values.
Results may differ from the reference program's by a relative error of at most 0.018.
The reference program's roundings to bfloat16 on the way count: a program that leaves them out, or rounds other values in their place, can miss the bound.
Values may be sent and summed in bfloat16 or wider, within the bound.
A program may use at most 320 MiB of HBM per device.

```python
import math
from functools import partial
import jax
import jax.numpy as jnp
import numpy as np
from jax import lax

D = 2048
HEADS = 16
HEAD_DIM = 128
F = 1024
EXPERTS = 10
TOP = 8
SEQ = 128
TOKENS = 4096


def route_table(key):
    seq_count = TOKENS // SEQ
    base_key = jax.random.fold_in(key, 17)
    noise_key, bias_key, forced_key, order_key = jax.random.split(base_key, 4)
    random_noise_values = jax.random.randint(noise_key, (seq_count, SEQ, EXPERTS), 0, 65536)
    expert_offset_bias = jax.random.randint(bias_key, (seq_count, 1, EXPERTS), 0, 65536)
    forced_choice = jax.random.randint(forced_key, (seq_count, 1, 1), 0, EXPERTS)
    target_labels = jnp.arange(EXPERTS, dtype=jnp.int32)[None, None, :]
    extra_reward = (target_labels == forced_choice).astype(jnp.int32) * 1048576
    routing_score = (random_noise_values + expert_offset_bias + extra_reward) * 16 + target_labels
    _, chosen = lax.top_k(routing_score, TOP)
    chosen = chosen.astype(jnp.int32)
    priority = jax.random.randint(order_key, (seq_count, SEQ), 0, 4096) * SEQ + jnp.arange(SEQ, dtype=jnp.int32)[None, :]
    order_perm = jnp.argsort(priority, axis=1, stable=True).astype(jnp.int32)
    inverse_perm = jnp.argsort(order_perm, axis=1, stable=True).astype(jnp.int32)
    route_hits = jnp.sum((chosen[:, :, :, None] == target_labels[:, :, None, :]).astype(jnp.int32), axis=2)
    ordered = jnp.take_along_axis(route_hits, jnp.broadcast_to(order_perm[:, :, None], route_hits.shape), axis=1)
    before_count = jnp.cumsum(ordered, axis=1) - ordered
    before_count = jnp.take_along_axis(before_count, jnp.broadcast_to(inverse_perm[:, :, None], route_hits.shape), axis=1)
    slot_table = jnp.take_along_axis(before_count, chosen, axis=2)
    return (chosen.reshape(TOKENS, TOP), slot_table.reshape(TOKENS, TOP).astype(jnp.int32))


def draw_routes(key, part):
    return route_table(key)[0]


def draw_slot_ids(key, part):
    return route_table(key)[1]


def block_levels(key, extent, shards, least, top_value):
    def one(dim, shards_of):
        steps = jax.random.uniform(jax.random.fold_in(jax.random.fold_in(key, 6), dim), (shards_of,), jnp.float32, least / len(shards), top_value / len(shards))
        return jnp.repeat(jnp.exp(steps), extent[dim] // shards_of).reshape((-1,) + (1,) * (len(extent) - dim - 1))

    loudness = one(*shards[0])
    for cut in shards[1:]:
        loudness = loudness * one(*cut)
    return loudness


def profile(number_of, total, limit, skew):
    portions = [(1 << 20) // math.isqrt(grade ** skew) + 1 for grade in range(2, number_of + 1)]
    spare, holding = total - limit - (number_of - 1), [1] * (number_of - 1)
    while spare > 0:
        free = [i for i in range(number_of - 1) if holding[i] < limit]
        pool, left = sum([portions[i] for i in free]), spare
        for i in free:
            addition = min(limit - holding[i], max(1, left * portions[i] // pool), spare)
            holding[i] = holding[i] + addition
            spare = spare - addition
    return np.array([limit] + holding)


def ragged_sizes(rng, count, total, bound, lean):
    if count == 2:
        one = jax.random.randint(rng, (), max(1, total - bound), min(bound, total - 1) + 1)
        return jnp.stack([one, total - one])
    sizes = jnp.asarray(profile(count, total, bound, lean), jnp.int32)
    pairs = (count - 1) // 2
    source_of, sink = sizes[1:1 + 2 * pairs:2], sizes[2:2 + 2 * pairs:2]
    slack = jnp.minimum(source_of - 1, bound - sink)
    passed = jax.random.randint(jax.random.fold_in(rng, 1), (pairs,), 0, 1 << 20) % (slack + 1)
    sizes = sizes.at[1:1 + 2 * pairs:2].set(source_of - passed).at[2:2 + 2 * pairs:2].set(sink + passed)
    return sizes[jax.random.permutation(jax.random.fold_in(rng, 2), count)]


def normal_values(stream_key, shape, scale, most, pieces=(), kind=jnp.bfloat16):
    values = scale * jax.random.normal(stream_key, shape, jnp.float32)
    if pieces:
        values = values * block_levels(stream_key, shape, pieces, -0.22, 0.18)
    return jnp.clip(values, -most, most).astype(kind)


def setup_inputs(seed: int = 0) -> dict:
    seeds = jax.random.split(jax.random.key(seed), 18)
    return {
        "tokens": normal_values(seeds[0], (TOKENS, D), 1.0, 6.0, ((0, 32),)),
        "segments": jnp.searchsorted(jnp.cumsum(ragged_sizes(seeds[1], TOKENS // (SEQ // 4), TOKENS, SEQ, 2)), jnp.arange(TOKENS), side="right").astype(jnp.int32),
        "routes": draw_routes(jax.random.fold_in(seeds[17], 71), 0),
        "slot_ids": draw_slot_ids(jax.random.fold_in(seeds[17], 71), 0),
        "attn_gain": jnp.clip(1.0 + 0.15 * jax.random.normal(seeds[4], (D,), jnp.float32), 0.25, 1.75),
        "w_query": normal_values(seeds[5], (D, D), D ** -0.5, 0.125, ((0, 8),), jnp.float32),
        "w_key": normal_values(seeds[6], (D, D), D ** -0.5, 0.125, ((0, 8),), jnp.float32),
        "w_value": normal_values(seeds[7], (D, D), D ** -0.5, 0.125, ((0, 8),), jnp.float32),
        "w_out": normal_values(seeds[8], (D, D), (D // 8) ** -0.5, 0.375, ((0, 8),), jnp.float32),
        "query_gain": jnp.clip(1.0 + 0.15 * jax.random.normal(seeds[9], (HEAD_DIM,), jnp.float32), 0.25, 1.75),
        "key_gain": jnp.clip(1.0 + 0.15 * jax.random.normal(seeds[10], (HEAD_DIM,), jnp.float32), 0.25, 1.75),
        "ffn_gain": jnp.clip(1.0 + 0.15 * jax.random.normal(seeds[11], (D,), jnp.float32), 0.25, 1.75),
        "router": normal_values(seeds[12], (D, EXPERTS), (4 * D) ** -0.5, 0.0625, ((0, 8),), jnp.float32),
        "w_gate": normal_values(seeds[13], (EXPERTS, D, F), D ** -0.5, 0.125, ((1, 8),), jnp.float32),
        "w_up": normal_values(seeds[14], (EXPERTS, D, F), D ** -0.5, 0.125, ((1, 8),), jnp.float32),
        "w_down": normal_values(seeds[15], (EXPERTS, F, D), (F // 16) ** -0.5, 0.75, ((1, 8),), jnp.float32),
        "cotangent": normal_values(seeds[16], (TOKENS, D), 1.0, 6.0, ((0, 32),)),
    }


epsilon = 1e-06
rope_base = 50000.0
highest = lax.Precision.HIGHEST

@jax.custom_vjp
def low(v):
    return lax.optimization_barrier(v.astype(jnp.bfloat16)).astype(jnp.float32)

@jax.custom_vjp
def low_back(v):
    return v

def low_keep(v):
    return (low(v), None)

def low_pass(kept, grad):
    return (grad,)

def back_keep(v):
    return (v, None)

def back_low(kept, grad):
    return (low(grad),)
low.defvjp(low_keep, low_pass)
low_back.defvjp(back_keep, back_low)

def rms_scale(value, scale_gain):
    return value * lax.rsqrt(lax.optimization_barrier(jnp.mean(value * value, axis=-1, keepdims=True)) + epsilon) * scale_gain

def rotate(value):
    half_dim = value.shape[-1] // 2
    position = jnp.arange(value.shape[1], dtype=jnp.float32)
    frequency = rope_base ** (-jnp.arange(half_dim, dtype=jnp.float32) * 2.0 / value.shape[-1])
    angles = position[:, None] * frequency[None, :]
    cosine = jnp.cos(angles)[:, None, :]
    sine_table = jnp.sin(angles)[:, None, :]
    first_half = value[..., :half_dim]
    second_half = value[..., half_dim:]
    return jnp.concatenate([first_half * cosine - second_half * sine_table, second_half * cosine + first_half * sine_table], axis=-1)

def dispatch(row_values, places):
    seq_len = row_values.shape[0]
    spread = jnp.broadcast_to(row_values[:, None, :], (seq_len, TOP, D)).reshape(seq_len * TOP, D)
    return jnp.zeros((EXPERTS * seq_len, D), jnp.float32).at[places.reshape(-1)].set(spread)

def collect(row_values, places):
    return row_values[places]

def layer_block(lowered, hidden, segment, route, slot):
    attn_gain, w_query, w_key, w_value, w_out, query_gain, key_gain, ffn_gain, router, w_gate, w_up, w_down = lowered
    batch_size, seq_len, _ = hidden.shape
    normed = low(rms_scale(hidden, attn_gain))
    queries = low_back(jnp.einsum('bsd,de->bse', normed, w_query, precision=highest)).reshape(batch_size, seq_len, HEADS, HEAD_DIM)
    key_rows = low_back(jnp.einsum('bsd,de->bse', normed, w_key, precision=highest)).reshape(batch_size, seq_len, HEADS, HEAD_DIM)
    values = low(low_back(jnp.einsum('bsd,de->bse', normed, w_value, precision=highest))).reshape(batch_size, seq_len, HEADS, HEAD_DIM)
    query_rot = low(rotate(rms_scale(queries, query_gain)))
    key_rot = low(rotate(rms_scale(key_rows, key_gain)))
    scores = low_back(jnp.einsum('bqhd,bkhd->bhqk', query_rot, key_rot, precision=highest) * HEAD_DIM ** (-0.5))
    same_doc = (segment[:, :, None] == segment[:, None, :])[:, None, :, :]
    scores = jnp.where(same_doc, scores, -1000000000.0)
    attn_probs = low(jax.nn.softmax(scores, axis=-1))
    mixed_out = low(low_back(jnp.einsum('bhqk,bkhd->bqhd', attn_probs, values, precision=highest))).reshape(batch_size, seq_len, D)
    attended = hidden + low_back(jnp.einsum('bsd,de->bse', mixed_out, w_out, precision=highest))
    routed = low(rms_scale(attended, ffn_gain))
    logits = low_back(jnp.einsum('bsd,de->bse', routed, router, precision=highest))
    router_probs = jax.nn.softmax(logits, axis=-1)
    route_gates = jnp.take_along_axis(router_probs, route, axis=-1)
    flat_index = route * seq_len + slot
    buffer = jax.vmap(dispatch)(routed, flat_index).reshape(batch_size, EXPERTS, seq_len, D)
    gate_pre = low_back(jnp.einsum('becd,edf->becf', buffer, w_gate, precision=highest))
    up_pre = low_back(jnp.einsum('becd,edf->becf', buffer, w_up, precision=highest))
    inner_act = low(jax.nn.silu(gate_pre) * up_pre)
    expert_rows = low_back(jnp.einsum('becf,efd->becd', inner_act, w_down, precision=highest)).reshape(batch_size, EXPERTS * seq_len, D)
    picked = jax.vmap(collect)(expert_rows, flat_index)
    return attended + lax.optimization_barrier(jnp.sum(route_gates[..., None] * picked, axis=2))

def reference(tokens, segments, routes, slot_ids, attn_gain, w_query, w_key, w_value, w_out, query_gain, key_gain, ffn_gain, router, w_gate, w_up, w_down, cotangent):
    masters = (attn_gain, w_query, w_key, w_value, w_out, query_gain, key_gain, ffn_gain, router, w_gate, w_up, w_down)
    seq_count = tokens.shape[0] // SEQ
    group_size = 8
    rounds = seq_count // group_size
    seg_groups = segments.reshape(rounds, group_size, SEQ)
    route_groups = routes.reshape(rounds, group_size, SEQ, TOP)
    slot_groups = slot_ids.reshape(rounds, group_size, SEQ, TOP)

    def forward(hidden, params):
        lowered = tuple((low(p) for p in params))
        stacked = hidden.reshape(rounds, group_size, SEQ, D)
        block_fn = jax.checkpoint(partial(layer_block, lowered))

        def scan_step(unused, scan_item):
            return (unused, block_fn(scan_item[0], scan_item[1], scan_item[2], scan_item[3]))
        _, result = lax.scan(scan_step, None, (stacked, seg_groups, route_groups, slot_groups))
        return result.reshape(-1, D)
    result, pull_back = jax.vjp(forward, tokens.astype(jnp.float32), masters)
    grad_in, weight_grads = pull_back(cotangent.astype(jnp.float32))
    return (result.astype(jnp.bfloat16), grad_in, weight_grads[0], weight_grads[1], weight_grads[2], weight_grads[3], weight_grads[4], weight_grads[5], weight_grads[6], weight_grads[7], weight_grads[8], weight_grads[9], weight_grads[10], weight_grads[11])
```

```python
import jax
import jax.numpy as jnp
from jax import lax
from jax.sharding import PartitionSpec as P

HEAD_DIM = 128

epsilon = 1e-06
rope_base = 50000.0
BF = jnp.bfloat16
F32 = jnp.float32


def inverse_rms(value):
    return lax.rsqrt(jnp.mean(value * value, axis=-1, keepdims=True) + epsilon)


def rope_tables(seq_len, head_width):
    half_dim = head_width // 2
    position = jnp.arange(seq_len, dtype=jnp.float32)
    frequency = rope_base ** (-jnp.arange(half_dim, dtype=jnp.float32) * 2.0 / head_width)
    angles = position[:, None] * frequency[None, :]
    return (jnp.cos(angles)[:, None, :], jnp.sin(angles)[:, None, :])


def rotate(value, cosine, sine_table, direction):
    half_dim = value.shape[-1] // 2
    first_half = value[..., :half_dim]
    second_half = value[..., half_dim:]
    return jnp.concatenate(
        [
            first_half * cosine - direction * second_half * sine_table,
            second_half * cosine + direction * first_half * sine_table,
        ],
        axis=-1,
    )


def head_back(grad_rot, value_hat, inverse, scale_gain, cosine, sine_table):
    grad_scaled = rotate(grad_rot, cosine, sine_table, -1.0)
    grad_gain = jnp.sum(grad_scaled * value_hat, axis=(0, 1, 2))
    grad_hat = grad_scaled * scale_gain
    grad_value = inverse * (
        grad_hat - value_hat * jnp.mean(grad_hat * value_hat, axis=-1, keepdims=True)
    )
    return (grad_value.astype(BF), grad_gain)


def dot(a, b, dims):
    return lax.dot_general(a, b, (dims, ((), ())), preferred_element_type=F32)


def shards(
    tokens, segments, routes, slot_ids, attn_gain, w_query, w_key, w_value, w_out,
    query_gain, key_gain, ffn_gain, router, w_gate, w_up, w_down, cotangent,
):
    n_shard = lax.axis_size("shard")
    me = lax.axis_index("shard")
    seq, width = tokens.shape
    experts, rows, hidden_f = w_gate.shape
    f_loc = w_down.shape[1]
    cols = width // n_shard
    heads = cols // HEAD_DIM
    group = n_shard * seq
    scale = HEAD_DIM ** (-0.5)

    def gather(x, axis=0):
        return lax.all_gather(x, "shard", axis=axis, tiled=True)

    def scatter(x):
        return lax.psum_scatter(x, "shard", scatter_dimension=0, tiled=True)

    qkv_rows = jnp.stack([w_query, w_key, w_value]).astype(BF)
    qkv = lax.all_to_all(qkv_rows, "shard", split_axis=2, concat_axis=1, tiled=True)
    w_out_b = w_out.astype(BF)
    gu_rows = jnp.concatenate([w_gate, w_up]).astype(BF)
    gu = lax.all_to_all(gu_rows, "shard", split_axis=2, concat_axis=1, tiled=True)
    w_down_b = w_down.astype(BF)
    gains = gather(jnp.concatenate([attn_gain, ffn_gain, query_gain, key_gain]).astype(BF)[None])
    g_attn = gains[:, :rows].reshape(width).astype(F32)
    g_ffn = gains[:, rows : 2 * rows].reshape(width).astype(F32)
    hd = HEAD_DIM // n_shard
    g_query = gains[:, 2 * rows : 2 * rows + hd].reshape(HEAD_DIM).astype(F32)
    g_key = gains[:, 2 * rows + hd :].reshape(HEAD_DIM).astype(F32)
    router_b = gather(router.astype(BF))
    dy_all = gather(cotangent)
    seg_all = gather(segments).reshape(n_shard, seq)

    h = tokens.astype(F32)
    r1 = inverse_rms(h)
    n1 = h * r1
    x1 = (n1 * g_attn).astype(BF)
    x1_all = gather(x1)
    split = (n_shard, seq, heads, HEAD_DIM)
    q = dot(x1_all, qkv[0], ((1,), (0,))).reshape(split)
    k = dot(x1_all, qkv[1], ((1,), (0,))).reshape(split)
    v = dot(x1_all, qkv[2], ((1,), (0,))).astype(BF).reshape(split)
    cosine, sine = rope_tables(seq, HEAD_DIM)
    rq = inverse_rms(q)
    q_hat = q * rq
    qr = rotate(q_hat * g_query, cosine, sine, 1.0).astype(BF)
    rk = inverse_rms(k)
    k_hat = k * rk
    kr = rotate(k_hat * g_key, cosine, sine, 1.0).astype(BF)
    same = (seg_all[:, :, None] == seg_all[:, None, :])[:, None]
    s = jnp.einsum("bqhd,bkhd->bhqk", qr, kr, preferred_element_type=F32) * scale
    s = jnp.where(same, s, -1000000000.0)
    top = jnp.max(s, axis=-1, keepdims=True)
    e = jnp.exp(s - top)
    probs = e / jnp.sum(e, axis=-1, keepdims=True)
    probs_b = probs.astype(BF)
    a = (
        jnp.einsum("bhqk,bkhd->bqhd", probs_b, v, preferred_element_type=F32)
        .astype(BF)
        .reshape(group, cols)
    )
    h1 = h + scatter(dot(a, w_out_b, ((1,), (0,))).astype(BF)).astype(F32)
    r2 = inverse_rms(h1)
    n2 = h1 * r2
    x2 = (n2 * g_ffn).astype(BF)
    pr = jax.nn.softmax(dot(x2, router_b, ((1,), (0,))), axis=-1)
    hit = jnp.sum(
        (routes[:, :, None] == jnp.arange(experts, dtype=jnp.int32)).astype(F32), axis=1
    )
    gate = pr * hit
    x2_all = gather(x2)
    gate_all = gather(gate)

    dy = cotangent.astype(F32)
    gus = gu.reshape(2, experts, width, f_loc)
    g_pre = jnp.einsum("td,edf->etf", x2_all, gus[0], preferred_element_type=F32)
    u_pre = jnp.einsum("td,edf->etf", x2_all, gus[1], preferred_element_type=F32)
    z_pre = jnp.einsum("td,efd->etf", dy_all, w_down_b, preferred_element_type=F32)
    gate_t = gate_all.T[:, :, None]
    sig = jax.nn.sigmoid(g_pre)
    act = g_pre * sig
    hh = act * u_pre
    dgate_part = jnp.sum(hh.astype(BF).astype(F32) * z_pre, axis=-1).T
    gh = (gate_t * hh).astype(BF)
    dh = gate_t * z_pre
    d_gate = (dh * u_pre * sig * (1.0 + g_pre * (1.0 - sig))).astype(BF)
    d_up = (dh * act).astype(BF)
    out_part = jnp.einsum("etf,efd->td", gh, w_down_b, preferred_element_type=F32)
    output = (h1 + scatter(out_part.astype(BF)).astype(F32)).astype(BF)
    dgate = scatter(dgate_part)
    dx2_part = jnp.einsum("etf,edf->td", d_gate, gus[0], preferred_element_type=F32) + jnp.einsum(
        "etf,edf->td", d_up, gus[1], preferred_element_type=F32
    )
    gw_down = jnp.einsum("etf,td->efd", gh, dy_all, preferred_element_type=F32).astype(BF)
    gw_gate = jnp.einsum("td,etf->edf", x2_all, d_gate, preferred_element_type=F32).astype(BF)
    gw_up = jnp.einsum("td,etf->edf", x2_all, d_up, preferred_element_type=F32).astype(BF)
    gw_gu = lax.all_to_all(
        jnp.concatenate([gw_gate, gw_up]), "shard", split_axis=1, concat_axis=2, tiled=True
    )
    gw_gu = lax.psum(gw_gu, "rep").astype(F32)
    gw_down = lax.psum(gw_down, "rep").astype(F32)

    dpr = dgate * hit
    dz = (pr * (dpr - jnp.sum(pr * dpr, axis=-1, keepdims=True))).astype(BF)
    gw_router = scatter(dot(x2, dz, ((0,), (0,))))
    dx2 = scatter(dx2_part.astype(BF)).astype(F32) + dot(dz, router_b, ((1,), (1,)))
    gg_ffn = jnp.sum(dx2 * n2, axis=0)
    e2 = dx2 * g_ffn
    dh1 = dy + r2 * (e2 - n2 * jnp.mean(e2 * n2, axis=-1, keepdims=True))

    da_all = gather(dh1.astype(BF))
    gw_out = dot(a, da_all, ((0,), (0,)))
    do = dot(da_all, w_out_b, ((1,), (1,))).astype(BF).reshape(split)
    dv = jnp.einsum("bhqk,bqhd->bkhd", probs_b, do, preferred_element_type=F32).astype(BF)
    dp = jnp.einsum("bqhd,bkhd->bhqk", do, v, preferred_element_type=F32)
    ds = (probs * (dp - jnp.sum(probs * dp, axis=-1, keepdims=True))).astype(BF)
    dqr = jnp.einsum("bhqk,bkhd->bqhd", ds, kr, preferred_element_type=F32) * scale
    dkr = jnp.einsum("bhqk,bqhd->bkhd", ds, qr, preferred_element_type=F32) * scale
    dq, gg_query = head_back(dqr, q_hat, rq, g_query, cosine, sine)
    dk, gg_key = head_back(dkr, k_hat, rk, g_key, cosine, sine)
    d_qkv = jnp.stack([x.reshape(group, cols) for x in (dq, dk, dv)])
    gw_qkv = jnp.einsum("td,wtc->wdc", x1_all, d_qkv, preferred_element_type=F32).astype(BF)
    gw_qkv = lax.all_to_all(gw_qkv, "shard", split_axis=1, concat_axis=2, tiled=True)
    dx1 = scatter(
        jnp.einsum("wtc,wdc->td", d_qkv, qkv, preferred_element_type=F32).astype(BF)
    ).astype(F32)
    gg_attn = jnp.sum(dx1 * n1, axis=0)
    e1 = dx1 * g_attn
    grad_tokens = dh1 + r1 * (e1 - n1 * jnp.mean(e1 * n1, axis=-1, keepdims=True))

    def own(x):
        return x.reshape(n_shard, -1)

    small = scatter(
        jnp.concatenate([own(gg_attn), own(gg_ffn), own(gg_query), own(gg_key)], axis=1)
    )[0]
    small = lax.psum(jnp.concatenate([small, gw_router.reshape(-1)]), "rep")
    gw_qkv = lax.psum(gw_qkv, "rep").astype(F32)
    gw_out = lax.psum(gw_out.astype(BF), "rep").astype(F32)
    c = [0, rows, 2 * rows, 2 * rows + hd, 2 * rows + 2 * hd]
    return (
        output,
        grad_tokens,
        small[: c[1]],
        gw_qkv[0],
        gw_qkv[1],
        gw_qkv[2],
        gw_out,
        small[c[2] : c[3]],
        small[c[3] : c[4]],
        small[c[1] : c[2]],
        small[c[4] :].reshape(rows, experts),
        gw_gu[:experts],
        gw_gu[experts:],
        gw_down,
    )


def solution(mesh):
    both = P(("rep", "shard"), None)
    row = P("shard", None)
    vec = P("shard")
    exp = P(None, "shard", None)
    return jax.shard_map(
        shards,
        mesh=mesh,
        in_specs=(
            both, P(("rep", "shard")), both, both, vec, row, row, row, row,
            vec, vec, vec, row, exp, exp, exp, both,
        ),
        out_specs=(both, both, vec, row, row, row, row, vec, vec, vec, row, exp, exp, exp),
        check_vma=False,
    )
```

```python
import jax
import jax.numpy as jnp
from jax import lax
from jax.sharding import PartitionSpec as P

HEAD_DIM = 128

epsilon = 1e-06
rope_base = 50000.0
BF = jnp.bfloat16
F32 = jnp.float32


def inverse_rms(value):
    return lax.rsqrt(jnp.mean(value * value, axis=-1, keepdims=True) + epsilon)


def rope_tables(seq_len, head_width):
    half_dim = head_width // 2
    position = jnp.arange(seq_len, dtype=jnp.float32)
    frequency = rope_base ** (-jnp.arange(half_dim, dtype=jnp.float32) * 2.0 / head_width)
    angles = position[:, None] * frequency[None, :]
    return (jnp.cos(angles)[:, None, :], jnp.sin(angles)[:, None, :])


def rotate(value, cosine, sine_table, direction):
    half_dim = value.shape[-1] // 2
    first_half = value[..., :half_dim]
    second_half = value[..., half_dim:]
    return jnp.concatenate(
        [
            first_half * cosine - direction * second_half * sine_table,
            second_half * cosine + direction * first_half * sine_table,
        ],
        axis=-1,
    )


def head_back(grad_rot, value_hat, inverse, scale_gain, cosine, sine_table):
    grad_scaled = rotate(grad_rot, cosine, sine_table, -1.0)
    grad_gain = jnp.sum(grad_scaled * value_hat, axis=(0, 1, 2))
    grad_hat = grad_scaled * scale_gain
    grad_value = inverse * (
        grad_hat - value_hat * jnp.mean(grad_hat * value_hat, axis=-1, keepdims=True)
    )
    return (grad_value.astype(BF), grad_gain)


def dot(a, b, dims):
    return lax.dot_general(a, b, (dims, ((), ())), preferred_element_type=F32)


def shards(
    tokens, segments, routes, slot_ids, attn_gain, w_query, w_key, w_value, w_out,
    query_gain, key_gain, ffn_gain, router, w_gate, w_up, w_down, cotangent,
):
    n_shard = lax.axis_size("shard")
    me = lax.axis_index("shard")
    seq, width = tokens.shape
    experts, rows, hidden_f = w_gate.shape
    f_loc = w_down.shape[1]
    cols = width // n_shard
    heads = cols // HEAD_DIM
    group = n_shard * seq
    scale = HEAD_DIM ** (-0.5)

    def gather(x, axis=0):
        return lax.all_gather(x, "shard", axis=axis, tiled=True)

    def scatter(x):
        return lax.psum_scatter(x, "shard", scatter_dimension=0, tiled=True)

    n_rep = lax.axis_size("rep")

    def others(x):
        turn = lambda k: [(i, (i + k) % n_rep) for i in range(n_rep)]
        far = [lax.ppermute(x, "rep", turn(k)) for k in range(1, n_rep)]
        return gather(jnp.concatenate(far, axis=0)) if far else x[:0]

    qkv_rows = jnp.stack([w_query, w_key, w_value]).astype(BF)
    qkv = lax.all_to_all(qkv_rows, "shard", split_axis=2, concat_axis=1, tiled=True)
    w_out_b = w_out.astype(BF)
    gu_rows = jnp.concatenate([w_gate, w_up]).astype(BF)
    gu = lax.all_to_all(gu_rows, "shard", split_axis=2, concat_axis=1, tiled=True)
    w_down_b = w_down.astype(BF)
    gains = gather(jnp.concatenate([attn_gain, ffn_gain, query_gain, key_gain]).astype(BF)[None])
    g_attn = gains[:, :rows].reshape(width).astype(F32)
    g_ffn = gains[:, rows : 2 * rows].reshape(width).astype(F32)
    hd = HEAD_DIM // n_shard
    g_query = gains[:, 2 * rows : 2 * rows + hd].reshape(HEAD_DIM).astype(F32)
    g_key = gains[:, 2 * rows + hd :].reshape(HEAD_DIM).astype(F32)
    router_b = gather(router.astype(BF))
    dy_all = gather(cotangent)
    seg_all = gather(segments).reshape(n_shard, seq)
    hit = jnp.sum(
        (routes[:, :, None] == jnp.arange(experts, dtype=jnp.int32)).astype(F32), axis=1
    )
    hit_all = gather(hit.astype(BF)).astype(F32)
    hit_far = others(hit.astype(BF)).astype(F32)
    dy_far = others(cotangent)

    h = tokens.astype(F32)
    r1 = inverse_rms(h)
    n1 = h * r1
    x1 = (n1 * g_attn).astype(BF)
    x1_all = gather(x1)
    split = (n_shard, seq, heads, HEAD_DIM)
    q = dot(x1_all, qkv[0], ((1,), (0,))).reshape(split)
    k = dot(x1_all, qkv[1], ((1,), (0,))).reshape(split)
    v = dot(x1_all, qkv[2], ((1,), (0,))).astype(BF).reshape(split)
    cosine, sine = rope_tables(seq, HEAD_DIM)
    rq = inverse_rms(q)
    q_hat = q * rq
    qr = rotate(q_hat * g_query, cosine, sine, 1.0).astype(BF)
    rk = inverse_rms(k)
    k_hat = k * rk
    kr = rotate(k_hat * g_key, cosine, sine, 1.0).astype(BF)
    same = (seg_all[:, :, None] == seg_all[:, None, :])[:, None]
    s = jnp.einsum("bqhd,bkhd->bhqk", qr, kr, preferred_element_type=F32) * scale
    s = jnp.where(same, s, -1000000000.0)
    top = jnp.max(s, axis=-1, keepdims=True)
    e = jnp.exp(s - top)
    probs = e / jnp.sum(e, axis=-1, keepdims=True)
    probs_b = probs.astype(BF)
    a = (
        jnp.einsum("bhqk,bkhd->bqhd", probs_b, v, preferred_element_type=F32)
        .astype(BF)
        .reshape(group, cols)
    )
    h1 = h + scatter(dot(a, w_out_b, ((1,), (0,))).astype(BF)).astype(F32)
    r2 = inverse_rms(h1)
    n2 = h1 * r2
    x2 = (n2 * g_ffn).astype(BF)
    def gates(x, mask):
        p = jax.nn.softmax(dot(x, router_b, ((1,), (0,))), axis=-1)
        return (p, p * mask)

    pr, _ = gates(x2, hit)
    x2_all = gather(x2)
    x2_far = others(x2)

    dy = cotangent.astype(F32)
    gus = gu.reshape(2, experts, width, f_loc)

    def expert_pass(x, d, mask):
        g_pre = jnp.einsum("td,edf->etf", x, gus[0], preferred_element_type=F32)
        u_pre = jnp.einsum("td,edf->etf", x, gus[1], preferred_element_type=F32)
        z_pre = jnp.einsum("td,efd->etf", d, w_down_b, preferred_element_type=F32)
        gate = gates(x, mask)[1].T[:, :, None]
        sig = jax.nn.sigmoid(g_pre)
        act = g_pre * sig
        hh = act * u_pre
        part = jnp.sum(hh.astype(BF).astype(F32) * z_pre, axis=-1).T
        gh = (gate * hh).astype(BF)
        dh = gate * z_pre
        d_gate = (dh * u_pre * sig * (1.0 + g_pre * (1.0 - sig))).astype(BF)
        d_up = (dh * act).astype(BF)
        return (gh, d_gate, d_up, part)

    gh, d_gate, d_up, dgate_part = expert_pass(x2_all, dy_all, hit_all)
    dgate = scatter(dgate_part)
    dx2_part = jnp.einsum("etf,edf->td", d_gate, gus[0], preferred_element_type=F32) + jnp.einsum(
        "etf,edf->td", d_up, gus[1], preferred_element_type=F32
    )
    dx2_sum = scatter(dx2_part.astype(BF)).astype(F32)
    out_part = jnp.einsum("etf,efd->td", gh, w_down_b, preferred_element_type=F32)
    output = (h1 + scatter(out_part.astype(BF)).astype(F32)).astype(BF)
    gh_far, d_gate_far, d_up_far, _ = expert_pass(x2_far, dy_far, hit_far)

    def join(near, far):
        return jnp.concatenate([near, far], axis=-2)

    x2_every, dy_every = (join(x2_all, x2_far), join(dy_all, dy_far))
    gw_gate = jnp.einsum(
        "td,etf->edf", x2_every, join(d_gate, d_gate_far), preferred_element_type=F32
    ).astype(BF)
    gw_up = jnp.einsum(
        "td,etf->edf", x2_every, join(d_up, d_up_far), preferred_element_type=F32
    ).astype(BF)
    gw_down = jnp.einsum(
        "etf,td->efd", join(gh, gh_far), dy_every, preferred_element_type=F32
    )

    def back(x):
        return lax.all_to_all(x, "shard", split_axis=1, concat_axis=2, tiled=True).astype(F32)

    gw_gate, gw_up = (back(gw_gate), back(gw_up))

    dpr = dgate * hit
    dz = (pr * (dpr - jnp.sum(pr * dpr, axis=-1, keepdims=True))).astype(BF)
    gw_router = scatter(dot(x2, dz, ((0,), (0,))))
    dx2 = dx2_sum + dot(dz, router_b, ((1,), (1,)))
    gg_ffn = jnp.sum(dx2 * n2, axis=0)
    e2 = dx2 * g_ffn
    dh1 = dy + r2 * (e2 - n2 * jnp.mean(e2 * n2, axis=-1, keepdims=True))

    da_all = gather(dh1.astype(BF))
    gw_out = dot(a, da_all, ((0,), (0,)))
    do = dot(da_all, w_out_b, ((1,), (1,))).astype(BF).reshape(split)
    dv = jnp.einsum("bhqk,bqhd->bkhd", probs_b, do, preferred_element_type=F32).astype(BF)
    dp = jnp.einsum("bqhd,bkhd->bhqk", do, v, preferred_element_type=F32)
    ds = (probs * (dp - jnp.sum(probs * dp, axis=-1, keepdims=True))).astype(BF)
    dqr = jnp.einsum("bhqk,bkhd->bqhd", ds, kr, preferred_element_type=F32) * scale
    dkr = jnp.einsum("bhqk,bqhd->bkhd", ds, qr, preferred_element_type=F32) * scale
    dq, gg_query = head_back(dqr, q_hat, rq, g_query, cosine, sine)
    dk, gg_key = head_back(dkr, k_hat, rk, g_key, cosine, sine)
    d_qkv = jnp.stack([x.reshape(group, cols) for x in (dq, dk, dv)])
    gw_qkv = jnp.einsum("td,wtc->wdc", x1_all, d_qkv, preferred_element_type=F32).astype(BF)
    gw_qkv = lax.all_to_all(gw_qkv, "shard", split_axis=1, concat_axis=2, tiled=True)
    dx1 = scatter(
        jnp.einsum("wtc,wdc->td", d_qkv, qkv, preferred_element_type=F32).astype(BF)
    ).astype(F32)
    gg_attn = jnp.sum(dx1 * n1, axis=0)
    e1 = dx1 * g_attn
    grad_tokens = dh1 + r1 * (e1 - n1 * jnp.mean(e1 * n1, axis=-1, keepdims=True))

    def own(x):
        return x.reshape(n_shard, -1)

    small = scatter(
        jnp.concatenate([own(gg_attn), own(gg_ffn), own(gg_query), own(gg_key)], axis=1)
    )[0]
    small = lax.psum(jnp.concatenate([small, gw_router.reshape(-1)]), "rep")
    gw_qkv = lax.psum(gw_qkv, "rep").astype(F32)
    gw_out = lax.psum(gw_out.astype(BF), "rep").astype(F32)
    c = [0, rows, 2 * rows, 2 * rows + hd, 2 * rows + 2 * hd]
    return (
        output,
        grad_tokens,
        small[: c[1]],
        gw_qkv[0],
        gw_qkv[1],
        gw_qkv[2],
        gw_out,
        small[c[2] : c[3]],
        small[c[3] : c[4]],
        small[c[1] : c[2]],
        small[c[4] :].reshape(rows, experts),
        gw_gate,
        gw_up,
        gw_down,
    )


def solution(mesh):
    both = P(("rep", "shard"), None)
    row = P("shard", None)
    vec = P("shard")
    exp = P(None, "shard", None)
    return jax.shard_map(
        shards,
        mesh=mesh,
        in_specs=(
            both, P(("rep", "shard")), both, both, vec, row, row, row, row,
            vec, vec, vec, row, exp, exp, exp, both,
        ),
        out_specs=(both, both, vec, row, row, row, row, vec, vec, vec, row, exp, exp, exp),
        check_vma=False,
    )
```

```python
from functools import partial

import jax
import jax.numpy as jnp
from jax import lax
from jax.experimental import pallas as pl
from jax.experimental.pallas import tpu as pltpu
from jax.sharding import PartitionSpec as P

HEAD_DIM = 128

epsilon = 1e-06
rope_base = 50000.0
BF = jnp.bfloat16
F32 = jnp.float32


def inverse_rms(value):
    return lax.rsqrt(jnp.mean(value * value, axis=-1, keepdims=True) + epsilon)


def rope_tables(seq_len, head_width):
    half_dim = head_width // 2
    position = jnp.arange(seq_len, dtype=jnp.float32)
    frequency = rope_base ** (-jnp.arange(half_dim, dtype=jnp.float32) * 2.0 / head_width)
    angles = position[:, None] * frequency[None, :]
    return (jnp.cos(angles)[:, None, :], jnp.sin(angles)[:, None, :])


def rotate(value, cosine, sine_table, direction):
    half_dim = value.shape[-1] // 2
    first_half = value[..., :half_dim]
    second_half = value[..., half_dim:]
    return jnp.concatenate(
        [
            first_half * cosine - direction * second_half * sine_table,
            second_half * cosine + direction * first_half * sine_table,
        ],
        axis=-1,
    )


def head_back(grad_rot, value_hat, inverse, scale_gain, cosine, sine_table):
    grad_scaled = rotate(grad_rot, cosine, sine_table, -1.0)
    grad_gain = jnp.sum(grad_scaled * value_hat, axis=(0, 1, 2))
    grad_hat = grad_scaled * scale_gain
    grad_value = inverse * (
        grad_hat - value_hat * jnp.mean(grad_hat * value_hat, axis=-1, keepdims=True)
    )
    return (grad_value.astype(BF), grad_gain)


def dot(a, b, dims):
    return lax.dot_general(a, b, (dims, ((), ())), preferred_element_type=F32)


MESH = pl.DeviceIdType.MESH


def peer(bits):
    return (lax.axis_index("rep"), lax.axis_index("shard") ^ bits)


def along(rank):
    return (rank, lax.axis_index("shard"))


def meet(n_rep, n_shard):
    barrier = pltpu.get_barrier_semaphore()
    for bits in range(1, n_shard):
        pl.semaphore_signal(barrier, inc=1, device_id=peer(bits), device_id_type=MESH)
    rep, shard = lax.axis_index("rep"), lax.axis_index("shard")
    for bits in range(1, n_rep):
        pl.semaphore_signal(barrier, inc=1, device_id=(rep ^ bits, shard), device_id_type=MESH)
    pl.semaphore_wait(barrier, n_shard + n_rep - 2)


def remote(src, dst, send, recv, to):
    return pltpu.make_async_remote_copy(
        src_ref=src, dst_ref=dst, send_sem=send, recv_sem=recv, device_id=to, device_id_type=MESH
    )


class Line:
    def __init__(self, part, into1, into2, total, bufs, sems, ring):
        self.part, self.into1, self.into2, self.total = part, into1, into2, total
        self.pbuf, self.ibuf, self.sbuf, self.tbuf = bufs
        (self.s1, self.r1, self.s2, self.r2, self.s3, self.r3, self.ld, self.st) = sems
        self.ring = ring
        rank = lax.axis_index("rep")
        self.middle = (rank == 1) | (rank == 2)
        self.end = (rank == 0) | (rank == 3)
        self.next = along(rank ^ 1)
        self.across = along(rank ^ 3)

    def first(self, u):
        return remote(self.part.at[u], self.into1.at[u], self.s1.at[u], self.r1.at[u], self.next)

    def second(self, u):
        slot = lax.rem(u, self.ring)
        return remote(
            self.sbuf.at[slot], self.into2.at[u], self.s2.at[u], self.r2.at[u], self.across
        )

    def third(self, u):
        slot = lax.rem(u, 2)
        return remote(self.tbuf.at[slot], self.total.at[u], self.s3.at[u], self.r3.at[u], self.next)

    def keep(self, u):
        slot = lax.rem(u, 2)
        return pltpu.make_async_copy(self.tbuf.at[slot], self.total.at[u], self.st.at[slot])

    def launch(self, u):
        @pl.when(self.end)
        def _():
            self.first(u).start()

    def add_first(self, u):
        @pl.when(self.middle)
        def _():
            own = pltpu.make_async_copy(self.part.at[u], self.pbuf, self.ld.at[0])
            own.start()
            self.first(u).wait_recv()
            got = pltpu.make_async_copy(self.into1.at[u], self.ibuf, self.ld.at[1])
            got.start()
            own.wait()
            got.wait()
            self.sbuf[lax.rem(u, self.ring)] = (
                self.pbuf[...].astype(F32) + self.ibuf[...].astype(F32)
            ).astype(BF)
            self.second(u).start()

    def add_second(self, u, first=0):
        @pl.when(self.middle)
        def _():
            self.second(u).wait_recv()
            got = pltpu.make_async_copy(self.into2.at[u], self.ibuf, self.ld.at[1])
            got.start()

            @pl.when(u >= first + 2)
            def _():
                self.third(u - 2).wait_send()
                self.keep(u - 2).wait()

            got.wait()
            self.tbuf[lax.rem(u, 2)] = (
                self.sbuf[lax.rem(u, self.ring)].astype(F32) + self.ibuf[...].astype(F32)
            ).astype(BF)
            self.second(u).wait_send()
            self.third(u).start()
            self.keep(u).start()

    def finish(self, first, last):
        @pl.when(self.middle)
        def _():
            for u in range(last - 2, last):
                self.third(u).wait_send()
                self.keep(u).wait()

        @pl.when(self.end)
        def _():
            def body(u, c):
                self.first(u).wait_send()
                self.third(u).wait_recv()
                return c

            lax.fori_loop(first, last, body, 0)


def scatter_blocks(block, width, step, stage, in1, in2, acc, out, sems):
    s1, r1, s2, r2, so = sems
    pairs, seq = stage.shape[0], stage.shape[1]

    def cols(j):
        return pl.ds(pl.multiple_of(j * step, step), step)

    def pair(j):
        return remote(
            stage.at[:, :, cols(j)], in1.at[:, :, cols(j)], s1.at[j], r1.at[j], peer(1)
        )

    def odd(j, c):
        stage[:, :, cols(j)] = block(1, j).reshape(pairs, seq, step).astype(BF)
        pair(j).start()
        return c

    n = width // step
    lax.fori_loop(0, n, odd, 0)

    def sent(j, c):
        pair(j).wait_send()
        return c

    lax.fori_loop(0, n, sent, 0)

    def even(j, c):
        value = block(0, j).reshape(pairs, seq, step)
        pair(j).wait_recv()
        value = value + in1[:, :, cols(j)].astype(F32)
        acc[:, cols(j)] = value[0]
        stage[:, :, cols(j)] = value.astype(BF)
        return c

    lax.fori_loop(0, n, even, 0)
    far = [
        remote(stage.at[i], in2.at[i - 1], s2.at[i], r2.at[i], peer(2 * i)) for i in range(1, pairs)
    ]
    for copy in far:
        copy.start()

    def finish():
        for copy in far:
            copy.wait()
        for i in range(pairs - 1):
            acc[...] = acc[...] + in2[i].astype(F32)
        copy = pltpu.make_async_copy(acc, out, so)
        copy.start()
        copy.wait()

    return finish


def expert_kernel(
    n_rep, n_shard, experts, f_loc, head_units,
    x2_hbm, x2t_hbm, dy_hbm, gate_hbm, w_hbm, wd_hbm,
    part, into1, into2, total, gh_out, dx2_out, dgate_out,
    x2, x2t, dy, gate, w, wd, gh, dgu, dg, dstage, gstage, stage, in1, in2, acc, dgin,
    pbuf, ibuf, sbuf, tbuf,
    ld_sem, w_sem, d_sem, l_sem, a_send, a_recv, g_send, g_recv, rs_j, rr_j, rs_b, rr_b, o_sem,
    z1, y1, z2, y2, z3, y3, zl, zs,
):
    me = lax.axis_index("shard")
    tokens, width = x2.shape
    seq = tokens // n_shard
    rows = width // n_shard
    cols = 2 * f_loc
    half = n_shard // 2
    loads = [
        pltpu.make_async_copy(gate_hbm, gate, ld_sem.at[0]),
        pltpu.make_async_copy(x2_hbm, x2, ld_sem.at[1]),
        pltpu.make_async_copy(dy_hbm, dy, ld_sem.at[2]),
        pltpu.make_async_copy(x2t_hbm, x2t, ld_sem.at[3]),
    ]

    def ecols(e, size):
        return pl.ds(pl.multiple_of(e * size, size), size)

    def load_w(e):
        return (
            pltpu.make_async_copy(
                w_hbm.at[:, :, ecols(e, cols)], w.at[:, :, ecols(e, cols)], w_sem.at[0, e]
            ),
            pltpu.make_async_copy(wd_hbm.at[e], wd.at[e], w_sem.at[1, e]),
        )

    for copy in load_w(0):
        copy.start()
    for copy in loads:
        copy.start()
    for e in range(1, experts):
        for copy in load_w(e):
            copy.start()
    meet(n_rep, n_shard)
    dg[...] = jnp.zeros_like(dg)
    for copy in loads[:3]:
        copy.wait()
    line = Line(
        part, into1, into2, total, (pbuf, ibuf, sbuf, tbuf), (z1, y1, z2, y2, z3, y3, zl, zs), 4
    )

    def place(ref, e, owner):
        start = pl.multiple_of(lax.rem(owner, half) * rows, rows)
        return ref.at[3 * e + owner // half, pl.ds(start, rows), :]

    def send_block(e, b):
        return remote(
            gstage.at[lax.rem(e, 2), b], place(part, e, me), a_send.at[lax.rem(e, 2), b],
            a_recv.at[e, b], peer(b),
        )

    def own_block(e):
        return pltpu.make_async_copy(
            gstage.at[lax.rem(e, 2), 0], place(part, e, me), l_sem.at[lax.rem(e, 2)]
        )

    def down_unit(e):
        return pltpu.make_async_copy(
            dstage.at[lax.rem(e, 2)], part.at[3 * e + 2], d_sem.at[lax.rem(e, 2)]
        )

    tile = 2 * seq

    def expert(e, carry):
        for copy in load_w(e):
            copy.wait()
        slot = lax.rem(e, 2)

        def tokens_tile(i, c):
            r = pl.ds(pl.multiple_of(i * tile, tile), tile)
            pre = jnp.dot(
                x2[r, :],
                w[:, :, ecols(e, cols)].reshape(width, cols),
                preferred_element_type=F32,
            )
            g_pre, u_pre = (pre[:, :f_loc], pre[:, f_loc:])
            z = dot(dy[r, :], wd[e], ((1,), (1,)))
            lane = lax.broadcasted_iota(jnp.int32, (tile, gate.shape[1]), 1)
            own = lane == e
            gt = jnp.sum(jnp.where(own, gate[r, :], 0.0), axis=1, keepdims=True)
            sig = jax.nn.sigmoid(g_pre)
            act = g_pre * sig
            hh = act * u_pre
            dsum = jnp.sum(hh.astype(BF).astype(F32) * z, axis=1, keepdims=True)
            dg[r, :] = dg[r, :] + jnp.where(own, dsum, 0.0)
            gh[e, r, :] = (gt * hh).astype(BF)
            dh = gt * z
            d_gate = (dh * u_pre * sig * (1.0 + g_pre * (1.0 - sig))).astype(BF)
            d_up = (dh * act).astype(BF)
            dgu[e, i] = jnp.concatenate([d_gate, d_up], axis=1).reshape(2, seq, cols)
            return c

        lax.fori_loop(0, tokens // tile, tokens_tile, 0)

        @pl.when(e == 0)
        def _():
            loads[3].wait()

        @pl.when(e >= 2)
        def _():
            for b in range(1, n_shard):
                send_block(e - 2, b).wait_send()

        def grad_block(b, c):
            owner = me ^ b
            r = pl.ds(pl.multiple_of(owner * rows, rows), rows)
            value = jnp.dot(
                x2t[r, :], dgu[e].reshape(tokens, cols), preferred_element_type=F32
            ).astype(BF)
            gstage[slot, b] = value

            @pl.when(b > 0)
            def _():
                send_block(e, b).start()

            return c

        lax.fori_loop(0, n_shard, grad_block, 0)
        own_block(e).start()

        ght = gh[e].T

        def down_block(j, c):
            r = pl.ds(pl.multiple_of(j * f_loc, f_loc), f_loc)
            dstage[slot, r, :] = jnp.dot(
                ght, dy[:, ecols(j, cols)], preferred_element_type=F32
            ).astype(BF)
            return c

        lax.fori_loop(0, width // cols, down_block, 0)
        down_unit(e).start()

        def ready(x):
            for b in range(1, n_shard):
                send_block(x, b).wait_recv()
            own_block(x).wait()
            down_unit(x).wait()

        @pl.when(e >= 1)
        def _():
            ready(e - 1)

        @pl.when(e == experts - 1)
        def _():
            ready(e)

        if head_units:
            @pl.when((e >= 1) & (3 * e <= head_units))
            def _():
                for k in range(3):
                    line.launch(3 * (e - 1) + k)

            @pl.when((e >= 3) & (lax.rem(e, 2) == 1))
            def _():
                line.add_first((e - 3) // 2)

            @pl.when((e >= 6) & (lax.rem(e, 2) == 0))
            def _():
                line.add_second((e - 6) // 2)

        return carry

    lax.fori_loop(0, experts, expert, 0)
    for e in (experts - 2, experts - 1):
        for b in range(1, n_shard):
            send_block(e, b).wait_send()
    gh_copy = pltpu.make_async_copy(gh, gh_out, ld_sem.at[0])
    gh_copy.start()

    def gate_copy(b):
        return remote(
            dg.at[pl.ds(b * seq, seq), :], dgin.at[b - 1], g_send.at[b], g_recv.at[b], peer(b)
        )

    for b in range(1, n_shard):
        gate_copy(b).start()

    def dx2_block(parity, j):
        total_block = None
        for e in range(experts):
            lhs = dgu[e, :, parity].reshape(half * seq, cols)
            term = dot(lhs, w[j, :, e * cols : (e + 1) * cols], ((1,), (1,)))
            total_block = term if total_block is None else total_block + term
        return total_block

    finish = scatter_blocks(
        dx2_block, width, rows, stage, in1, in2, acc, dx2_out, (rs_j, rr_j, rs_b, rr_b, o_sem)
    )
    if head_units:
        line.add_first(4)
        line.add_second(2)
        line.add_second(3)
    for b in range(1, n_shard):
        gate_copy(b).wait()
        dg[pl.ds(0, seq), :] = dg[pl.ds(0, seq), :] + dgin[b - 1]
    copy = pltpu.make_async_copy(dg.at[pl.ds(0, seq), :], dgate_out, ld_sem.at[1])
    copy.start()
    if head_units:
        line.add_first(5)
        line.add_second(4)
    finish()
    copy.wait()
    gh_copy.wait()
    if head_units:
        line.add_second(5)
        line.finish(0, head_units)


def experts_call(x2, x2t, dy, gate, w, wd, n_rep, n_shard):
    tokens, width = x2.shape
    experts, f_loc = wd.shape[:2]
    seq, rows, cols, half = tokens // n_shard, width // n_shard, 2 * f_loc, n_shard // 2
    head_units = 6 if n_rep == 4 else 0
    units = 3 * experts
    slots = max(head_units, 1)
    unit = (width // 2, cols)
    dma = pltpu.SemaphoreType.DMA
    anyspec = pl.BlockSpec(memory_space=pl.ANY)
    shape = jax.ShapeDtypeStruct
    return pl.pallas_call(
        partial(expert_kernel, n_rep, n_shard, experts, f_loc, head_units),
        out_shape=(
            shape((units,) + unit, BF),
            shape((slots,) + unit, BF),
            shape((slots,) + unit, BF),
            shape((slots,) + unit, BF),
            shape((experts, tokens, f_loc), BF),
            shape((seq, width), F32),
            shape((seq, gate.shape[1]), F32),
        ),
        in_specs=[anyspec] * 6,
        out_specs=(anyspec,) * 7,
        scratch_shapes=[
            pltpu.VMEM((tokens, width), BF),
            pltpu.VMEM((width, tokens), BF),
            pltpu.VMEM((tokens, width), BF),
            pltpu.VMEM(gate.shape, F32),
            pltpu.VMEM(w.shape, BF),
            pltpu.VMEM(wd.shape, BF),
            pltpu.VMEM((experts, tokens, f_loc), BF),
            pltpu.VMEM((experts, half, 2, seq, cols), BF),
            pltpu.VMEM(gate.shape, F32),
            pltpu.VMEM((2,) + unit, BF),
            pltpu.VMEM((2, n_shard, rows, cols), BF),
            pltpu.VMEM((half, seq, width), BF),
            pltpu.VMEM((half, seq, width), BF),
            pltpu.VMEM((half - 1, seq, width), BF),
            pltpu.VMEM((seq, width), F32),
            pltpu.VMEM((n_shard - 1, seq, gate.shape[1]), F32),
            pltpu.VMEM(unit, BF),
            pltpu.VMEM(unit, BF),
            pltpu.VMEM((4 if head_units else 1,) + unit, BF),
            pltpu.VMEM((2 if head_units else 1,) + unit, BF),
            dma((4,)),
            dma((2, experts)),
            dma((2,)),
            dma((2,)),
            dma((2, n_shard)),
            dma((experts, n_shard)),
            dma((n_shard,)),
            dma((n_shard,)),
            dma((n_shard,)),
            dma((n_shard,)),
            dma((half,)),
            dma((half,)),
            dma,
        ]
        + [dma((slots,)) for _ in range(6)]
        + [dma((2,)), dma((2,))],
        compiler_params=pltpu.CompilerParams(
            collective_id=1, has_side_effects=True, vmem_limit_bytes=67000000
        ),
        name="experts",
    )(x2, x2t, dy, gate, w, wd)


def shards(
    tokens, segments, routes, slot_ids, attn_gain, w_query, w_key, w_value, w_out,
    query_gain, key_gain, ffn_gain, router, w_gate, w_up, w_down, cotangent,
):
    n_shard = lax.axis_size("shard")
    me = lax.axis_index("shard")
    seq, width = tokens.shape
    experts, rows, hidden_f = w_gate.shape
    f_loc = w_down.shape[1]
    cols = width // n_shard
    heads = cols // HEAD_DIM
    group = n_shard * seq
    scale = HEAD_DIM ** (-0.5)

    def gather(x, axis=0):
        return lax.all_gather(x, "shard", axis=axis, tiled=True)

    def scatter(x):
        return lax.psum_scatter(x, "shard", scatter_dimension=0, tiled=True)

    qkv_rows = jnp.stack([w_query, w_key, w_value]).astype(BF)
    qkv = lax.all_to_all(qkv_rows, "shard", split_axis=2, concat_axis=1, tiled=True)
    w_out_b = w_out.astype(BF)
    n_rep = lax.axis_size("rep")
    near = me ^ jnp.arange(n_shard)

    def blocks(w):
        return w.astype(BF).reshape(experts, rows, n_shard, f_loc).transpose(2, 1, 0, 3)

    gu = jnp.concatenate([blocks(w_gate), blocks(w_up)], axis=-1)
    gu = gu.reshape(n_shard, rows, experts * 2 * f_loc)
    gu = lax.all_to_all(gu, "shard", split_axis=0, concat_axis=0, tiled=True)
    w_down_b = w_down.astype(BF)
    gains = gather(jnp.concatenate([attn_gain, ffn_gain, query_gain, key_gain]).astype(BF)[None])
    g_attn = gains[:, :rows].reshape(width).astype(F32)
    g_ffn = gains[:, rows : 2 * rows].reshape(width).astype(F32)
    hd = HEAD_DIM // n_shard
    g_query = gains[:, 2 * rows : 2 * rows + hd].reshape(HEAD_DIM).astype(F32)
    g_key = gains[:, 2 * rows + hd :].reshape(HEAD_DIM).astype(F32)
    router_b = gather(router.astype(BF))
    dy_all = gather(cotangent)
    seg_all = gather(segments).reshape(n_shard, seq)

    h = tokens.astype(F32)
    r1 = inverse_rms(h)
    n1 = h * r1
    x1 = (n1 * g_attn).astype(BF)
    x1_all = gather(x1)
    split = (n_shard, seq, heads, HEAD_DIM)
    q = dot(x1_all, qkv[0], ((1,), (0,))).reshape(split)
    k = dot(x1_all, qkv[1], ((1,), (0,))).reshape(split)
    v = dot(x1_all, qkv[2], ((1,), (0,))).astype(BF).reshape(split)
    cosine, sine = rope_tables(seq, HEAD_DIM)
    rq = inverse_rms(q)
    q_hat = q * rq
    qr = rotate(q_hat * g_query, cosine, sine, 1.0).astype(BF)
    rk = inverse_rms(k)
    k_hat = k * rk
    kr = rotate(k_hat * g_key, cosine, sine, 1.0).astype(BF)
    same = (seg_all[:, :, None] == seg_all[:, None, :])[:, None]
    s = jnp.einsum("bqhd,bkhd->bhqk", qr, kr, preferred_element_type=F32) * scale
    s = jnp.where(same, s, -1000000000.0)
    top = jnp.max(s, axis=-1, keepdims=True)
    e = jnp.exp(s - top)
    probs = e / jnp.sum(e, axis=-1, keepdims=True)
    probs_b = probs.astype(BF)
    a = (
        jnp.einsum("bhqk,bkhd->bqhd", probs_b, v, preferred_element_type=F32)
        .astype(BF)
        .reshape(group, cols)
    )
    h1 = h + scatter(dot(a, w_out_b, ((1,), (0,))).astype(BF)).astype(F32)
    r2 = inverse_rms(h1)
    n2 = h1 * r2
    x2 = (n2 * g_ffn).astype(BF)
    pr = jax.nn.softmax(dot(x2, router_b, ((1,), (0,))), axis=-1)
    hit = jnp.sum(
        (routes[:, :, None] == jnp.arange(experts, dtype=jnp.int32)).astype(F32), axis=1
    )
    gate = pr * hit
    def by_distance(x):
        return jnp.take(x.reshape(n_shard, seq, -1), near, axis=0).reshape(group, -1)

    x2_all = by_distance(gather(x2))
    gate_all = by_distance(gather(jnp.pad(gate, ((0, 0), (0, 128 - experts)))))
    dy = cotangent.astype(F32)
    part, _, _, total, gh, dx2_sum, dgate = experts_call(
        x2_all, x2_all.T, by_distance(dy_all), gate_all, gu, w_down_b, n_rep, n_shard
    )
    dgate = dgate[:, :experts]
    nat = jnp.take(gh.reshape(experts, n_shard, seq, f_loc), near, axis=1)
    nat = nat.reshape(experts, group, f_loc)
    out_part = jnp.einsum("etf,efd->td", nat, w_down_b, preferred_element_type=F32)
    output = (h1 + scatter(out_part.astype(BF)).astype(F32)).astype(BF)
    if n_rep == 4:
        summed = jnp.concatenate([total, lax.psum(part[total.shape[0] :], "rep")])
    else:
        summed = lax.psum(part, "rep")
    summed = summed.reshape(experts, 3, -1, 2 * f_loc)
    gw_gu = summed[:, :2].reshape(experts, n_shard, rows, 2, f_loc).transpose(3, 0, 2, 1, 4)
    gw_gu = gw_gu.reshape(2, experts, rows, hidden_f).astype(F32)
    gw_down = summed[:, 2].reshape(experts, -1, f_loc, 2 * f_loc).transpose(0, 2, 1, 3)
    gw_down = gw_down.reshape(experts, f_loc, width).astype(F32)

    dpr = dgate * hit
    dz = (pr * (dpr - jnp.sum(pr * dpr, axis=-1, keepdims=True))).astype(BF)
    gw_router = scatter(dot(x2, dz, ((0,), (0,))))
    dx2 = dx2_sum + dot(dz, router_b, ((1,), (1,)))
    gg_ffn = jnp.sum(dx2 * n2, axis=0)
    e2 = dx2 * g_ffn
    dh1 = dy + r2 * (e2 - n2 * jnp.mean(e2 * n2, axis=-1, keepdims=True))

    da_all = gather(dh1.astype(BF))
    gw_out = dot(a, da_all, ((0,), (0,)))
    do = dot(da_all, w_out_b, ((1,), (1,))).astype(BF).reshape(split)
    dv = jnp.einsum("bhqk,bqhd->bkhd", probs_b, do, preferred_element_type=F32).astype(BF)
    dp = jnp.einsum("bqhd,bkhd->bhqk", do, v, preferred_element_type=F32)
    ds = (probs * (dp - jnp.sum(probs * dp, axis=-1, keepdims=True))).astype(BF)
    dqr = jnp.einsum("bhqk,bkhd->bqhd", ds, kr, preferred_element_type=F32) * scale
    dkr = jnp.einsum("bhqk,bqhd->bkhd", ds, qr, preferred_element_type=F32) * scale
    dq, gg_query = head_back(dqr, q_hat, rq, g_query, cosine, sine)
    dk, gg_key = head_back(dkr, k_hat, rk, g_key, cosine, sine)
    d_qkv = jnp.stack([x.reshape(group, cols) for x in (dq, dk, dv)])
    gw_qkv = jnp.einsum("td,wtc->wdc", x1_all, d_qkv, preferred_element_type=F32).astype(BF)
    gw_qkv = lax.all_to_all(gw_qkv, "shard", split_axis=1, concat_axis=2, tiled=True)
    dx1 = scatter(
        jnp.einsum("wtc,wdc->td", d_qkv, qkv, preferred_element_type=F32).astype(BF)
    ).astype(F32)
    gg_attn = jnp.sum(dx1 * n1, axis=0)
    e1 = dx1 * g_attn
    grad_tokens = dh1 + r1 * (e1 - n1 * jnp.mean(e1 * n1, axis=-1, keepdims=True))

    def own(x):
        return x.reshape(n_shard, -1)

    small = scatter(
        jnp.concatenate([own(gg_attn), own(gg_ffn), own(gg_query), own(gg_key)], axis=1)
    )[0]
    small = lax.psum(jnp.concatenate([small, gw_router.reshape(-1)]), "rep")
    gw_qkv = lax.psum(gw_qkv, "rep").astype(F32)
    gw_out = lax.psum(gw_out.astype(BF), "rep").astype(F32)
    c = [0, rows, 2 * rows, 2 * rows + hd, 2 * rows + 2 * hd]
    return (
        output,
        grad_tokens,
        small[: c[1]],
        gw_qkv[0],
        gw_qkv[1],
        gw_qkv[2],
        gw_out,
        small[c[2] : c[3]],
        small[c[3] : c[4]],
        small[c[1] : c[2]],
        small[c[4] :].reshape(rows, experts),
        gw_gu[0],
        gw_gu[1],
        gw_down,
    )


def solution(mesh):
    both = P(("rep", "shard"), None)
    row = P("shard", None)
    vec = P("shard")
    exp = P(None, "shard", None)
    return jax.shard_map(
        shards,
        mesh=mesh,
        in_specs=(
            both, P(("rep", "shard")), both, both, vec, row, row, row, row,
            vec, vec, vec, row, exp, exp, exp, both,
        ),
        out_specs=(both, both, vec, row, row, row, row, vec, vec, vec, row, exp, exp, exp),
        check_vma=False,
    )
```

```python
from functools import partial

import jax
import jax.numpy as jnp
from jax import lax
from jax.experimental import pallas as pl
from jax.experimental.pallas import tpu as pltpu
from jax.sharding import PartitionSpec as P

HEAD_DIM = 128
HEAD_UNITS = 20
HEAD_EXPERTS = 1
SENT_AHEAD = 3
CROSSED = 2
WINDOW = 2
LAG = 2
PUMPS = (3, 1, 1, 1, 1, 1, 1, 1, 1, 1, 1, 1, 1)

epsilon = 1e-06
rope_base = 50000.0
BF = jnp.bfloat16
F32 = jnp.float32


def inverse_rms(value):
    return lax.rsqrt(jnp.mean(value * value, axis=-1, keepdims=True) + epsilon)


def rope_tables(seq_len, head_width):
    half_dim = head_width // 2
    position = jnp.arange(seq_len, dtype=jnp.float32)
    frequency = rope_base ** (-jnp.arange(half_dim, dtype=jnp.float32) * 2.0 / head_width)
    angles = position[:, None] * frequency[None, :]
    return (jnp.cos(angles)[:, None, :], jnp.sin(angles)[:, None, :])


def rotate(value, cosine, sine_table, direction):
    half_dim = value.shape[-1] // 2
    first_half = value[..., :half_dim]
    second_half = value[..., half_dim:]
    return jnp.concatenate(
        [
            first_half * cosine - direction * second_half * sine_table,
            second_half * cosine + direction * first_half * sine_table,
        ],
        axis=-1,
    )


def head_back(grad_rot, value_hat, inverse, scale_gain, cosine, sine_table):
    grad_scaled = rotate(grad_rot, cosine, sine_table, -1.0)
    grad_gain = jnp.sum(grad_scaled * value_hat, axis=(0, 1, 2))
    grad_hat = grad_scaled * scale_gain
    grad_value = inverse * (
        grad_hat - value_hat * jnp.mean(grad_hat * value_hat, axis=-1, keepdims=True)
    )
    return (grad_value.astype(BF), grad_gain)


def dot(a, b, dims):
    return lax.dot_general(a, b, (dims, ((), ())), preferred_element_type=F32)


MESH = pl.DeviceIdType.MESH


def peer(bits):
    return (lax.axis_index("rep"), lax.axis_index("shard") ^ bits)


def along(rank):
    return (rank, lax.axis_index("shard"))


def meet(n_rep, n_shard):
    barrier = pltpu.get_barrier_semaphore()
    for bits in range(1, n_shard):
        pl.semaphore_signal(barrier, inc=1, device_id=peer(bits), device_id_type=MESH)
    rep, shard = lax.axis_index("rep"), lax.axis_index("shard")
    for bits in range(1, n_rep):
        pl.semaphore_signal(barrier, inc=1, device_id=(rep ^ bits, shard), device_id_type=MESH)
    pl.semaphore_wait(barrier, n_shard + n_rep - 2)


def remote(src, dst, send, recv, to):
    return pltpu.make_async_remote_copy(
        src_ref=src, dst_ref=dst, send_sem=send, recv_sem=recv, device_id=to, device_id_type=MESH
    )


def down_at(e):
    return jnp.maximum(3 * e - 2, 0)


def gate_up_at(e, experts):
    return 3 * e + jnp.where(e == experts - 1, 1, 2)


class Line:
    def __init__(self, part, into1, into2, total, bufs, sems, base=0, landed=0, crossed=0, window=2, lag=2):
        self.part, self.into1, self.into2, self.total = part, into1, into2, total
        self.pbuf, self.ibuf, self.sbuf, self.tbuf = bufs
        (self.s1, self.r1, self.s2, self.r2, self.s3, self.r3, self.ld, self.st) = sems
        self.ring = self.sbuf.shape[0]
        self.base = base
        self.fresh = base + landed
        self.crossed = base + crossed
        self.lag = lag
        self.window = window
        rank = lax.axis_index("rep")
        self.middle = (rank == 1) | (rank == 2)
        self.end = (rank == 0) | (rank == 3)
        self.next = along(rank ^ 1)
        self.across = along(rank ^ 3)

    def first(self, u):
        i = u - self.base
        return remote(self.part.at[u], self.into1.at[u], self.s1.at[i], self.r1.at[i], self.next)

    def second(self, u):
        i = u - self.base
        slot = lax.rem(i, self.ring)
        return remote(
            self.sbuf.at[slot], self.into2.at[u], self.s2.at[i], self.r2.at[i], self.across
        )

    def third(self, u):
        i = u - self.base
        slot = lax.rem(i, 2)
        return remote(self.tbuf.at[slot], self.total.at[u], self.s3.at[i], self.r3.at[i], self.next)

    def keep(self, u):
        i = u - self.base
        slot = lax.rem(i, 2)
        return pltpu.make_async_copy(self.tbuf.at[slot], self.total.at[u], self.st.at[slot])

    def launch(self, u):
        @pl.when(self.end)
        def _():
            self.first(u).start()

    def add(self, dst, x, y):
        tile = 128

        def body(i, c):
            r = pl.ds(pl.multiple_of(i * tile, tile), tile)
            dst[r, :] = (x[r, :].astype(F32) + y[r, :].astype(F32)).astype(BF)
            return c

        lax.fori_loop(0, dst.shape[0] // tile, body, 0)

    def add_first(self, u):
        i = u - self.base

        @pl.when(self.middle & (u >= self.crossed))
        def _():
            own = pltpu.make_async_copy(self.part.at[u], self.pbuf, self.ld.at[0])
            own.start()

            @pl.when(u >= self.fresh)
            def _():
                self.first(u).wait_recv()

            got = pltpu.make_async_copy(self.into1.at[u], self.ibuf, self.ld.at[1])
            got.start()
            own.wait()
            got.wait()
            self.add(self.sbuf.at[lax.rem(i, self.ring)], self.pbuf, self.ibuf)
            self.second(u).start()

    def kept(self, u):
        slot = lax.rem(u - self.base, self.ring)
        return pltpu.make_async_copy(
            self.sbuf.at[slot], self.part.at[u], self.st.at[2 + lax.rem(u, 2)]
        )

    def add_second(self, u):
        i = u - self.base

        @pl.when(self.middle)
        def _():
            slot = lax.rem(i, self.ring)
            again = pltpu.make_async_copy(self.part.at[u], self.sbuf.at[slot], self.ld.at[0])

            @pl.when(u >= self.crossed)
            def _():
                self.second(u).wait_recv()

            @pl.when(u < self.crossed)
            def _():
                again.start()

            got = pltpu.make_async_copy(self.into2.at[u], self.ibuf, self.ld.at[1])
            got.start()

            @pl.when(i >= 2)
            def _():
                self.third(u - 2).wait_send()
                self.keep(u - 2).wait()

            @pl.when(u < self.crossed)
            def _():
                again.wait()

            got.wait()
            self.add(self.tbuf.at[lax.rem(i, 2)], self.sbuf.at[slot], self.ibuf)

            @pl.when(u >= self.crossed)
            def _():
                self.second(u).wait_send()

            self.third(u).start()
            self.keep(u).start()

    def step(self, u, limit):
        narrow = limit - 2 - self.window if self.window > 2 else 0

        @pl.when(self.end & (u >= self.fresh))
        def _():
            self.first(u).wait_send()

            @pl.when((u >= narrow + self.window - 2) & (u + 2 < limit))
            def _():
                self.first(u + 2).start()

            @pl.when(u < narrow)
            def _():
                self.first(u + self.window).start()

        self.add_first(u)

        @pl.when(u >= self.crossed + self.lag)
        def _():
            self.add_second(u - self.lag)

    def steps(self, low, high, limit):
        def body(u, c):
            self.step(u, limit)
            return c

        lax.fori_loop(low, high, body, 0)

    def finish(self, last, ahead=0, cross=0):
        for i in range(self.lag):
            self.add_second(last - self.lag + i)
            if i < cross:
                self.add_first(last + i)

                @pl.when(self.middle)
                def _():
                    self.kept(last + i).start()

        for u in range(last, last + ahead):
            @pl.when(self.end)
            def _():
                self.first(u).wait_send()
                if u + 2 < last + ahead:
                    self.first(u + 2).start()

            @pl.when(self.middle)
            def _():
                if u >= last + cross:
                    self.first(u).wait_recv()

        @pl.when(self.middle)
        def _():
            for u in range(last, last + cross):
                self.second(u).wait()
                self.kept(u).wait()

        @pl.when(self.middle)
        def _():
            for u in range(last - 2, last):
                self.third(u).wait_send()
                self.keep(u).wait()

        @pl.when(self.end)
        def _():
            def body(u, c):
                self.third(u).wait_recv()
                return c

            lax.fori_loop(self.base, last, body, 0)


def line_scratch(slots):
    dma = pltpu.SemaphoreType.DMA
    return [dma((slots,)) for _ in range(6)] + [dma((2,)), dma((4,))]


def scatter_blocks(block, width, step, stage, in1, in2, acc, out, sems):
    s1, r1, s2, r2, so = sems
    pairs, seq = stage.shape[0], stage.shape[1]

    def cols(j):
        return pl.ds(pl.multiple_of(j * step, step), step)

    def pair(j):
        return remote(
            stage.at[:, :, cols(j)], in1.at[:, :, cols(j)], s1.at[j], r1.at[j], peer(1)
        )

    def odd(j, c):
        stage[:, :, cols(j)] = block(1, j).reshape(pairs, seq, step).astype(BF)
        pair(j).start()
        return c

    n = width // step
    lax.fori_loop(0, n, odd, 0)

    def sent(j, c):
        pair(j).wait_send()
        return c

    lax.fori_loop(0, n, sent, 0)

    def even(j, c):
        value = block(0, j).reshape(pairs, seq, step)
        pair(j).wait_recv()
        value = value + in1[:, :, cols(j)].astype(F32)
        acc[:, cols(j)] = value[0]
        stage[:, :, cols(j)] = value.astype(BF)
        return c

    lax.fori_loop(0, n, even, 0)
    far = [
        remote(stage.at[i], in2.at[i - 1], s2.at[i], r2.at[i], peer(2 * i)) for i in range(1, pairs)
    ]

    def send():
        for copy in far:
            copy.start()

    def finish():
        for copy in far:
            copy.wait()
        for i in range(pairs - 1):
            acc[...] = acc[...] + in2[i].astype(F32)
        if out is not None:
            copy = pltpu.make_async_copy(acc, out, so)
            copy.start()
            copy.wait()

    return send, finish


class Columns:
    def __init__(self, gate_hbm, up_hbm, place, fbuf, stage, sems, first, last):
        self.gate, self.up, self.place = gate_hbm, up_hbm, place
        self.fbuf, self.stage = fbuf, stage
        self.ld, self.send, self.recv = sems
        self.first, self.last = first, last
        self.me = lax.axis_index("shard")
        self.n = stage.shape[1]

    def loads(self, e):
        slot = lax.rem(e, 2)
        return (
            pltpu.make_async_copy(self.gate.at[e], self.fbuf.at[slot, 0], self.ld.at[slot, 0]),
            pltpu.make_async_copy(self.up.at[e], self.fbuf.at[slot, 1], self.ld.at[slot, 1]),
        )

    def load(self, e):
        for copy in self.loads(e):
            copy.start()

    def copy_to(self, e, owner):
        away = owner ^ self.me
        slot = lax.rem(e, 2)
        return remote(
            self.stage.at[slot, owner], self.place(e, self.me), self.send.at[slot, away],
            self.recv.at[e, away], peer(away),
        )

    def sent(self, e):
        for b in range(1, self.n):
            self.copy_to(e, self.me ^ b).wait_send()

    def prepare(self, e, keep):
        for copy in self.loads(e):
            copy.wait()

        @pl.when(e >= self.first + 2)
        def _():
            self.sent(e - 2)

        slot = lax.rem(e, 2)
        size = self.fbuf.shape[3] // self.n
        for owner in range(self.n):
            c = slice(owner * size, (owner + 1) * size)
            block = jnp.concatenate([self.fbuf[slot, i, :, c] for i in range(2)], axis=1)
            self.stage[slot, owner] = block.astype(BF)

            @pl.when(owner != self.me)
            def _():
                self.copy_to(e, owner).start()

        keep(e, slot)

        @pl.when(e + 2 < self.last)
        def _():
            self.load(e + 2)

    def arrived(self, e):
        for b in range(1, self.n):
            self.copy_to(e, self.me ^ b).wait_recv()


def spread_sends(src, land, send, recv, n_shard):
    def copy(i):
        rows = src if i == 1 or i % 2 == 0 else land.at[i - 1]
        return remote(rows, land.at[i], send.at[i], recv.at[i], peer(i if i % 2 == 0 else 1))

    return copy


def expert_kernel(
    n_rep, n_shard, experts, f_loc, head_units, ahead,
    x2_hbm, dy_hbm, gate_hbm, w_hbm, wd_hbm, wg_hbm, wu_hbm, h1_hbm, pr_hbm, hit_hbm, small_hbm,
    part, into1, into2, total, gh_out, da_out, dh1_out, pay_out, wd_out,
    x2, x2t, dy, gate, w, wd, gh, dgu, dg, dstage, gstage, stage, in1, in2, acc, dgin,
    fbuf, cstage, wdf, h1, pr, hit, small, da, pay, pbuf, ibuf, sbuf, tbuf,
    ld_sem, w_sem, h_sem, c_ld, c_send, c_recv, d_sem, l_sem, a_send, a_recv, g_send, g_recv, rs_j, rr_j, rs_b, rr_b, o_sem,
    z1, y1, z2, y2, z3, y3, zl, zs,
):
    me = lax.axis_index("shard")
    tokens, width = x2.shape
    seq = tokens // n_shard
    rows = width // n_shard
    cols = 2 * f_loc
    half = n_shard // 2
    loads = [
        pltpu.make_async_copy(gate_hbm, gate, ld_sem.at[0]),
        pltpu.make_async_copy(x2_hbm, x2, ld_sem.at[1]),
        pltpu.make_async_copy(dy_hbm, dy, ld_sem.at[2]),
    ]
    late = ((h1_hbm, h1), (pr_hbm, pr), (hit_hbm, hit), (small_hbm, small))
    late = [pltpu.make_async_copy(x, y, ld_sem.at[3 + i]) for i, (x, y) in enumerate(late)]

    def ecols(e, size):
        return pl.ds(pl.multiple_of(e * size, size), size)

    head = w_hbm.shape[2] // cols

    def load_head(e):
        c = pl.ds(e * cols, cols)
        return pltpu.make_async_copy(w_hbm.at[:, :, c], w.at[:, :, c], w_sem.at[0, e])

    def load_down(e):
        slot = lax.rem(e, 2)
        return pltpu.make_async_copy(wd_hbm.at[e], wdf.at[slot], w_sem.at[1, slot])

    columns = Columns(
        wg_hbm, wu_hbm, lambda e, src: w.at[src, :, ecols(e, cols)], fbuf, cstage,
        (c_ld, c_send, c_recv), head, experts,
    )

    def keep(e, slot):
        w[me, :, ecols(e, cols)] = cstage[slot, me]

    load_down(0).start()
    for e in range(head):
        load_head(e).start()
    for copy in loads:
        copy.start()
    columns.load(head)
    columns.load(head + 1)
    load_down(1).start()
    meet(n_rep, n_shard)
    columns.prepare(head, keep)
    dg[...] = jnp.zeros_like(dg)
    for copy in loads:
        copy.wait()

    for e in range(head):
        load_head(e).wait()
    line = Line(
        part, into1, into2, total, (pbuf, ibuf, sbuf, tbuf), (z1, y1, z2, y2, z3, y3, zl, zs)
    )

    def place(ref, e, owner):
        start = pl.multiple_of(lax.rem(owner, half) * rows, rows)
        return ref.at[gate_up_at(e, experts) + owner // half, pl.ds(start, rows), :]

    def send_block(e, b):
        return remote(
            gstage.at[lax.rem(e, 2), b], place(part, e, me), a_send.at[lax.rem(e, 2), b],
            a_recv.at[e, b], peer(b),
        )

    def own_block(e):
        return pltpu.make_async_copy(
            gstage.at[lax.rem(e, 2), 0], place(part, e, me), l_sem.at[lax.rem(e, 2)]
        )

    def down_unit(e):
        return pltpu.make_async_copy(
            dstage.at[lax.rem(e, 2)], part.at[down_at(e)], d_sem.at[lax.rem(e, 2)]
        )

    def gh_copy(e):
        return pltpu.make_async_copy(gh.at[lax.rem(e, 2)], gh_out.at[e], h_sem.at[lax.rem(e, 2)])

    tile = 2 * seq

    def expert(e, carry):
        load_down(e).wait()
        slot = lax.rem(e, 2)
        wd[e] = wdf[slot].astype(BF)

        @pl.when(e + 2 < experts)
        def _():
            load_down(e + 2).start()

        @pl.when(e >= 2)
        def _():
            gh_copy(e - 2).wait()

        @pl.when(e >= head)
        def _():
            columns.arrived(e)

        def tokens_tile(i, c):
            r = pl.ds(pl.multiple_of(i * tile, tile), tile)
            pre = jnp.dot(
                x2[r, :],
                w[:, :, ecols(e, cols)].reshape(width, cols),
                preferred_element_type=F32,
            )
            g_pre, u_pre = (pre[:, :f_loc], pre[:, f_loc:])
            z = dot(dy[r, :], wd[e], ((1,), (1,)))
            lane = lax.broadcasted_iota(jnp.int32, (tile, gate.shape[1]), 1)
            own = lane == e
            gt = jnp.sum(jnp.where(own, gate[r, :], 0.0), axis=1, keepdims=True)
            sig = jax.nn.sigmoid(g_pre)
            act = g_pre * sig
            hh = act * u_pre
            dsum = jnp.sum(hh.astype(BF).astype(F32) * z, axis=1, keepdims=True)
            dg[r, :] = dg[r, :] + jnp.where(own, dsum, 0.0)
            gh[slot, r, :] = (gt * hh).astype(BF)
            dh = gt * z
            d_gate = (dh * u_pre * sig * (1.0 + g_pre * (1.0 - sig))).astype(BF)
            d_up = (dh * act).astype(BF)
            dgu[e, i] = jnp.concatenate([d_gate, d_up], axis=1).reshape(2, seq, cols)
            return c

        lax.fori_loop(0, tokens // tile, tokens_tile, 0)

        if head_units:
            @pl.when(e >= 2)
            def _():
                line.step(2 * e - 3, head_units + ahead)

        @pl.when((e == 1) | (e == 2))
        def _():
            columns.prepare(e + 1, keep)

        gh_copy(e).start()
        ght = gh[slot].T

        def down_block(j, c):
            r = pl.ds(pl.multiple_of(j * f_loc, f_loc), f_loc)
            dstage[slot, r, :] = jnp.dot(
                ght, dy[:, ecols(j, cols)], preferred_element_type=F32
            ).astype(BF)
            return c

        lax.fori_loop(0, width // cols, down_block, 0)
        down_unit(e).start()
        down_unit(e).wait()

        if head_units:
            @pl.when(e < 2)
            def _():
                line.launch(e)

        @pl.when(e == 0)
        def _():
            def turn(i, c):
                for j in range(n_shard):
                    x2t[j * rows : (j + 1) * rows, ecols(i, seq)] = x2[
                        ecols(i, seq), j * rows : (j + 1) * rows
                    ].T
                return c

            lax.fori_loop(0, n_shard, turn, 0)

        @pl.when(e >= 2)
        def _():
            for b in range(1, n_shard):
                send_block(e - 2, b).wait_send()

        def grad_block(b, c):
            owner = me ^ b
            r = pl.ds(pl.multiple_of(owner * rows, rows), rows)
            value = jnp.dot(
                x2t[r, :], dgu[e].reshape(tokens, cols), preferred_element_type=F32
            ).astype(BF)
            gstage[slot, b] = value

            @pl.when(b > 0)
            def _():
                send_block(e, b).start()

            return c

        lax.fori_loop(0, n_shard, grad_block, 0)
        own_block(e).start()

        @pl.when((e >= 2) & (e + 2 < experts))
        def _():
            columns.prepare(e + 2, keep)

        def ready(x):
            for b in range(1, n_shard):
                send_block(x, b).wait_recv()
            own_block(x).wait()

        @pl.when(e >= 1)
        def _():
            ready(e - 1)

        @pl.when(e == experts - 1)
        def _():
            ready(e)

        if head_units:
            @pl.when(e >= 1)
            def _():
                line.step(2 * e - 2, head_units + ahead)

        return carry

    lax.fori_loop(0, experts, expert, 0)
    for e in (experts - 2, experts - 1):
        columns.sent(e)
        for b in range(1, n_shard):
            send_block(e, b).wait_send()

    wd_copy = pltpu.make_async_copy(wd, wd_out, ld_sem.at[0])
    wd_copy.start()

    def gate_copy(b):
        return remote(
            dg.at[pl.ds(b * seq, seq), :], dgin.at[b - 1], g_send.at[b], g_recv.at[b], peer(b)
        )

    for b in range(1, n_shard):
        gate_copy(b).start()

    def dx2_block(parity, j):
        total_block = None
        for e in range(experts):
            lhs = dgu[e, :, parity].reshape(half * seq, cols)
            term = dot(lhs, w[j, :, e * cols : (e + 1) * cols], ((1,), (1,)))
            total_block = term if total_block is None else total_block + term
        return total_block

    for copy in late:
        copy.start()
    send, finish = scatter_blocks(
        dx2_block, width, rows, stage, in1, in2, acc, None, (rs_j, rr_j, rs_b, rr_b, None)
    )
    send()
    if head_units:
        line.steps(2 * experts - 3, head_units - 1, head_units + ahead)
    for b in range(1, n_shard):
        gate_copy(b).wait()
        dg[pl.ds(0, seq), :] = dg[pl.ds(0, seq), :] + dgin[b - 1]
    finish()
    for copy in late:
        copy.wait()

    probs = pr[...]
    dpr = dg[pl.ds(0, seq), :] * hit[...]
    dz = probs * (dpr - jnp.sum(probs * dpr, axis=-1, keepdims=True))
    low = dz.astype(BF)
    taps = pltpu.roll(low.astype(F32), 2, 1)[:, :16].astype(BF)
    pay[...] = jnp.zeros_like(pay)
    pay[2 : experts + 2, :] = dot(low.T, x2[pl.ds(0, seq), :], ((1,), (0,)))[:experts]
    gain = small[1:2, :].astype(BF).astype(F32)
    inverse = lax.rsqrt(jnp.mean(h1[...] * h1[...], axis=-1, keepdims=True) + epsilon)
    n2 = h1[...] * inverse
    dx2 = acc[...] + dot(taps, small[...].astype(BF), ((1,), (0,)))
    pay[1:2, :] = jnp.sum(dx2 * n2, axis=0, keepdims=True)
    e2 = dx2 * gain
    dh1 = dy[pl.ds(0, seq), :].astype(F32) + inverse * (
        e2 - n2 * jnp.mean(e2 * n2, axis=-1, keepdims=True)
    )
    acc[...] = dh1
    da[...] = dh1.astype(BF)
    outs = ((acc, dh1_out), (da, da_out), (pay, pay_out))
    outs = [pltpu.make_async_copy(x, y, ld_sem.at[3 + i]) for i, (x, y) in enumerate(outs)]
    for copy in outs:
        copy.start()
    for copy in outs:
        copy.wait()
    wd_copy.wait()
    for e in (experts - 2, experts - 1):
        gh_copy(e).wait()
    if head_units:
        line.step(head_units - 1, head_units + ahead)
        line.finish(head_units, ahead, CROSSED)


def experts_call(
    x2, dy, gate, w, wd, w_gate, w_up, h1, pr, hit, small, n_rep, n_shard
):
    tokens, width = x2.shape
    experts, f_loc = wd.shape[:2]
    seq, rows, cols, half = tokens // n_shard, width // n_shard, 2 * f_loc, n_shard // 2
    head_units = HEAD_UNITS if n_rep == 4 else 0
    units = 3 * experts + 8
    ahead = SENT_AHEAD if head_units else 0
    slots = max(head_units, 1) + ahead
    unit = (width // 2, cols)
    dma = pltpu.SemaphoreType.DMA
    anyspec = pl.BlockSpec(memory_space=pl.ANY)
    shape = jax.ShapeDtypeStruct
    return pl.pallas_call(
        partial(expert_kernel, n_rep, n_shard, experts, f_loc, head_units, ahead),
        out_shape=(
            shape((units,) + unit, BF),
            shape((units if head_units else 1,) + unit, BF),
            shape((units if head_units else 1,) + unit, BF),
            shape((units if head_units else 1,) + unit, BF),
            shape((experts, tokens, f_loc), BF),
            shape((seq, width), BF),
            shape((seq, width), F32),
            shape((16, width), F32),
            shape(wd.shape, BF),
        ),
        in_specs=[anyspec] * 11,
        out_specs=(anyspec,) * 9,
        scratch_shapes=[
            pltpu.VMEM((tokens, width), BF),
            pltpu.VMEM((width, tokens), BF),
            pltpu.VMEM((tokens, width), BF),
            pltpu.VMEM(gate.shape, F32),
            pltpu.VMEM((n_shard, rows, experts * cols), BF),
            pltpu.VMEM(wd.shape, BF),
            pltpu.VMEM((2, tokens, f_loc), BF),
            pltpu.VMEM((experts, half, 2, seq, cols), BF),
            pltpu.VMEM(gate.shape, F32),
            pltpu.VMEM((2,) + unit, BF),
            pltpu.VMEM((2, n_shard, rows, cols), BF),
            pltpu.VMEM((half, seq, width), BF),
            pltpu.VMEM((half, seq, width), BF),
            pltpu.VMEM((half - 1, seq, width), BF),
            pltpu.VMEM((seq, width), F32),
            pltpu.VMEM((n_shard - 1, seq, gate.shape[1]), F32),
            pltpu.VMEM((2, 2) + w_gate.shape[1:], F32),
            pltpu.VMEM((2, n_shard, rows, cols), BF),
            pltpu.VMEM((2,) + wd.shape[1:], F32),
            pltpu.VMEM(h1.shape, F32),
            pltpu.VMEM(pr.shape, F32),
            pltpu.VMEM(hit.shape, F32),
            pltpu.VMEM(small.shape, F32),
            pltpu.VMEM((seq, width), BF),
            pltpu.VMEM((16, width), F32),
            pltpu.VMEM(unit if head_units else (8, cols), BF),
            pltpu.VMEM(unit if head_units else (8, cols), BF),
            pltpu.VMEM((4 if head_units else 1,) + unit, BF),
            pltpu.VMEM((2 if head_units else 1,) + unit, BF),
            dma((7,)),
            dma((2, experts)),
            dma((2,)),
            dma((2, 2)),
            dma((2, n_shard)),
            dma((experts, n_shard)),
            dma((2,)),
            dma((2,)),
            dma((2, n_shard)),
            dma((experts, n_shard)),
            dma((n_shard,)),
            dma((n_shard,)),
            dma((n_shard,)),
            dma((n_shard,)),
            dma((half,)),
            dma((half,)),
            dma,
        ]
        + line_scratch(slots),
        compiler_params=pltpu.CompilerParams(
            collective_id=1, has_side_effects=True, vmem_limit_bytes=67000000
        ),
        name="experts",
    )(x2, dy, gate, w, wd, w_gate, w_up, h1, pr, hit, small)


def attention_kernel(
    n_rep, n_shard, experts, f_loc, head_units, ahead,
    da_hbm, x1_hbm, a_hbm, wqkv_hbm, wo_hbm, qkvr_hbm, q_hbm, k_hbm, seg_hbm, table_hbm, gain_hbm,
    gh_hbm, wd_hbm, tok_hbm, pay_hbm, h1_hbm, dh1_hbm, small_hbm, part_in, into1_in, into2_in, total_in,
    part, into1, into2, total, gtok_out, out_out, pay_out,
    da, x1, a, wqkv, wo, qkvr, q, k, seg, table, gain, gh, wd, tok, pay, h1, dh1, small,
    do, dqkv, ggain, payin, payrep, dstage, gstage, stage, in1, in2, acc,
    pbuf, ibuf, sbuf, tbuf,
    ld_sem, f_send, f_recv, d_sem, l_sem, a_send, a_recv,
    rs_j, rr_j, rs_b, rr_b, ts_j, tr_j, ts_b, tr_b, p_send, p_recv, q_send, q_recv, o_sem,
    z1, y1, z2, y2, z3, y3, zl, zs,
):
    me = lax.axis_index("shard")
    half, seq, width = stage.shape
    tokens = n_shard * seq
    rows = width // n_shard
    cols = rows
    heads = cols // HEAD_DIM
    scale = HEAD_DIM ** (-0.5)
    first_unit = 3 * experts
    pairs = (
        (x1_hbm, x1), (a_hbm, a), (wo_hbm, wo), (qkvr_hbm, qkvr), (q_hbm, q), (k_hbm, k),
        (seg_hbm, seg), (table_hbm, table), (gain_hbm, gain), (wqkv_hbm, wqkv), (gh_hbm, gh),
        (wd_hbm, wd), (tok_hbm, tok), (pay_hbm, pay),
        (h1_hbm, h1), (dh1_hbm, dh1), (small_hbm, small),
    )
    loads = [pltpu.make_async_copy(x, y, ld_sem.at[i]) for i, (x, y) in enumerate(pairs)]
    mine = pltpu.make_async_copy(da_hbm, da.at[0], ld_sem.at[len(pairs)])
    mine.start()
    for copy in loads:
        copy.start()
    meet(n_rep, n_shard)
    line = Line(
        part, into1, into2, total, (pbuf, ibuf, sbuf, tbuf), (z1, y1, z2, y2, z3, y3, zl, zs),
        head_units, ahead, CROSSED, WINDOW, LAG,
    )
    last_unit = first_unit + 8

    place_of = [head_units + sum(PUMPS[:i]) for i in range(len(PUMPS) + 1)]

    def pump(i):
        if head_units and PUMPS[i]:
            line.steps(place_of[i], place_of[i + 1], last_unit)

    if head_units:
        for u in range(WINDOW):
            line.launch(head_units + ahead + u)

    def block_cols(j, size):
        return pl.ds(pl.multiple_of(j * size, size), size)

    def cross_over():
        if head_units:
            for u in range(head_units, head_units + CROSSED):
                line.add_second(u)

    spread = spread_sends(da_hbm, da, f_send, f_recv, n_shard)
    for i in list(range(2, n_shard, 2)) + [1]:
        spread(i).start()
    cross_over()
    pump(0)
    for copy in loads[10:12]:
        copy.wait()

    def out_part(parity, j):
        total_block = None
        for e in range(experts):
            lhs = gh[e, :, parity].reshape(half * seq, f_loc)
            term = dot(lhs, wd[e, :, block_cols(j, cols)], ((1,), (0,)))
            total_block = term if total_block is None else total_block + term
        return total_block

    send_out, finish_out = scatter_blocks(
        out_part, width, rows, stage, in1.at[1], in2.at[1], acc.at[1], None,
        (ts_j, tr_j, ts_b, tr_b, None),
    )
    send_out()
    pump(1)
    for i in range(2, n_shard, 2):
        spread(i).wait_recv()
        spread(i + 1).start()
    for i in range(1, n_shard, 2):
        spread(i).wait_recv()
    for i in range(1, n_shard):
        spread(i).wait_send()
    mine.wait()
    for copy in loads[:9]:
        copy.wait()
    pump(2)

    at = a[...].T

    def out_block(j, c):
        r = block_cols(lax.rem(j, half), cols)
        value = jnp.dot(
            at, da[:, :, block_cols(j, cols)].reshape(tokens, cols), preferred_element_type=F32
        )
        dstage[j // half, r, :] = value.astype(BF)
        return c

    lax.fori_loop(0, n_shard, out_block, 0)
    outs = [
        pltpu.make_async_copy(dstage.at[i], part.at[first_unit + i], d_sem.at[i]) for i in range(2)
    ]
    for copy in outs:
        copy.start()

    def do_block(i, c):
        r = block_cols(i, 2 * seq)
        lhs = da[pl.ds(2 * i, 2)].reshape(2 * seq, width)
        do[r, :] = dot(lhs, wo[...], ((1,), (1,))).astype(BF)
        return c

    lax.fori_loop(0, half, do_block, 0)
    for copy in outs:
        copy.wait()
    pump(3)
    finish_out()

    cosine, sine = (table[0], table[1])

    def head_grad(grad, x, gain_row):
        inverse = lax.rsqrt(jnp.mean(x * x, axis=-1, keepdims=True) + epsilon)
        x_hat = x * inverse
        back = grad * cosine - pltpu.roll(grad, HEAD_DIM // 2, 1) * sine
        scaled = back * gain_row
        value = inverse * (scaled - x_hat * jnp.mean(scaled * x_hat, axis=-1, keepdims=True))
        return (value.astype(BF), jnp.sum(back * x_hat, axis=0, keepdims=True))

    ggain[...] = jnp.zeros_like(ggain)

    def sequence(b, carry):
        r = block_cols(b, seq)
        row = jnp.broadcast_to(seg[b].astype(F32), (seq, seq))
        same = row == row.T
        for i in range(heads):
            c = slice(i * HEAD_DIM, (i + 1) * HEAD_DIM)
            qr, kr, v = (qkvr[n, r, c] for n in range(3))
            d = do[r, c]
            s = jnp.where(same, dot(qr, kr, ((1,), (1,))) * scale, -1000000000.0)
            e = jnp.exp(s - jnp.max(s, axis=-1, keepdims=True))
            p = e / jnp.sum(e, axis=-1, keepdims=True)
            dv = dot(p.astype(BF).T, d, ((1,), (0,)))
            dp = dot(d, v, ((1,), (1,)))
            ds = (p * (dp - jnp.sum(p * dp, axis=-1, keepdims=True))).astype(BF)
            dqr = dot(ds, kr, ((1,), (0,))) * scale
            dkr = dot(ds.T, qr, ((1,), (0,))) * scale
            dq, gq = head_grad(dqr, q[r, c], gain[0:1, :])
            dk, gk = head_grad(dkr, k[r, c], gain[1:2, :])
            dqkv[0, r, c] = dq
            dqkv[1, r, c] = dk
            dqkv[2, r, c] = dv.astype(BF)
            ggain[0:1, :] = ggain[0:1, :] + gq
            ggain[1:2, :] = ggain[1:2, :] + gk
        return carry

    lax.fori_loop(0, half, sequence, 0)
    pump(4)
    lax.fori_loop(half, n_shard, sequence, 0)
    pump(5)
    for copy in (loads[9], *loads[12:]):
        copy.wait()

    def place(n, owner):
        start = pl.multiple_of(lax.rem(owner, half) * rows, rows)
        unit = first_unit + 2 + 2 * (2 - n) + owner // half
        return part.at[unit, pl.ds(start, rows), :]

    def send_block(n, b):
        return remote(gstage.at[n, b], place(n, me), a_send.at[n, b], a_recv.at[n, b], peer(b))

    def own_block(n):
        return pltpu.make_async_copy(gstage.at[n, 0], place(n, me), l_sem.at[n])

    def weight_grad(i, carry):
        n = 2 - i
        grad_t = dqkv[n].T

        def block(b, c):
            owner = me ^ b
            value = jnp.dot(
                grad_t,
                x1[:, :, block_cols(owner, rows)].reshape(tokens, rows),
                preferred_element_type=F32,
            )
            gstage[n, b] = value.T.astype(BF)

            @pl.when(b > 0)
            def _():
                send_block(n, b).start()

            return c

        lax.fori_loop(0, n_shard, block, 0)
        own_block(n).start()
        return carry

    lax.fori_loop(0, 3, weight_grad, 0)
    pump(6)

    def grad_ready(n):
        for b in range(1, n_shard):
            send_block(n, b).wait()
        own_block(n).wait()

    def dx1_block(parity, j):
        total_block = None
        for n in range(3):
            lhs = dqkv[n].reshape(half, 2, seq, cols)[:, parity].reshape(half * seq, cols)
            term = dot(lhs, wqkv[block_cols(j, rows), n * cols : (n + 1) * cols], ((1,), (1,)))
            total_block = term if total_block is None else total_block + term
        return total_block

    send_dx1, finish_dx1 = scatter_blocks(
        dx1_block, width, rows, stage, in1.at[0], in2.at[0], acc.at[0], None,
        (rs_j, rr_j, rs_b, rr_b, None),
    )
    pump(7)
    for n in (2, 1, 0):
        grad_ready(n)
    send_dx1()
    pump(8)
    pump(9)
    finish_dx1()
    pump(10)

    rank = lax.axis_index("rep")
    h = tok[...].astype(F32)
    r1 = lax.rsqrt(jnp.mean(h * h, axis=-1, keepdims=True) + epsilon)
    n1 = h * r1
    dx1 = acc[0]
    pay[0:1, :] = jnp.sum(dx1 * n1, axis=0, keepdims=True)
    e1 = dx1 * small[0:1, :].astype(BF).astype(F32)
    dh1[...] = dh1[...] + r1 * (e1 - n1 * jnp.mean(e1 * n1, axis=-1, keepdims=True))
    tok[...] = (h1[...] + acc[1]).astype(BF)
    done = ((dh1, gtok_out), (tok, out_out))
    done = [pltpu.make_async_copy(x, y, o_sem.at[i]) for i, (x, y) in enumerate(done)]
    for copy in done:
        copy.start()
    for i in range(width // HEAD_DIM):
        pay[experts + 2 : experts + 4, i * HEAD_DIM : (i + 1) * HEAD_DIM] = ggain[0:2, :]

    def owner_copy(b):
        return remote(
            pay.at[:, block_cols(me ^ b, cols)], payin.at[b], p_send.at[b], p_recv.at[b], peer(b)
        )

    for b in range(1, n_shard):
        owner_copy(b).start()
    payin[0] = pay[:, block_cols(me, cols)]
    pump(11)
    for b in range(1, n_shard):
        owner_copy(b).wait()
        payin[0] = payin[0] + payin[b]

    def rep_copy(b):
        return remote(
            payin.at[0], payrep.at[rank], q_send.at[b], q_recv.at[b], along(rank ^ b)
        )

    for b in range(1, n_rep):
        rep_copy(b).start()
    payrep[rank] = payin[0]
    pump(12)
    for b in range(1, n_rep):
        rep_copy(b).wait()
    summed = payrep[0]
    for i in range(1, n_rep):
        summed = summed + payrep[i]
    payin[1] = summed
    copy = pltpu.make_async_copy(payin.at[1], pay_out, o_sem.at[2])
    copy.start()
    copy.wait()
    for copy in done:
        copy.wait()
    if head_units:
        line.steps(place_of[-1], last_unit, last_unit)
        line.finish(last_unit)


def attention_call(
    da, x1, a, wqkv, wo, qkvr, q, k, seg, table, gain, gh, wd, tok, pay, h1, dh1, small, part, into1,
    into2, total, n_rep, n_shard, head_units,
):
    seq, width = da.shape
    tokens, cols = a.shape
    experts, f_loc = wd.shape[:2]
    half = n_shard // 2
    units = part.shape[0]
    slots = units - head_units if head_units else 1
    unit = part.shape[1:]
    gh = gh.reshape(experts, half, 2, seq, f_loc)
    dma = pltpu.SemaphoreType.DMA
    anyspec = pl.BlockSpec(memory_space=pl.ANY)
    shape = jax.ShapeDtypeStruct
    whole = (x1, a, wqkv, wo, qkvr, q, k, seg, table, gain, gh, wd, tok, pay, h1, dh1, small)
    return pl.pallas_call(
        partial(
            attention_kernel, n_rep, n_shard, experts, f_loc, head_units,
            SENT_AHEAD if head_units else 0,
        ),
        out_shape=(
            shape(part.shape, BF),
            shape(into1.shape, BF),
            shape(into2.shape, BF),
            shape(total.shape, BF),
            shape((seq, width), F32),
            shape((seq, width), BF),
            shape((pay.shape[0], width // n_shard), F32),
        ),
        in_specs=[anyspec] * 22,
        out_specs=(anyspec,) * 7,
        input_output_aliases={18: 0, 19: 1, 20: 2, 21: 3},
        scratch_shapes=[pltpu.VMEM((n_shard, seq, width), BF)]
        + [pltpu.VMEM(x.shape, x.dtype) for x in whole]
        + [
            pltpu.VMEM((tokens, cols), BF),
            pltpu.VMEM((3, tokens, cols), BF),
            pltpu.VMEM((8, HEAD_DIM), F32),
            pltpu.VMEM((n_shard, pay.shape[0], cols), F32),
            pltpu.VMEM((n_rep, pay.shape[0], cols), F32),
            pltpu.VMEM((2,) + unit, BF),
            pltpu.VMEM((3, n_shard, cols, cols), BF),
            pltpu.VMEM((half, seq, width), BF),
            pltpu.VMEM((2, half, seq, width), BF),
            pltpu.VMEM((2, half - 1, seq, width), BF),
            pltpu.VMEM((2, seq, width), F32),
            pltpu.VMEM(unit, BF),
            pltpu.VMEM(unit, BF),
            pltpu.VMEM((4 if head_units else 1,) + unit, BF),
            pltpu.VMEM((2 if head_units else 1,) + unit, BF),
            dma((18,)),
            dma((n_shard,)),
            dma((n_shard,)),
            dma((2,)),
            dma((3,)),
            dma((3, n_shard)),
            dma((3, n_shard)),
            dma((n_shard,)),
            dma((n_shard,)),
            dma((half,)),
            dma((half,)),
            dma((n_shard,)),
            dma((n_shard,)),
            dma((half,)),
            dma((half,)),
            dma((n_shard,)),
            dma((n_shard,)),
            dma((n_rep,)),
            dma((n_rep,)),
            dma((3,)),
        ]
        + line_scratch(slots),
        compiler_params=pltpu.CompilerParams(
            collective_id=2, has_side_effects=True, vmem_limit_bytes=67000000
        ),
        name="attention",
    )(da, *whole, part, into1, into2, total)


def forward_kernel(
    n_rep, n_shard, experts, head,
    tok_hbm, small_hbm, seg_hbm, route_hbm, dy_hbm, wq_hbm, wk_hbm, wv_hbm, wo_hbm, table_hbm,
    wg_hbm, wu_hbm,
    x1_out, x2_out, dy_out, gate_out, w_out, wqkv_out, wo_out, qkvr_out, q_out, k_out, a_out,
    seg_out, h1_out, pr_out, small_out, hit_out, gain_out,
    tok, small, seg, hit, gain, route, wf, wof, table, x1, wqkv, wst, wo, qkvr, q, k, a, x2, gate, pr,
    stage, in1, in2, acc, fbuf, cstage,
    ld_sem, t_send, t_recv, s_send, s_recv, e_send, e_recv, w_send, w_recv, d_send, d_recv,
    x_send, x_recv, g_send, g_recv, c_ld, c_send, c_recv, o_sem, rs_j, rr_j, rs_b, rr_b,
):
    me = lax.axis_index("shard")
    half, seq, width = stage.shape
    rows = width // n_shard
    cols = rows
    tokens = n_shard * seq
    heads = cols // HEAD_DIM
    scale = HEAD_DIM ** (-0.5)
    cut = w_out.shape[2] // head

    def block_cols(j, size):
        return pl.ds(pl.multiple_of(j * size, size), size)

    pairs = (
        (tok_hbm, tok.at[0]), (small_hbm, small.at[:, block_cols(me, rows)]),
        (wq_hbm, wf.at[0]), (wk_hbm, wf.at[1]), (wv_hbm, wf.at[2]), (wo_hbm, wof),
        (seg_hbm, seg.at[0]), (route_hbm, route), (table_hbm, table),
    )
    loads = [pltpu.make_async_copy(x, y, ld_sem.at[i]) for i, (x, y) in enumerate(pairs)]
    for copy in loads:
        copy.start()
    columns = Columns(
        wg_hbm, wu_hbm, lambda e, src: w_out.at[src, :, block_cols(e, cut)], fbuf, cstage,
        (c_ld, c_send, c_recv), 0, head,
    )
    for e in range(min(head, 2)):
        columns.load(e)
    dy_own = pltpu.make_async_copy(dy_hbm, dy_out.at[0], ld_sem.at[len(pairs)])
    dy_own.start()
    meet(n_rep, n_shard)

    def small_copy(b):
        return remote(
            small_hbm, small.at[:, block_cols(me, rows)], s_send.at[b], s_recv.at[b], peer(b)
        )

    def seg_copy(b):
        return remote(seg_hbm, seg.at[b], e_send.at[b], e_recv.at[b], peer(b))

    for b in range(1, n_shard):
        small_copy(b).start()
        seg_copy(b).start()
    spread = spread_sends(tok_hbm, tok, t_send, t_recv, n_shard)
    for i in list(range(2, n_shard, 2)) + [1]:
        spread(i).start()

    def w_copy(owner):
        away = owner ^ me
        return remote(
            wst.at[owner], wqkv.at[block_cols(me, rows), :], w_send.at[away], w_recv.at[away],
            peer(away),
        )

    for copy in loads[2:5]:
        copy.wait()

    def cast_block(owner, c):
        wst[owner] = jnp.concatenate(
            [wf[i, :, block_cols(owner, cols)] for i in range(3)], axis=1
        ).astype(BF)

        @pl.when(owner != me)
        def _():
            w_copy(owner).start()

        return c

    lax.fori_loop(0, n_shard, cast_block, 0)
    wqkv[block_cols(me, rows), :] = wst[me]
    for copy in (loads[0], loads[1], *loads[5:]):
        copy.wait()
    wo[...] = wof[...].astype(BF)
    for b in range(1, n_shard):
        small_copy(b).wait()
        seg_copy(b).wait()
    gain_attn = small[0:1, :].astype(BF).astype(F32)
    lane = lax.broadcasted_iota(jnp.int32, hit.shape, 1)
    named = jnp.zeros(hit.shape, F32)
    for j in range(route.shape[1]):
        named = named + (lane == route[:, j : j + 1]).astype(F32)
    hit[...] = named

    def norm_first(i):
        h = tok[i].astype(F32)
        n1 = h * lax.rsqrt(jnp.mean(h * h, axis=-1, keepdims=True) + epsilon)
        x1[i] = (n1 * gain_attn).astype(BF)

    norm_first(0)
    spread(1).wait_recv()
    norm_first(1)
    for i in range(2, n_shard, 2):
        spread(i).wait_recv()
        spread(i + 1).start()
        norm_first(i)
    for i in range(3, n_shard, 2):
        spread(i).wait_recv()
        norm_first(i)
    for b in range(1, n_shard):
        w_copy(me ^ b).wait_recv()

    spread_dy = spread_sends(dy_hbm, dy_out, d_send, d_recv, n_shard)
    for i in list(range(2, n_shard, 2)) + [1]:
        spread_dy(i).start()

    keeps = []

    def keep(e, slot):
        copy = pltpu.make_async_copy(
            cstage.at[slot, me], w_out.at[me, :, block_cols(e, cut)], o_sem.at[14 + e]
        )
        copy.start()
        keeps.append(copy)

    for e in range(head):
        columns.prepare(e, keep)

    def spread_gain(row):
        hd = HEAD_DIM // n_shard
        total = small[row : row + 1, :HEAD_DIM]
        for j in range(1, n_shard):
            part = small[row : row + 1, j * rows : j * rows + HEAD_DIM]
            total = total + pltpu.roll(part, j * hd, 1)
        return total.astype(BF).astype(F32)

    gain_q = spread_gain(experts + 2)
    gain_k = spread_gain(experts + 3)
    gain[...] = jnp.concatenate([gain_q, gain_k, jnp.zeros((6, HEAD_DIM), F32)], axis=0)
    cosine, sine = (table[0], table[1])

    def turned(x, gain):
        hat = x * lax.rsqrt(jnp.mean(x * x, axis=-1, keepdims=True) + epsilon) * gain
        return (hat * cosine + pltpu.roll(hat, HEAD_DIM // 2, 1) * sine).astype(BF)

    def two_sequences(i, carry):
        y = jnp.dot(
            x1[pl.ds(2 * i, 2)].reshape(2 * seq, width), wqkv[...], preferred_element_type=F32
        )
        r2 = block_cols(i, 2 * seq)
        q[r2, :] = y[:, :cols]
        k[r2, :] = y[:, cols : 2 * cols]
        qkvr[2, r2, :] = y[:, 2 * cols :].astype(BF)
        for j in range(2):
            r = block_cols(2 * i + j, seq)
            row = jnp.broadcast_to(seg[2 * i + j].astype(F32), (seq, seq))
            same = row == row.T
            for n in range(heads):
                c = slice(n * HEAD_DIM, (n + 1) * HEAD_DIM)
                qr = turned(q[r, c], gain_q)
                kr = turned(k[r, c], gain_k)
                qkvr[0, r, c] = qr
                qkvr[1, r, c] = kr
                s = jnp.where(same, dot(qr, kr, ((1,), (1,))) * scale, -1000000000.0)
                e = jnp.exp(s - jnp.max(s, axis=-1, keepdims=True))
                p = e / jnp.sum(e, axis=-1, keepdims=True)
                a[r, c] = dot(p.astype(BF), qkvr[2, r, c], ((1,), (0,))).astype(BF)
        return carry

    lax.fori_loop(0, half, two_sequences, 0)
    stores = [
        (q, q_out), (k, k_out), (qkvr, qkvr_out), (a, a_out), (x1, x1_out), (wqkv, wqkv_out),
        (wo, wo_out), (seg, seg_out), (small, small_out), (hit, hit_out),
        (gain, gain_out),
    ]
    stores = [pltpu.make_async_copy(x, y, o_sem.at[i]) for i, (x, y) in enumerate(stores)]

    def out_block(parity, j):
        lhs = a[...].reshape(half, 2, seq, cols)[:, parity].reshape(half * seq, cols)
        return dot(lhs, wo[:, block_cols(j, rows)], ((1,), (0,)))

    send, finish = scatter_blocks(
        out_block, width, rows, stage, in1, in2, acc, None, (rs_j, rr_j, rs_b, rr_b, None)
    )
    send()
    for i in range(2, n_shard, 2):
        spread_dy(i).wait_recv()
        spread_dy(i + 1).start()
    finish()
    h1 = tok[0].astype(F32) + acc[...]
    acc[...] = h1
    n2 = h1 * lax.rsqrt(jnp.mean(h1 * h1, axis=-1, keepdims=True) + epsilon)
    x2[...] = (n2 * small[1:2, :].astype(BF).astype(F32)).astype(BF)
    spread_x2 = spread_sends(x2, x2_out, x_send, x_recv, n_shard)
    for i in list(range(2, n_shard, 2)) + [1]:
        spread_x2(i).start()
    own = pltpu.make_async_copy(x2, x2_out.at[0], o_sem.at[11])
    own.start()
    lane = lax.broadcasted_iota(jnp.int32, (seq, 16), 1)
    z = dot(x2[...], small[...].astype(BF), ((1,), (1,)))
    valid = (lane >= 2) & (lane < experts + 2)
    z = jnp.where(valid, z, -1e30)
    e = jnp.exp(z - jnp.max(z, axis=-1, keepdims=True))
    probs = e / jnp.sum(e, axis=-1, keepdims=True)
    probs = jnp.concatenate([probs, jnp.zeros((seq, gate.shape[1] - 16), F32)], axis=1)
    probs = pltpu.roll(probs, gate.shape[1] - 2, 1)
    pr[...] = probs
    gate[...] = probs * hit[...]

    def gate_copy(b):
        return remote(gate, gate_out.at[b], g_send.at[b], g_recv.at[b], peer(b))

    for b in range(1, n_shard):
        gate_copy(b).start()
    more = [(gate, gate_out.at[0]), (pr, pr_out)]
    more = [pltpu.make_async_copy(x, y, o_sem.at[12 + i]) for i, (x, y) in enumerate(more)]
    last = pltpu.make_async_copy(acc, h1_out, ld_sem.at[0])
    for copy in (*stores, *more, last):
        copy.start()
    for i in range(2, n_shard, 2):
        spread_x2(i).wait_recv()
        spread_x2(i + 1).start()
    for i in range(1, n_shard, 2):
        spread_x2(i).wait_recv()
        spread_dy(i).wait_recv()
    for b in range(1, n_shard):
        gate_copy(b).wait()
        spread(b).wait_send()
        spread_dy(b).wait_send()
        spread_x2(b).wait_send()
        w_copy(me ^ b).wait_send()
    for e in range(head):
        columns.arrived(e)
        columns.sent(e)
    dy_own.wait()
    for copy in (own, *stores, *more, last, *keeps):
        copy.wait()


def forward_call(
    tok, small, seg, route, dy, wq, wk, wv, wo, table, w_gate, w_up, n_rep, n_shard, head
):
    seq, width = tok.shape
    experts = w_gate.shape[0]
    rows, half, tokens = width // n_shard, n_shard // 2, n_shard * seq
    cols = rows
    dma = pltpu.SemaphoreType.DMA
    anyspec = pl.BlockSpec(memory_space=pl.ANY)
    shape = jax.ShapeDtypeStruct
    group = (n_shard, seq, width)
    lanes = (seq, 128)
    return pl.pallas_call(
        partial(forward_kernel, n_rep, n_shard, experts, head),
        out_shape=(
            shape(group, BF),
            shape(group, BF),
            shape(group, BF),
            shape((n_shard,) + lanes, F32),
            shape((n_shard, rows, head * cols), BF),
            shape((width, 3 * cols), BF),
            shape((rows, width), BF),
            shape((3, tokens, cols), BF),
            shape((tokens, cols), F32),
            shape((tokens, cols), F32),
            shape((tokens, cols), BF),
            shape((n_shard,) + seg.shape, seg.dtype),
            shape((seq, width), F32),
            shape(lanes, F32),
            shape((16, width), F32),
            shape(lanes, F32),
            shape((8, HEAD_DIM), F32),
        ),
        in_specs=[anyspec] * 12,
        out_specs=(anyspec,) * 17,
        scratch_shapes=[
            pltpu.VMEM(group, BF),
            pltpu.VMEM((16, width), F32),
            pltpu.VMEM((n_shard,) + seg.shape, seg.dtype),
            pltpu.VMEM(lanes, F32),
            pltpu.VMEM((8, HEAD_DIM), F32),
            pltpu.VMEM(route.shape, route.dtype),
            pltpu.VMEM((3, rows, width), F32),
            pltpu.VMEM((rows, width), F32),
            pltpu.VMEM(table.shape, F32),
            pltpu.VMEM(group, BF),
            pltpu.VMEM((width, 3 * cols), BF),
            pltpu.VMEM((n_shard, rows, 3 * cols), BF),
            pltpu.VMEM((rows, width), BF),
            pltpu.VMEM((3, tokens, cols), BF),
            pltpu.VMEM((tokens, cols), F32),
            pltpu.VMEM((tokens, cols), F32),
            pltpu.VMEM((tokens, cols), BF),
            pltpu.VMEM((seq, width), BF),
            pltpu.VMEM(lanes, F32),
            pltpu.VMEM(lanes, F32),
            pltpu.VMEM((half, seq, width), BF),
            pltpu.VMEM((half, seq, width), BF),
            pltpu.VMEM((half - 1, seq, width), BF),
            pltpu.VMEM((seq, width), F32),
            pltpu.VMEM((2, 2) + w_gate.shape[1:], F32),
            pltpu.VMEM((2, n_shard, rows, cols), BF),
            dma((10,)),
        ]
        + [dma((n_shard,)) for _ in range(14)]
        + [
            dma((2, 2)),
            dma((2, n_shard)),
            dma((head, n_shard)),
            dma((14 + head,)),
            dma((n_shard,)),
            dma((n_shard,)),
            dma((half,)),
            dma((half,)),
        ],
        compiler_params=pltpu.CompilerParams(
            collective_id=3, has_side_effects=True, vmem_limit_bytes=67000000
        ),
        name="forward",
    )(tok, small, seg, route, dy, wq, wk, wv, wo, table, w_gate, w_up)


def unpack_experts(n_shard, d, ga, gb, gate, up, down):
    x = (ga, gb)
    rows, hidden = gate.shape[1:]
    f_loc = hidden // n_shard
    cols = 2 * f_loc
    half = n_shard // 2
    for j in range(n_shard):
        r = slice((j % half) * rows, (j % half + 1) * rows)
        gate[0, :, j * f_loc : (j + 1) * f_loc] = x[j // half][0, r, :f_loc].astype(F32)
        up[0, :, j * f_loc : (j + 1) * f_loc] = x[j // half][0, r, f_loc:].astype(F32)
    for j in range(down.shape[2] // cols):
        down[0, :, j * cols : (j + 1) * cols] = d[0, j * f_loc : (j + 1) * f_loc, :].astype(F32)


def unpack_attention(*refs):
    rows = refs[4].shape[0]
    for x, out in zip(refs[:4], refs[4:]):
        cols = x.shape[2]
        for j in range(2):
            out[:, j * cols : (j + 1) * cols] = x[0, j * rows : (j + 1) * rows, :].astype(F32)


def unpack(total, experts, n_shard):
    depth, cols = total.shape[1:]
    width, f_loc = 2 * depth, cols // 2
    rows = width // n_shard
    hidden = n_shard * f_loc
    shape = jax.ShapeDtypeStruct
    by = lambda e: (e, 0, 0)
    params = pltpu.CompilerParams(vmem_limit_bytes=48 << 20)
    gate, up, down = pl.pallas_call(
        partial(unpack_experts, n_shard),
        grid=(experts,),
        out_shape=(
            shape((experts, rows, hidden), F32),
            shape((experts, rows, hidden), F32),
            shape((experts, f_loc, width), F32),
        ),
        in_specs=[
            pl.BlockSpec((1, depth, cols), lambda e: (down_at(e), 0, 0)),
            pl.BlockSpec((1, depth, cols), lambda e: (gate_up_at(e, experts), 0, 0)),
            pl.BlockSpec((1, depth, cols), lambda e: (gate_up_at(e, experts) + 1, 0, 0)),
        ],
        out_specs=(
            pl.BlockSpec((1, rows, hidden), by),
            pl.BlockSpec((1, rows, hidden), by),
            pl.BlockSpec((1, f_loc, width), by),
        ),
        compiler_params=params,
        name="unpack_experts",
    )(total, total, total)
    return gate, up, down


def unpack_rest(total, first, n_shard):
    depth, cols = total.shape[1:]
    width, half = 2 * depth, n_shard // 2
    rows = width // n_shard

    def unit(i):
        step = half // 2
        return pl.BlockSpec((1, 2 * rows, cols), lambda j: (first + 2 * i + j // step, j % step, 0))

    return pl.pallas_call(
        unpack_attention,
        grid=(half,),
        out_shape=(jax.ShapeDtypeStruct((rows, width), F32),) * 4,
        in_specs=[unit(i) for i in range(4)],
        out_specs=(pl.BlockSpec((rows, 2 * cols), lambda j: (0, j)),) * 4,
        name="unpack_attention",
    )(*([total] * 4))


def shards(
    tokens, segments, routes, slot_ids, attn_gain, w_query, w_key, w_value, w_out,
    query_gain, key_gain, ffn_gain, router, w_gate, w_up, w_down, cotangent,
):
    n_shard = lax.axis_size("shard")
    me = lax.axis_index("shard")
    seq, width = tokens.shape
    experts, rows, hidden_f = w_gate.shape
    f_loc = w_down.shape[1]
    cols = width // n_shard
    group = n_shard * seq
    n_rep = lax.axis_size("rep")
    hd = HEAD_DIM // n_shard

    row = jnp.arange(16)[:, None]

    def wide(g):
        return jnp.pad(g, (0, rows - g.shape[0]))[None]

    small = jnp.pad(router.T, ((2, 14 - experts), (0, 0)))
    for i, g in (
        (0, attn_gain), (1, ffn_gain), (experts + 2, query_gain), (experts + 3, key_gain)
    ):
        small = jnp.where(row == i, wide(g), small)
    cosine, sine = rope_tables(seq, HEAD_DIM)
    cos2, sin2 = (cosine[:, 0], sine[:, 0])
    table = jnp.stack(
        [jnp.concatenate([cos2, cos2], axis=1), jnp.concatenate([-sin2, sin2], axis=1)]
    )
    (
        x1_all, x2_all, dy_all, gate_all, gu, qkv, w_out_b, qkvr, q, k, a, seg_all, h1, pr, small,
        hit, gains,
    ) = forward_call(
        tokens, small, segments.reshape(1, seq), routes, cotangent, w_query, w_key, w_value, w_out, table,
        w_gate, w_up, n_rep, n_shard, HEAD_EXPERTS,
    )
    part, into1, into2, total, gh, da, dh1, pay, w_down_b = experts_call(
        x2_all.reshape(group, width), dy_all.reshape(group, width), gate_all.reshape(group, -1),
        gu, w_down, w_gate, w_up, h1, pr, hit, small, n_rep, n_shard,
    )
    part, _, _, total, grad_tokens, output, sums = attention_call(
        da, x1_all, a, qkv, w_out_b, qkvr, q, k, seg_all, table,
        gains, gh, w_down_b, tokens, pay, h1, dh1,
        small, part, into1, into2, total,
        n_rep, n_shard, HEAD_UNITS if n_rep == 4 else 0,
    )
    summed = total if n_rep == 4 else lax.psum(part, "rep")
    gw_gate, gw_up, gw_down = unpack(summed, experts, n_shard)
    gw_out, gw_value, gw_key, gw_query = unpack_rest(summed, 3 * experts, n_shard)
    small = sums
    gg_query = lax.dynamic_slice(small[experts + 2, :HEAD_DIM], (me * hd,), (hd,))
    gg_key = lax.dynamic_slice(small[experts + 3, :HEAD_DIM], (me * hd,), (hd,))
    return (
        output,
        grad_tokens,
        small[0],
        gw_query,
        gw_key,
        gw_value,
        gw_out,
        gg_query,
        gg_key,
        small[1],
        small[2 : experts + 2].T,
        gw_gate,
        gw_up,
        gw_down,
    )


def solution(mesh):
    both = P(("rep", "shard"), None)
    row = P("shard", None)
    vec = P("shard")
    exp = P(None, "shard", None)
    return jax.shard_map(
        shards,
        mesh=mesh,
        in_specs=(
            both, P(("rep", "shard")), both, both, vec, row, row, row, row,
            vec, vec, vec, row, exp, exp, exp, both,
        ),
        out_specs=(both, both, vec, row, row, row, row, vec, vec, vec, row, exp, exp, exp),
        check_vma=False,
    )
```

```python
from functools import partial

import jax
import jax.numpy as jnp
from jax import lax
from jax.experimental import pallas as pl
from jax.experimental.pallas import tpu as pltpu
from jax.sharding import PartitionSpec as P

HEAD_DIM = 128
HEAD_UNITS = 20
HEAD_EXPERTS = 1
SENT_AHEAD = 3
CROSSED = 2
WINDOW = 2
LAG = 1
PUMPS = (3, 1, 1, 1, 1, 1, 1, 1, 1, 2, 2, 1, 1)

epsilon = 1e-06
rope_base = 50000.0
BF = jnp.bfloat16
F32 = jnp.float32


def inverse_rms(value):
    return lax.rsqrt(jnp.mean(value * value, axis=-1, keepdims=True) + epsilon)


def rope_tables(seq_len, head_width):
    half_dim = head_width // 2
    position = jnp.arange(seq_len, dtype=jnp.float32)
    frequency = rope_base ** (-jnp.arange(half_dim, dtype=jnp.float32) * 2.0 / head_width)
    angles = position[:, None] * frequency[None, :]
    return (jnp.cos(angles)[:, None, :], jnp.sin(angles)[:, None, :])


def rotate(value, cosine, sine_table, direction):
    half_dim = value.shape[-1] // 2
    first_half = value[..., :half_dim]
    second_half = value[..., half_dim:]
    return jnp.concatenate(
        [
            first_half * cosine - direction * second_half * sine_table,
            second_half * cosine + direction * first_half * sine_table,
        ],
        axis=-1,
    )


def head_back(grad_rot, value_hat, inverse, scale_gain, cosine, sine_table):
    grad_scaled = rotate(grad_rot, cosine, sine_table, -1.0)
    grad_gain = jnp.sum(grad_scaled * value_hat, axis=(0, 1, 2))
    grad_hat = grad_scaled * scale_gain
    grad_value = inverse * (
        grad_hat - value_hat * jnp.mean(grad_hat * value_hat, axis=-1, keepdims=True)
    )
    return (grad_value.astype(BF), grad_gain)


def dot(a, b, dims):
    return lax.dot_general(a, b, (dims, ((), ())), preferred_element_type=F32)


MESH = pl.DeviceIdType.MESH


def peer(bits):
    return (lax.axis_index("rep"), lax.axis_index("shard") ^ bits)


def along(rank):
    return (rank, lax.axis_index("shard"))


def meet(n_rep, n_shard):
    barrier = pltpu.get_barrier_semaphore()
    for bits in range(1, n_shard):
        pl.semaphore_signal(barrier, inc=1, device_id=peer(bits), device_id_type=MESH)
    rep, shard = lax.axis_index("rep"), lax.axis_index("shard")
    for bits in range(1, n_rep):
        pl.semaphore_signal(barrier, inc=1, device_id=(rep ^ bits, shard), device_id_type=MESH)
    pl.semaphore_wait(barrier, n_shard + n_rep - 2)


def remote(src, dst, send, recv, to):
    return pltpu.make_async_remote_copy(
        src_ref=src, dst_ref=dst, send_sem=send, recv_sem=recv, device_id=to, device_id_type=MESH
    )


def down_at(e):
    return jnp.maximum(3 * e - 2, 0)


def gate_up_at(e, experts):
    return 3 * e + jnp.where(e == experts - 1, 1, 2)


class Line:
    def __init__(self, part, into1, into2, total, bufs, sems, base=0, landed=0, crossed=0, window=2, lag=2):
        self.part, self.into1, self.into2, self.total = part, into1, into2, total
        self.pbuf, self.ibuf, self.sbuf, self.tbuf = bufs
        (self.s1, self.r1, self.s2, self.r2, self.s3, self.r3, self.ld, self.st) = sems
        self.ring = self.sbuf.shape[0]
        self.base = base
        self.fresh = base + landed
        self.crossed = base + crossed
        self.lag = lag
        self.window = window
        rank = lax.axis_index("rep")
        self.middle = (rank == 1) | (rank == 2)
        self.end = (rank == 0) | (rank == 3)
        self.next = along(rank ^ 1)
        self.across = along(rank ^ 3)

    def first(self, u):
        i = u - self.base
        return remote(self.part.at[u], self.into1.at[u], self.s1.at[i], self.r1.at[i], self.next)

    def second(self, u):
        i = u - self.base
        slot = lax.rem(i, self.ring)
        return remote(
            self.sbuf.at[slot], self.into2.at[u], self.s2.at[i], self.r2.at[i], self.across
        )

    def third(self, u):
        i = u - self.base
        slot = lax.rem(i, 2)
        return remote(self.tbuf.at[slot], self.total.at[u], self.s3.at[i], self.r3.at[i], self.next)

    def keep(self, u):
        i = u - self.base
        slot = lax.rem(i, 2)
        return pltpu.make_async_copy(self.tbuf.at[slot], self.total.at[u], self.st.at[slot])

    def launch(self, u):
        @pl.when(self.end)
        def _():
            self.first(u).start()

    def add(self, dst, x, y):
        tile = 128

        def body(i, c):
            r = pl.ds(pl.multiple_of(i * tile, tile), tile)
            dst[r, :] = (x[r, :].astype(F32) + y[r, :].astype(F32)).astype(BF)
            return c

        lax.fori_loop(0, dst.shape[0] // tile, body, 0)

    def add_first(self, u):
        i = u - self.base

        @pl.when(self.middle & (u >= self.crossed))
        def _():
            own = pltpu.make_async_copy(self.part.at[u], self.pbuf, self.ld.at[0])
            own.start()

            @pl.when(u >= self.fresh)
            def _():
                self.first(u).wait_recv()

            got = pltpu.make_async_copy(self.into1.at[u], self.ibuf, self.ld.at[1])
            got.start()
            own.wait()
            got.wait()
            self.add(self.sbuf.at[lax.rem(i, self.ring)], self.pbuf, self.ibuf)
            self.second(u).start()

    def kept(self, u):
        slot = lax.rem(u - self.base, self.ring)
        return pltpu.make_async_copy(
            self.sbuf.at[slot], self.part.at[u], self.st.at[2 + lax.rem(u, 2)]
        )

    def add_second(self, u):
        i = u - self.base

        @pl.when(self.middle)
        def _():
            slot = lax.rem(i, self.ring)
            again = pltpu.make_async_copy(self.part.at[u], self.sbuf.at[slot], self.ld.at[0])

            @pl.when(u >= self.crossed)
            def _():
                self.second(u).wait_recv()

            @pl.when(u < self.crossed)
            def _():
                again.start()

            got = pltpu.make_async_copy(self.into2.at[u], self.ibuf, self.ld.at[1])
            got.start()

            @pl.when(i >= 2)
            def _():
                self.third(u - 2).wait_send()
                self.keep(u - 2).wait()

            @pl.when(u < self.crossed)
            def _():
                again.wait()

            got.wait()
            self.add(self.tbuf.at[lax.rem(i, 2)], self.sbuf.at[slot], self.ibuf)

            @pl.when(u >= self.crossed)
            def _():
                self.second(u).wait_send()

            self.third(u).start()
            self.keep(u).start()

    def step(self, u, limit):
        narrow = limit - 2 - self.window if self.window > 2 else 0

        @pl.when(self.end & (u >= self.fresh))
        def _():
            self.first(u).wait_send()

            @pl.when((u >= narrow + self.window - 2) & (u + 2 < limit))
            def _():
                self.first(u + 2).start()

            @pl.when(u < narrow)
            def _():
                self.first(u + self.window).start()

        self.add_first(u)

        @pl.when(u >= self.crossed + self.lag)
        def _():
            self.add_second(u - self.lag)

    def steps(self, low, high, limit):
        def body(u, c):
            self.step(u, limit)
            return c

        lax.fori_loop(low, high, body, 0)

    def finish(self, last, ahead=0, cross=0):
        for i in range(self.lag):
            self.add_second(last - self.lag + i)
            if i < cross:
                self.add_first(last + i)

                @pl.when(self.middle)
                def _():
                    self.kept(last + i).start()

        for u in range(last, last + ahead):
            @pl.when(self.end)
            def _():
                self.first(u).wait_send()
                if u + 2 < last + ahead:
                    self.first(u + 2).start()

            @pl.when(self.middle)
            def _():
                if u >= last + cross:
                    self.first(u).wait_recv()

        @pl.when(self.middle)
        def _():
            for u in range(last, last + cross):
                self.second(u).wait()
                self.kept(u).wait()

        @pl.when(self.middle)
        def _():
            for u in range(last - 2, last):
                self.third(u).wait_send()
                self.keep(u).wait()

        @pl.when(self.end)
        def _():
            def body(u, c):
                self.third(u).wait_recv()
                return c

            lax.fori_loop(self.base, last, body, 0)


def line_scratch(slots):
    dma = pltpu.SemaphoreType.DMA
    return [dma((slots,)) for _ in range(6)] + [dma((2,)), dma((4,))]


def scatter_blocks(block, width, step, stage, in1, in2, acc, out, sems):
    s1, r1, s2, r2, so = sems
    pairs, seq = stage.shape[0], stage.shape[1]

    def cols(j):
        return pl.ds(pl.multiple_of(j * step, step), step)

    def pair(j):
        return remote(
            stage.at[:, :, cols(j)], in1.at[:, :, cols(j)], s1.at[j], r1.at[j], peer(1)
        )

    def odd(j, c):
        stage[:, :, cols(j)] = block(1, j).reshape(pairs, seq, step).astype(BF)
        pair(j).start()
        return c

    n = width // step
    lax.fori_loop(0, n, odd, 0)

    def sent(j, c):
        pair(j).wait_send()
        return c

    lax.fori_loop(0, n, sent, 0)

    def even(j, c):
        value = block(0, j).reshape(pairs, seq, step)
        pair(j).wait_recv()
        value = value + in1[:, :, cols(j)].astype(F32)
        acc[:, cols(j)] = value[0]
        stage[:, :, cols(j)] = value.astype(BF)
        return c

    lax.fori_loop(0, n, even, 0)
    far = [
        remote(stage.at[i], in2.at[i - 1], s2.at[i], r2.at[i], peer(2 * i)) for i in range(1, pairs)
    ]

    def send():
        for copy in far:
            copy.start()

    def finish():
        for copy in far:
            copy.wait()
        for i in range(pairs - 1):
            acc[...] = acc[...] + in2[i].astype(F32)
        if out is not None:
            copy = pltpu.make_async_copy(acc, out, so)
            copy.start()
            copy.wait()

    return send, finish


class Columns:
    def __init__(self, gate_hbm, up_hbm, place, fbuf, stage, sems, first, last):
        self.gate, self.up, self.place = gate_hbm, up_hbm, place
        self.fbuf, self.stage = fbuf, stage
        self.ld, self.send, self.recv = sems
        self.first, self.last = first, last
        self.me = lax.axis_index("shard")
        self.n = stage.shape[1]

    def loads(self, e):
        slot = lax.rem(e, 2)
        return (
            pltpu.make_async_copy(self.gate.at[e], self.fbuf.at[slot, 0], self.ld.at[slot, 0]),
            pltpu.make_async_copy(self.up.at[e], self.fbuf.at[slot, 1], self.ld.at[slot, 1]),
        )

    def load(self, e):
        for copy in self.loads(e):
            copy.start()

    def copy_to(self, e, owner):
        away = owner ^ self.me
        slot = lax.rem(e, 2)
        return remote(
            self.stage.at[slot, owner], self.place(e, self.me), self.send.at[slot, away],
            self.recv.at[e, away], peer(away),
        )

    def sent(self, e):
        for b in range(1, self.n):
            self.copy_to(e, self.me ^ b).wait_send()

    def prepare(self, e, keep):
        for copy in self.loads(e):
            copy.wait()

        @pl.when(e >= self.first + 2)
        def _():
            self.sent(e - 2)

        slot = lax.rem(e, 2)
        size = self.fbuf.shape[3] // self.n
        for owner in range(self.n):
            c = slice(owner * size, (owner + 1) * size)
            block = jnp.concatenate([self.fbuf[slot, i, :, c] for i in range(2)], axis=1)
            self.stage[slot, owner] = block.astype(BF)

            @pl.when(owner != self.me)
            def _():
                self.copy_to(e, owner).start()

        keep(e, slot)

        @pl.when(e + 2 < self.last)
        def _():
            self.load(e + 2)

    def arrived(self, e):
        for b in range(1, self.n):
            self.copy_to(e, self.me ^ b).wait_recv()


def spread_sends(src, land, send, recv, n_shard):
    def copy(i):
        rows = src if i == 1 or i % 2 == 0 else land.at[i - 1]
        return remote(rows, land.at[i], send.at[i], recv.at[i], peer(i if i % 2 == 0 else 1))

    return copy


def expert_kernel(
    n_rep, n_shard, experts, f_loc, head_units, ahead,
    x2_hbm, dy_hbm, gate_hbm, w_hbm, wd_hbm, wg_hbm, wu_hbm, h1_hbm, pr_hbm, hit_hbm, small_hbm,
    part, into1, into2, total, gh_out, da_out, dh1_out, pay_out, wd_out,
    x2, x2t, dy, gate, w, wd, gh, dgu, dg, dstage, gstage, stage, in1, in2, acc, dgin,
    fbuf, cstage, wdf, h1, pr, hit, small, da, pay, pbuf, ibuf, sbuf, tbuf,
    ld_sem, w_sem, h_sem, c_ld, c_send, c_recv, d_sem, l_sem, a_send, a_recv, g_send, g_recv, rs_j, rr_j, rs_b, rr_b, o_sem,
    z1, y1, z2, y2, z3, y3, zl, zs,
):
    me = lax.axis_index("shard")
    tokens, width = x2.shape
    seq = tokens // n_shard
    rows = width // n_shard
    cols = 2 * f_loc
    half = n_shard // 2
    loads = [
        pltpu.make_async_copy(gate_hbm, gate, ld_sem.at[0]),
        pltpu.make_async_copy(x2_hbm, x2, ld_sem.at[1]),
        pltpu.make_async_copy(dy_hbm, dy, ld_sem.at[2]),
    ]
    late = ((h1_hbm, h1), (pr_hbm, pr), (hit_hbm, hit), (small_hbm, small))
    late = [pltpu.make_async_copy(x, y, ld_sem.at[3 + i]) for i, (x, y) in enumerate(late)]

    def ecols(e, size):
        return pl.ds(pl.multiple_of(e * size, size), size)

    head = w_hbm.shape[2] // cols

    def load_head(e):
        c = pl.ds(e * cols, cols)
        return pltpu.make_async_copy(w_hbm.at[:, :, c], w.at[:, :, c], w_sem.at[0, e])

    def load_down(e):
        slot = lax.rem(e, 2)
        return pltpu.make_async_copy(wd_hbm.at[e], wdf.at[slot], w_sem.at[1, slot])

    columns = Columns(
        wg_hbm, wu_hbm, lambda e, src: w.at[src, :, ecols(e, cols)], fbuf, cstage,
        (c_ld, c_send, c_recv), head, experts,
    )

    def keep(e, slot):
        w[me, :, ecols(e, cols)] = cstage[slot, me]

    load_down(0).start()
    for e in range(head):
        load_head(e).start()
    for copy in loads:
        copy.start()
    columns.load(head)
    columns.load(head + 1)
    load_down(1).start()
    meet(n_rep, n_shard)
    columns.prepare(head, keep)
    dg[...] = jnp.zeros_like(dg)
    for copy in loads:
        copy.wait()

    for e in range(head):
        load_head(e).wait()
    line = Line(
        part, into1, into2, total, (pbuf, ibuf, sbuf, tbuf), (z1, y1, z2, y2, z3, y3, zl, zs)
    )

    def place(ref, e, owner):
        start = pl.multiple_of(lax.rem(owner, half) * rows, rows)
        return ref.at[gate_up_at(e, experts) + owner // half, pl.ds(start, rows), :]

    def send_block(e, b):
        return remote(
            gstage.at[lax.rem(e, 2), b], place(part, e, me), a_send.at[lax.rem(e, 2), b],
            a_recv.at[e, b], peer(b),
        )

    def own_block(e):
        return pltpu.make_async_copy(
            gstage.at[lax.rem(e, 2), 0], place(part, e, me), l_sem.at[lax.rem(e, 2)]
        )

    def down_unit(e):
        return pltpu.make_async_copy(
            dstage.at[lax.rem(e, 2)], part.at[down_at(e)], d_sem.at[lax.rem(e, 2)]
        )

    def gh_copy(e):
        return pltpu.make_async_copy(gh.at[lax.rem(e, 2)], gh_out.at[e], h_sem.at[lax.rem(e, 2)])

    tile = 2 * seq

    def expert(e, carry):
        load_down(e).wait()
        slot = lax.rem(e, 2)
        wd[e] = wdf[slot].astype(BF)

        @pl.when(e + 2 < experts)
        def _():
            load_down(e + 2).start()

        @pl.when(e >= 2)
        def _():
            gh_copy(e - 2).wait()

        @pl.when(e >= head)
        def _():
            columns.arrived(e)

        def tokens_tile(i, c):
            r = pl.ds(pl.multiple_of(i * tile, tile), tile)
            pre = jnp.dot(
                x2[r, :],
                w[:, :, ecols(e, cols)].reshape(width, cols),
                preferred_element_type=F32,
            )
            g_pre, u_pre = (pre[:, :f_loc], pre[:, f_loc:])
            z = dot(dy[r, :], wd[e], ((1,), (1,)))
            lane = lax.broadcasted_iota(jnp.int32, (tile, gate.shape[1]), 1)
            own = lane == e
            gt = jnp.sum(jnp.where(own, gate[r, :], 0.0), axis=1, keepdims=True)
            sig = jax.nn.sigmoid(g_pre)
            act = g_pre * sig
            hh = act * u_pre
            dsum = jnp.sum(hh.astype(BF).astype(F32) * z, axis=1, keepdims=True)
            dg[r, :] = dg[r, :] + jnp.where(own, dsum, 0.0)
            gh[slot, r, :] = (gt * hh).astype(BF)
            dh = gt * z
            d_gate = (dh * u_pre * sig * (1.0 + g_pre * (1.0 - sig))).astype(BF)
            d_up = (dh * act).astype(BF)
            dgu[e, i] = jnp.concatenate([d_gate, d_up], axis=1).reshape(2, seq, cols)
            return c

        lax.fori_loop(0, tokens // tile, tokens_tile, 0)

        if head_units:
            @pl.when(e >= 2)
            def _():
                line.step(2 * e - 3, head_units + ahead)

        @pl.when((e >= 1) & (e + 1 < experts))
        def _():
            columns.prepare(e + 1, keep)

        gh_copy(e).start()
        ght = gh[slot].T

        def down_block(j, c):
            r = pl.ds(pl.multiple_of(j * f_loc, f_loc), f_loc)
            dstage[slot, r, :] = jnp.dot(
                ght, dy[:, ecols(j, cols)], preferred_element_type=F32
            ).astype(BF)
            return c

        lax.fori_loop(0, width // cols, down_block, 0)
        down_unit(e).start()
        down_unit(e).wait()

        if head_units:
            @pl.when(e < 2)
            def _():
                line.launch(e)

        @pl.when(e == 0)
        def _():
            def turn(i, c):
                for j in range(n_shard):
                    x2t[j * rows : (j + 1) * rows, ecols(i, seq)] = x2[
                        ecols(i, seq), j * rows : (j + 1) * rows
                    ].T
                return c

            lax.fori_loop(0, n_shard, turn, 0)

        @pl.when(e >= 2)
        def _():
            for b in range(1, n_shard):
                send_block(e - 2, b).wait_send()

        def grad_block(b, c):
            owner = me ^ b
            r = pl.ds(pl.multiple_of(owner * rows, rows), rows)
            value = jnp.dot(
                x2t[r, :], dgu[e].reshape(tokens, cols), preferred_element_type=F32
            ).astype(BF)
            gstage[slot, b] = value

            @pl.when(b > 0)
            def _():
                send_block(e, b).start()

            return c

        lax.fori_loop(0, n_shard, grad_block, 0)
        own_block(e).start()

        def ready(x):
            for b in range(1, n_shard):
                send_block(x, b).wait_recv()
            own_block(x).wait()

        @pl.when(e >= 1)
        def _():
            ready(e - 1)

        @pl.when(e == experts - 1)
        def _():
            ready(e)

        if head_units:
            @pl.when(e >= 1)
            def _():
                line.step(2 * e - 2, head_units + ahead)

        return carry

    lax.fori_loop(0, experts, expert, 0)
    for e in (experts - 2, experts - 1):
        columns.sent(e)
        for b in range(1, n_shard):
            send_block(e, b).wait_send()

    wd_copy = pltpu.make_async_copy(wd, wd_out, ld_sem.at[0])
    wd_copy.start()

    def gate_copy(b):
        return remote(
            dg.at[pl.ds(b * seq, seq), :], dgin.at[b - 1], g_send.at[b], g_recv.at[b], peer(b)
        )

    for b in range(1, n_shard):
        gate_copy(b).start()

    def dx2_block(parity, j):
        total_block = None
        for e in range(experts):
            lhs = dgu[e, :, parity].reshape(half * seq, cols)
            term = dot(lhs, w[j, :, e * cols : (e + 1) * cols], ((1,), (1,)))
            total_block = term if total_block is None else total_block + term
        return total_block

    for copy in late:
        copy.start()
    send, finish = scatter_blocks(
        dx2_block, width, rows, stage, in1, in2, acc, None, (rs_j, rr_j, rs_b, rr_b, None)
    )
    send()
    if head_units:
        line.steps(2 * experts - 3, head_units - 1, head_units + ahead)
    for b in range(1, n_shard):
        gate_copy(b).wait()
        dg[pl.ds(0, seq), :] = dg[pl.ds(0, seq), :] + dgin[b - 1]
    finish()
    for copy in late:
        copy.wait()

    probs = pr[...]
    dpr = dg[pl.ds(0, seq), :] * hit[...]
    dz = probs * (dpr - jnp.sum(probs * dpr, axis=-1, keepdims=True))
    low = dz.astype(BF)
    taps = pltpu.roll(low.astype(F32), 2, 1)[:, :16].astype(BF)
    pay[...] = jnp.zeros_like(pay)
    pay[2 : experts + 2, :] = dot(low.T, x2[pl.ds(0, seq), :], ((1,), (0,)))[:experts]
    gain = small[1:2, :].astype(BF).astype(F32)
    inverse = lax.rsqrt(jnp.mean(h1[...] * h1[...], axis=-1, keepdims=True) + epsilon)
    n2 = h1[...] * inverse
    dx2 = acc[...] + dot(taps, small[...].astype(BF), ((1,), (0,)))
    pay[1:2, :] = jnp.sum(dx2 * n2, axis=0, keepdims=True)
    e2 = dx2 * gain
    dh1 = dy[pl.ds(0, seq), :].astype(F32) + inverse * (
        e2 - n2 * jnp.mean(e2 * n2, axis=-1, keepdims=True)
    )
    acc[...] = dh1
    da[...] = dh1.astype(BF)
    outs = ((acc, dh1_out), (da, da_out), (pay, pay_out))
    outs = [pltpu.make_async_copy(x, y, ld_sem.at[3 + i]) for i, (x, y) in enumerate(outs)]
    for copy in outs:
        copy.start()
    for copy in outs:
        copy.wait()
    wd_copy.wait()
    for e in (experts - 2, experts - 1):
        gh_copy(e).wait()
    if head_units:
        line.step(head_units - 1, head_units + ahead)
        line.finish(head_units, ahead, CROSSED)


def experts_call(
    x2, dy, gate, w, wd, w_gate, w_up, h1, pr, hit, small, n_rep, n_shard
):
    tokens, width = x2.shape
    experts, f_loc = wd.shape[:2]
    seq, rows, cols, half = tokens // n_shard, width // n_shard, 2 * f_loc, n_shard // 2
    head_units = HEAD_UNITS if n_rep == 4 else 0
    units = 3 * experts + 8
    ahead = SENT_AHEAD if head_units else 0
    slots = max(head_units, 1) + ahead
    unit = (width // 2, cols)
    dma = pltpu.SemaphoreType.DMA
    anyspec = pl.BlockSpec(memory_space=pl.ANY)
    shape = jax.ShapeDtypeStruct
    return pl.pallas_call(
        partial(expert_kernel, n_rep, n_shard, experts, f_loc, head_units, ahead),
        out_shape=(
            shape((units,) + unit, BF),
            shape((units if head_units else 1,) + unit, BF),
            shape((units if head_units else 1,) + unit, BF),
            shape((units if head_units else 1,) + unit, BF),
            shape((experts, tokens, f_loc), BF),
            shape((seq, width), BF),
            shape((seq, width), F32),
            shape((16, width), F32),
            shape(wd.shape, BF),
        ),
        in_specs=[anyspec] * 11,
        out_specs=(anyspec,) * 9,
        scratch_shapes=[
            pltpu.VMEM((tokens, width), BF),
            pltpu.VMEM((width, tokens), BF),
            pltpu.VMEM((tokens, width), BF),
            pltpu.VMEM(gate.shape, F32),
            pltpu.VMEM((n_shard, rows, experts * cols), BF),
            pltpu.VMEM(wd.shape, BF),
            pltpu.VMEM((2, tokens, f_loc), BF),
            pltpu.VMEM((experts, half, 2, seq, cols), BF),
            pltpu.VMEM(gate.shape, F32),
            pltpu.VMEM((2,) + unit, BF),
            pltpu.VMEM((2, n_shard, rows, cols), BF),
            pltpu.VMEM((half, seq, width), BF),
            pltpu.VMEM((half, seq, width), BF),
            pltpu.VMEM((half - 1, seq, width), BF),
            pltpu.VMEM((seq, width), F32),
            pltpu.VMEM((n_shard - 1, seq, gate.shape[1]), F32),
            pltpu.VMEM((2, 2) + w_gate.shape[1:], F32),
            pltpu.VMEM((2, n_shard, rows, cols), BF),
            pltpu.VMEM((2,) + wd.shape[1:], F32),
            pltpu.VMEM(h1.shape, F32),
            pltpu.VMEM(pr.shape, F32),
            pltpu.VMEM(hit.shape, F32),
            pltpu.VMEM(small.shape, F32),
            pltpu.VMEM((seq, width), BF),
            pltpu.VMEM((16, width), F32),
            pltpu.VMEM(unit if head_units else (8, cols), BF),
            pltpu.VMEM(unit if head_units else (8, cols), BF),
            pltpu.VMEM((4 if head_units else 1,) + unit, BF),
            pltpu.VMEM((2 if head_units else 1,) + unit, BF),
            dma((7,)),
            dma((2, experts)),
            dma((2,)),
            dma((2, 2)),
            dma((2, n_shard)),
            dma((experts, n_shard)),
            dma((2,)),
            dma((2,)),
            dma((2, n_shard)),
            dma((experts, n_shard)),
            dma((n_shard,)),
            dma((n_shard,)),
            dma((n_shard,)),
            dma((n_shard,)),
            dma((half,)),
            dma((half,)),
            dma,
        ]
        + line_scratch(slots),
        compiler_params=pltpu.CompilerParams(
            collective_id=1, has_side_effects=True, vmem_limit_bytes=67000000
        ),
        name="experts",
    )(x2, dy, gate, w, wd, w_gate, w_up, h1, pr, hit, small)


def attention_kernel(
    n_rep, n_shard, experts, f_loc, head_units, ahead,
    da_hbm, x1_hbm, a_hbm, wqkv_hbm, wo_hbm, qkvr_hbm, q_hbm, k_hbm, seg_hbm, table_hbm, gain_hbm,
    gh_hbm, wd_hbm, tok_hbm, pay_hbm, h1_hbm, dh1_hbm, small_hbm, part_in, into1_in, into2_in, total_in,
    part, into1, into2, total, gtok_out, out_out, pay_out,
    da, x1, a, wqkv, wo, qkvr, q, k, seg, table, gain, gh, wd, tok, pay, h1, dh1, small,
    do, dqkv, ggain, payin, payrep, dstage, gstage, stage, in1, in2, acc,
    pbuf, ibuf, sbuf, tbuf,
    ld_sem, f_send, f_recv, d_sem, l_sem, a_send, a_recv,
    rs_j, rr_j, rs_b, rr_b, ts_j, tr_j, ts_b, tr_b, p_send, p_recv, q_send, q_recv, o_sem,
    z1, y1, z2, y2, z3, y3, zl, zs,
):
    me = lax.axis_index("shard")
    half, seq, width = stage.shape
    tokens = n_shard * seq
    rows = width // n_shard
    cols = rows
    heads = cols // HEAD_DIM
    scale = HEAD_DIM ** (-0.5)
    first_unit = 3 * experts
    pairs = (
        (x1_hbm, x1), (a_hbm, a), (wo_hbm, wo), (qkvr_hbm, qkvr), (q_hbm, q), (k_hbm, k),
        (seg_hbm, seg), (table_hbm, table), (gain_hbm, gain), (wqkv_hbm, wqkv), (gh_hbm, gh),
        (wd_hbm, wd), (tok_hbm, tok), (pay_hbm, pay),
        (h1_hbm, h1), (dh1_hbm, dh1), (small_hbm, small),
    )
    loads = [pltpu.make_async_copy(x, y, ld_sem.at[i]) for i, (x, y) in enumerate(pairs)]
    mine = pltpu.make_async_copy(da_hbm, da.at[0], ld_sem.at[len(pairs)])
    mine.start()
    for copy in loads:
        copy.start()
    meet(n_rep, n_shard)
    line = Line(
        part, into1, into2, total, (pbuf, ibuf, sbuf, tbuf), (z1, y1, z2, y2, z3, y3, zl, zs),
        head_units, ahead, CROSSED, WINDOW, LAG,
    )
    last_unit = first_unit + 8

    place_of = [head_units + sum(PUMPS[:i]) for i in range(len(PUMPS) + 1)]

    def pump(i):
        if head_units and PUMPS[i]:
            line.steps(place_of[i], place_of[i + 1], last_unit)

    if head_units:
        for u in range(WINDOW):
            line.launch(head_units + ahead + u)

    def block_cols(j, size):
        return pl.ds(pl.multiple_of(j * size, size), size)

    def cross_over():
        if head_units:
            for u in range(head_units, head_units + CROSSED):
                line.add_second(u)

    spread = spread_sends(da_hbm, da, f_send, f_recv, n_shard)
    for i in list(range(2, n_shard, 2)) + [1]:
        spread(i).start()
    cross_over()
    pump(0)
    for copy in loads[10:12]:
        copy.wait()

    def out_part(parity, j):
        total_block = None
        for e in range(experts):
            lhs = gh[e, :, parity].reshape(half * seq, f_loc)
            term = dot(lhs, wd[e, :, block_cols(j, cols)], ((1,), (0,)))
            total_block = term if total_block is None else total_block + term
        return total_block

    send_out, finish_out = scatter_blocks(
        out_part, width, rows, stage, in1.at[1], in2.at[1], acc.at[1], None,
        (ts_j, tr_j, ts_b, tr_b, None),
    )
    send_out()
    pump(1)
    for i in range(2, n_shard, 2):
        spread(i).wait_recv()
        spread(i + 1).start()
    for i in range(1, n_shard, 2):
        spread(i).wait_recv()
    for i in range(1, n_shard):
        spread(i).wait_send()
    mine.wait()
    for copy in loads[:9]:
        copy.wait()
    pump(2)

    at = a[...].T

    def out_block(j, c):
        r = block_cols(lax.rem(j, half), cols)
        value = jnp.dot(
            at, da[:, :, block_cols(j, cols)].reshape(tokens, cols), preferred_element_type=F32
        )
        dstage[j // half, r, :] = value.astype(BF)
        return c

    lax.fori_loop(0, n_shard, out_block, 0)
    outs = [
        pltpu.make_async_copy(dstage.at[i], part.at[first_unit + i], d_sem.at[i]) for i in range(2)
    ]
    for copy in outs:
        copy.start()

    def do_block(i, c):
        r = block_cols(i, 2 * seq)
        lhs = da[pl.ds(2 * i, 2)].reshape(2 * seq, width)
        do[r, :] = dot(lhs, wo[...], ((1,), (1,))).astype(BF)
        return c

    lax.fori_loop(0, half, do_block, 0)
    for copy in outs:
        copy.wait()
    pump(3)
    finish_out()

    cosine, sine = (table[0], table[1])

    def head_grad(grad, x, gain_row):
        inverse = lax.rsqrt(jnp.mean(x * x, axis=-1, keepdims=True) + epsilon)
        x_hat = x * inverse
        back = grad * cosine - pltpu.roll(grad, HEAD_DIM // 2, 1) * sine
        scaled = back * gain_row
        value = inverse * (scaled - x_hat * jnp.mean(scaled * x_hat, axis=-1, keepdims=True))
        return (value.astype(BF), jnp.sum(back * x_hat, axis=0, keepdims=True))

    ggain[...] = jnp.zeros_like(ggain)

    def sequence(b, carry):
        r = block_cols(b, seq)
        row = jnp.broadcast_to(seg[b].astype(F32), (seq, seq))
        same = row == row.T
        for i in range(heads):
            c = slice(i * HEAD_DIM, (i + 1) * HEAD_DIM)
            qr, kr, v = (qkvr[n, r, c] for n in range(3))
            d = do[r, c]
            s = jnp.where(same, dot(qr, kr, ((1,), (1,))) * scale, -1000000000.0)
            e = jnp.exp(s - jnp.max(s, axis=-1, keepdims=True))
            p = e / jnp.sum(e, axis=-1, keepdims=True)
            dv = dot(p.astype(BF).T, d, ((1,), (0,)))
            dp = dot(d, v, ((1,), (1,)))
            ds = (p * (dp - jnp.sum(p * dp, axis=-1, keepdims=True))).astype(BF)
            dqr = dot(ds, kr, ((1,), (0,))) * scale
            dkr = dot(ds.T, qr, ((1,), (0,))) * scale
            dq, gq = head_grad(dqr, q[r, c], gain[0:1, :])
            dk, gk = head_grad(dkr, k[r, c], gain[1:2, :])
            dqkv[0, r, c] = dq
            dqkv[1, r, c] = dk
            dqkv[2, r, c] = dv.astype(BF)
            ggain[0:1, :] = ggain[0:1, :] + gq
            ggain[1:2, :] = ggain[1:2, :] + gk
        return carry

    lax.fori_loop(0, half, sequence, 0)
    pump(4)
    lax.fori_loop(half, n_shard, sequence, 0)
    pump(5)
    for copy in (loads[9], *loads[12:]):
        copy.wait()

    def place(n, owner):
        start = pl.multiple_of(lax.rem(owner, half) * rows, rows)
        unit = first_unit + 2 + 2 * (2 - n) + owner // half
        return part.at[unit, pl.ds(start, rows), :]

    def send_block(n, b):
        return remote(gstage.at[n, b], place(n, me), a_send.at[n, b], a_recv.at[n, b], peer(b))

    def own_block(n):
        return pltpu.make_async_copy(gstage.at[n, 0], place(n, me), l_sem.at[n])

    def weight_grad(i, carry):
        n = 2 - i
        grad_t = dqkv[n].T

        def block(b, c):
            owner = me ^ b
            value = jnp.dot(
                grad_t,
                x1[:, :, block_cols(owner, rows)].reshape(tokens, rows),
                preferred_element_type=F32,
            )
            gstage[n, b] = value.T.astype(BF)

            @pl.when(b > 0)
            def _():
                send_block(n, b).start()

            return c

        lax.fori_loop(0, n_shard, block, 0)
        own_block(n).start()
        return carry

    lax.fori_loop(0, 3, weight_grad, 0)
    pump(6)

    def grad_ready(n):
        for b in range(1, n_shard):
            send_block(n, b).wait()
        own_block(n).wait()

    def dx1_block(parity, j):
        total_block = None
        for n in range(3):
            lhs = dqkv[n].reshape(half, 2, seq, cols)[:, parity].reshape(half * seq, cols)
            term = dot(lhs, wqkv[block_cols(j, rows), n * cols : (n + 1) * cols], ((1,), (1,)))
            total_block = term if total_block is None else total_block + term
        return total_block

    send_dx1, finish_dx1 = scatter_blocks(
        dx1_block, width, rows, stage, in1.at[0], in2.at[0], acc.at[0], None,
        (rs_j, rr_j, rs_b, rr_b, None),
    )
    pump(7)
    for n in (2, 1, 0):
        grad_ready(n)
    send_dx1()
    pump(8)
    pump(9)
    finish_dx1()
    pump(10)

    rank = lax.axis_index("rep")
    h = tok[...].astype(F32)
    r1 = lax.rsqrt(jnp.mean(h * h, axis=-1, keepdims=True) + epsilon)
    n1 = h * r1
    dx1 = acc[0]
    pay[0:1, :] = jnp.sum(dx1 * n1, axis=0, keepdims=True)
    e1 = dx1 * small[0:1, :].astype(BF).astype(F32)
    dh1[...] = dh1[...] + r1 * (e1 - n1 * jnp.mean(e1 * n1, axis=-1, keepdims=True))
    tok[...] = (h1[...] + acc[1]).astype(BF)
    done = ((dh1, gtok_out), (tok, out_out))
    done = [pltpu.make_async_copy(x, y, o_sem.at[i]) for i, (x, y) in enumerate(done)]
    for copy in done:
        copy.start()
    for i in range(width // HEAD_DIM):
        pay[experts + 2 : experts + 4, i * HEAD_DIM : (i + 1) * HEAD_DIM] = ggain[0:2, :]

    def owner_copy(b):
        return remote(
            pay.at[:, block_cols(me ^ b, cols)], payin.at[b], p_send.at[b], p_recv.at[b], peer(b)
        )

    for b in range(1, n_shard):
        owner_copy(b).start()
    payin[0] = pay[:, block_cols(me, cols)]
    pump(11)
    for b in range(1, n_shard):
        owner_copy(b).wait()
        payin[0] = payin[0] + payin[b]

    def rep_copy(b):
        return remote(
            payin.at[0], payrep.at[rank], q_send.at[b], q_recv.at[b], along(rank ^ b)
        )

    for b in range(1, n_rep):
        rep_copy(b).start()
    payrep[rank] = payin[0]
    pump(12)
    for b in range(1, n_rep):
        rep_copy(b).wait()
    summed = payrep[0]
    for i in range(1, n_rep):
        summed = summed + payrep[i]
    payin[1] = summed
    copy = pltpu.make_async_copy(payin.at[1], pay_out, o_sem.at[2])
    copy.start()
    copy.wait()
    for copy in done:
        copy.wait()
    if head_units:
        line.steps(place_of[-1], last_unit, last_unit)
        line.finish(last_unit)


def attention_call(
    da, x1, a, wqkv, wo, qkvr, q, k, seg, table, gain, gh, wd, tok, pay, h1, dh1, small, part, into1,
    into2, total, n_rep, n_shard, head_units,
):
    seq, width = da.shape
    tokens, cols = a.shape
    experts, f_loc = wd.shape[:2]
    half = n_shard // 2
    units = part.shape[0]
    slots = units - head_units if head_units else 1
    unit = part.shape[1:]
    gh = gh.reshape(experts, half, 2, seq, f_loc)
    dma = pltpu.SemaphoreType.DMA
    anyspec = pl.BlockSpec(memory_space=pl.ANY)
    shape = jax.ShapeDtypeStruct
    whole = (x1, a, wqkv, wo, qkvr, q, k, seg, table, gain, gh, wd, tok, pay, h1, dh1, small)
    return pl.pallas_call(
        partial(
            attention_kernel, n_rep, n_shard, experts, f_loc, head_units,
            SENT_AHEAD if head_units else 0,
        ),
        out_shape=(
            shape(part.shape, BF),
            shape(into1.shape, BF),
            shape(into2.shape, BF),
            shape(total.shape, BF),
            shape((seq, width), F32),
            shape((seq, width), BF),
            shape((pay.shape[0], width // n_shard), F32),
        ),
        in_specs=[anyspec] * 22,
        out_specs=(anyspec,) * 7,
        input_output_aliases={18: 0, 19: 1, 20: 2, 21: 3},
        scratch_shapes=[pltpu.VMEM((n_shard, seq, width), BF)]
        + [pltpu.VMEM(x.shape, x.dtype) for x in whole]
        + [
            pltpu.VMEM((tokens, cols), BF),
            pltpu.VMEM((3, tokens, cols), BF),
            pltpu.VMEM((8, HEAD_DIM), F32),
            pltpu.VMEM((n_shard, pay.shape[0], cols), F32),
            pltpu.VMEM((n_rep, pay.shape[0], cols), F32),
            pltpu.VMEM((2,) + unit, BF),
            pltpu.VMEM((3, n_shard, cols, cols), BF),
            pltpu.VMEM((half, seq, width), BF),
            pltpu.VMEM((2, half, seq, width), BF),
            pltpu.VMEM((2, half - 1, seq, width), BF),
            pltpu.VMEM((2, seq, width), F32),
            pltpu.VMEM(unit, BF),
            pltpu.VMEM(unit, BF),
            pltpu.VMEM((4 if head_units else 1,) + unit, BF),
            pltpu.VMEM((2 if head_units else 1,) + unit, BF),
            dma((18,)),
            dma((n_shard,)),
            dma((n_shard,)),
            dma((2,)),
            dma((3,)),
            dma((3, n_shard)),
            dma((3, n_shard)),
            dma((n_shard,)),
            dma((n_shard,)),
            dma((half,)),
            dma((half,)),
            dma((n_shard,)),
            dma((n_shard,)),
            dma((half,)),
            dma((half,)),
            dma((n_shard,)),
            dma((n_shard,)),
            dma((n_rep,)),
            dma((n_rep,)),
            dma((3,)),
        ]
        + line_scratch(slots),
        compiler_params=pltpu.CompilerParams(
            collective_id=2, has_side_effects=True, vmem_limit_bytes=67000000
        ),
        name="attention",
    )(da, *whole, part, into1, into2, total)


def forward_kernel(
    n_rep, n_shard, experts, head,
    tok_hbm, small_hbm, seg_hbm, route_hbm, dy_hbm, wq_hbm, wk_hbm, wv_hbm, wo_hbm, table_hbm,
    wg_hbm, wu_hbm,
    x1_out, x2_out, dy_out, gate_out, w_out, wqkv_out, wo_out, qkvr_out, q_out, k_out, a_out,
    seg_out, h1_out, pr_out, small_out, hit_out, gain_out,
    tok, small, seg, hit, gain, route, wf, wof, table, x1, wqkv, wst, wo, qkvr, q, k, a, x2, gate, pr,
    stage, in1, in2, acc, fbuf, cstage,
    ld_sem, t_send, t_recv, s_send, s_recv, e_send, e_recv, w_send, w_recv, d_send, d_recv,
    x_send, x_recv, g_send, g_recv, c_ld, c_send, c_recv, o_sem, rs_j, rr_j, rs_b, rr_b,
):
    me = lax.axis_index("shard")
    half, seq, width = stage.shape
    rows = width // n_shard
    cols = rows
    tokens = n_shard * seq
    heads = cols // HEAD_DIM
    scale = HEAD_DIM ** (-0.5)
    cut = w_out.shape[2] // head

    def block_cols(j, size):
        return pl.ds(pl.multiple_of(j * size, size), size)

    pairs = (
        (tok_hbm, tok.at[0]), (small_hbm, small.at[:, block_cols(me, rows)]),
        (wq_hbm, wf.at[0]), (wk_hbm, wf.at[1]), (wv_hbm, wf.at[2]), (wo_hbm, wof),
        (seg_hbm, seg.at[0]), (route_hbm, route), (table_hbm, table),
    )
    loads = [pltpu.make_async_copy(x, y, ld_sem.at[i]) for i, (x, y) in enumerate(pairs)]
    for copy in loads:
        copy.start()
    columns = Columns(
        wg_hbm, wu_hbm, lambda e, src: w_out.at[src, :, block_cols(e, cut)], fbuf, cstage,
        (c_ld, c_send, c_recv), 0, head,
    )
    for e in range(min(head, 2)):
        columns.load(e)
    dy_own = pltpu.make_async_copy(dy_hbm, dy_out.at[0], ld_sem.at[len(pairs)])
    dy_own.start()
    meet(n_rep, n_shard)

    def small_copy(b):
        return remote(
            small_hbm, small.at[:, block_cols(me, rows)], s_send.at[b], s_recv.at[b], peer(b)
        )

    def seg_copy(b):
        return remote(seg_hbm, seg.at[b], e_send.at[b], e_recv.at[b], peer(b))

    for b in range(1, n_shard):
        small_copy(b).start()
        seg_copy(b).start()
    spread = spread_sends(tok_hbm, tok, t_send, t_recv, n_shard)
    for i in list(range(2, n_shard, 2)) + [1]:
        spread(i).start()

    def w_copy(owner):
        away = owner ^ me
        return remote(
            wst.at[owner], wqkv.at[block_cols(me, rows), :], w_send.at[away], w_recv.at[away],
            peer(away),
        )

    for copy in loads[2:5]:
        copy.wait()

    def cast_block(owner, c):
        wst[owner] = jnp.concatenate(
            [wf[i, :, block_cols(owner, cols)] for i in range(3)], axis=1
        ).astype(BF)

        @pl.when(owner != me)
        def _():
            w_copy(owner).start()

        return c

    lax.fori_loop(0, n_shard, cast_block, 0)
    wqkv[block_cols(me, rows), :] = wst[me]
    for copy in (loads[0], loads[1], *loads[5:]):
        copy.wait()
    wo[...] = wof[...].astype(BF)
    for b in range(1, n_shard):
        small_copy(b).wait()
        seg_copy(b).wait()
    gain_attn = small[0:1, :].astype(BF).astype(F32)
    lane = lax.broadcasted_iota(jnp.int32, hit.shape, 1)
    named = jnp.zeros(hit.shape, F32)
    for j in range(route.shape[1]):
        named = named + (lane == route[:, j : j + 1]).astype(F32)
    hit[...] = named

    def norm_first(i):
        h = tok[i].astype(F32)
        n1 = h * lax.rsqrt(jnp.mean(h * h, axis=-1, keepdims=True) + epsilon)
        x1[i] = (n1 * gain_attn).astype(BF)

    norm_first(0)
    spread(1).wait_recv()
    norm_first(1)
    for i in range(2, n_shard, 2):
        spread(i).wait_recv()
        spread(i + 1).start()
        norm_first(i)
    for i in range(3, n_shard, 2):
        spread(i).wait_recv()
        norm_first(i)
    for b in range(1, n_shard):
        w_copy(me ^ b).wait_recv()

    spread_dy = spread_sends(dy_hbm, dy_out, d_send, d_recv, n_shard)
    for i in list(range(2, n_shard, 2)) + [1]:
        spread_dy(i).start()

    keeps = []

    def keep(e, slot):
        copy = pltpu.make_async_copy(
            cstage.at[slot, me], w_out.at[me, :, block_cols(e, cut)], o_sem.at[14 + e]
        )
        copy.start()
        keeps.append(copy)

    for e in range(head):
        columns.prepare(e, keep)

    def spread_gain(row):
        hd = HEAD_DIM // n_shard
        total = small[row : row + 1, :HEAD_DIM]
        for j in range(1, n_shard):
            part = small[row : row + 1, j * rows : j * rows + HEAD_DIM]
            total = total + pltpu.roll(part, j * hd, 1)
        return total.astype(BF).astype(F32)

    gain_q = spread_gain(experts + 2)
    gain_k = spread_gain(experts + 3)
    gain[...] = jnp.concatenate([gain_q, gain_k, jnp.zeros((6, HEAD_DIM), F32)], axis=0)
    cosine, sine = (table[0], table[1])

    def turned(x, gain):
        hat = x * lax.rsqrt(jnp.mean(x * x, axis=-1, keepdims=True) + epsilon) * gain
        return (hat * cosine + pltpu.roll(hat, HEAD_DIM // 2, 1) * sine).astype(BF)

    def two_sequences(i, carry):
        y = jnp.dot(
            x1[pl.ds(2 * i, 2)].reshape(2 * seq, width), wqkv[...], preferred_element_type=F32
        )
        r2 = block_cols(i, 2 * seq)
        q[r2, :] = y[:, :cols]
        k[r2, :] = y[:, cols : 2 * cols]
        qkvr[2, r2, :] = y[:, 2 * cols :].astype(BF)
        for j in range(2):
            r = block_cols(2 * i + j, seq)
            row = jnp.broadcast_to(seg[2 * i + j].astype(F32), (seq, seq))
            same = row == row.T
            for n in range(heads):
                c = slice(n * HEAD_DIM, (n + 1) * HEAD_DIM)
                qr = turned(q[r, c], gain_q)
                kr = turned(k[r, c], gain_k)
                qkvr[0, r, c] = qr
                qkvr[1, r, c] = kr
                s = jnp.where(same, dot(qr, kr, ((1,), (1,))) * scale, -1000000000.0)
                e = jnp.exp(s - jnp.max(s, axis=-1, keepdims=True))
                p = e / jnp.sum(e, axis=-1, keepdims=True)
                a[r, c] = dot(p.astype(BF), qkvr[2, r, c], ((1,), (0,))).astype(BF)
        return carry

    lax.fori_loop(0, half, two_sequences, 0)
    stores = [
        (q, q_out), (k, k_out), (qkvr, qkvr_out), (a, a_out), (x1, x1_out), (wqkv, wqkv_out),
        (wo, wo_out), (seg, seg_out), (small, small_out), (hit, hit_out),
        (gain, gain_out),
    ]
    stores = [pltpu.make_async_copy(x, y, o_sem.at[i]) for i, (x, y) in enumerate(stores)]

    def out_block(parity, j):
        lhs = a[...].reshape(half, 2, seq, cols)[:, parity].reshape(half * seq, cols)
        return dot(lhs, wo[:, block_cols(j, rows)], ((1,), (0,)))

    send, finish = scatter_blocks(
        out_block, width, rows, stage, in1, in2, acc, None, (rs_j, rr_j, rs_b, rr_b, None)
    )
    send()
    for i in range(2, n_shard, 2):
        spread_dy(i).wait_recv()
        spread_dy(i + 1).start()
    finish()
    h1 = tok[0].astype(F32) + acc[...]
    acc[...] = h1
    n2 = h1 * lax.rsqrt(jnp.mean(h1 * h1, axis=-1, keepdims=True) + epsilon)
    x2[...] = (n2 * small[1:2, :].astype(BF).astype(F32)).astype(BF)
    spread_x2 = spread_sends(x2, x2_out, x_send, x_recv, n_shard)
    for i in list(range(2, n_shard, 2)) + [1]:
        spread_x2(i).start()
    own = pltpu.make_async_copy(x2, x2_out.at[0], o_sem.at[11])
    own.start()
    lane = lax.broadcasted_iota(jnp.int32, (seq, 16), 1)
    z = dot(x2[...], small[...].astype(BF), ((1,), (1,)))
    valid = (lane >= 2) & (lane < experts + 2)
    z = jnp.where(valid, z, -1e30)
    e = jnp.exp(z - jnp.max(z, axis=-1, keepdims=True))
    probs = e / jnp.sum(e, axis=-1, keepdims=True)
    probs = jnp.concatenate([probs, jnp.zeros((seq, gate.shape[1] - 16), F32)], axis=1)
    probs = pltpu.roll(probs, gate.shape[1] - 2, 1)
    pr[...] = probs
    gate[...] = probs * hit[...]

    def gate_copy(b):
        return remote(gate, gate_out.at[b], g_send.at[b], g_recv.at[b], peer(b))

    for b in range(1, n_shard):
        gate_copy(b).start()
    more = [(gate, gate_out.at[0]), (pr, pr_out)]
    more = [pltpu.make_async_copy(x, y, o_sem.at[12 + i]) for i, (x, y) in enumerate(more)]
    last = pltpu.make_async_copy(acc, h1_out, ld_sem.at[0])
    for copy in (*stores, *more, last):
        copy.start()
    for i in range(2, n_shard, 2):
        spread_x2(i).wait_recv()
        spread_x2(i + 1).start()
    for i in range(1, n_shard, 2):
        spread_x2(i).wait_recv()
        spread_dy(i).wait_recv()
    for b in range(1, n_shard):
        gate_copy(b).wait()
        spread(b).wait_send()
        spread_dy(b).wait_send()
        spread_x2(b).wait_send()
        w_copy(me ^ b).wait_send()
    for e in range(head):
        columns.arrived(e)
        columns.sent(e)
    dy_own.wait()
    for copy in (own, *stores, *more, last, *keeps):
        copy.wait()


def forward_call(
    tok, small, seg, route, dy, wq, wk, wv, wo, table, w_gate, w_up, n_rep, n_shard, head
):
    seq, width = tok.shape
    experts = w_gate.shape[0]
    rows, half, tokens = width // n_shard, n_shard // 2, n_shard * seq
    cols = rows
    dma = pltpu.SemaphoreType.DMA
    anyspec = pl.BlockSpec(memory_space=pl.ANY)
    shape = jax.ShapeDtypeStruct
    group = (n_shard, seq, width)
    lanes = (seq, 128)
    return pl.pallas_call(
        partial(forward_kernel, n_rep, n_shard, experts, head),
        out_shape=(
            shape(group, BF),
            shape(group, BF),
            shape(group, BF),
            shape((n_shard,) + lanes, F32),
            shape((n_shard, rows, head * cols), BF),
            shape((width, 3 * cols), BF),
            shape((rows, width), BF),
            shape((3, tokens, cols), BF),
            shape((tokens, cols), F32),
            shape((tokens, cols), F32),
            shape((tokens, cols), BF),
            shape((n_shard,) + seg.shape, seg.dtype),
            shape((seq, width), F32),
            shape(lanes, F32),
            shape((16, width), F32),
            shape(lanes, F32),
            shape((8, HEAD_DIM), F32),
        ),
        in_specs=[anyspec] * 12,
        out_specs=(anyspec,) * 17,
        scratch_shapes=[
            pltpu.VMEM(group, BF),
            pltpu.VMEM((16, width), F32),
            pltpu.VMEM((n_shard,) + seg.shape, seg.dtype),
            pltpu.VMEM(lanes, F32),
            pltpu.VMEM((8, HEAD_DIM), F32),
            pltpu.VMEM(route.shape, route.dtype),
            pltpu.VMEM((3, rows, width), F32),
            pltpu.VMEM((rows, width), F32),
            pltpu.VMEM(table.shape, F32),
            pltpu.VMEM(group, BF),
            pltpu.VMEM((width, 3 * cols), BF),
            pltpu.VMEM((n_shard, rows, 3 * cols), BF),
            pltpu.VMEM((rows, width), BF),
            pltpu.VMEM((3, tokens, cols), BF),
            pltpu.VMEM((tokens, cols), F32),
            pltpu.VMEM((tokens, cols), F32),
            pltpu.VMEM((tokens, cols), BF),
            pltpu.VMEM((seq, width), BF),
            pltpu.VMEM(lanes, F32),
            pltpu.VMEM(lanes, F32),
            pltpu.VMEM((half, seq, width), BF),
            pltpu.VMEM((half, seq, width), BF),
            pltpu.VMEM((half - 1, seq, width), BF),
            pltpu.VMEM((seq, width), F32),
            pltpu.VMEM((2, 2) + w_gate.shape[1:], F32),
            pltpu.VMEM((2, n_shard, rows, cols), BF),
            dma((10,)),
        ]
        + [dma((n_shard,)) for _ in range(14)]
        + [
            dma((2, 2)),
            dma((2, n_shard)),
            dma((head, n_shard)),
            dma((14 + head,)),
            dma((n_shard,)),
            dma((n_shard,)),
            dma((half,)),
            dma((half,)),
        ],
        compiler_params=pltpu.CompilerParams(
            collective_id=3, has_side_effects=True, vmem_limit_bytes=67000000
        ),
        name="forward",
    )(tok, small, seg, route, dy, wq, wk, wv, wo, table, w_gate, w_up)


def unpack_experts(n_shard, d, ga, gb, gate, up, down):
    x = (ga, gb)
    rows, hidden = gate.shape[1:]
    f_loc = hidden // n_shard
    cols = 2 * f_loc
    half = n_shard // 2
    for j in range(n_shard):
        r = slice((j % half) * rows, (j % half + 1) * rows)
        gate[0, :, j * f_loc : (j + 1) * f_loc] = x[j // half][0, r, :f_loc].astype(F32)
        up[0, :, j * f_loc : (j + 1) * f_loc] = x[j // half][0, r, f_loc:].astype(F32)
    for j in range(down.shape[2] // cols):
        down[0, :, j * cols : (j + 1) * cols] = d[0, j * f_loc : (j + 1) * f_loc, :].astype(F32)


def unpack_attention(*refs):
    rows = refs[4].shape[0]
    for x, out in zip(refs[:4], refs[4:]):
        cols = x.shape[2]
        for j in range(2):
            out[:, j * cols : (j + 1) * cols] = x[0, j * rows : (j + 1) * rows, :].astype(F32)


def unpack(total, experts, n_shard):
    depth, cols = total.shape[1:]
    width, f_loc = 2 * depth, cols // 2
    rows = width // n_shard
    hidden = n_shard * f_loc
    shape = jax.ShapeDtypeStruct
    by = lambda e: (e, 0, 0)
    params = pltpu.CompilerParams(vmem_limit_bytes=48 << 20)
    gate, up, down = pl.pallas_call(
        partial(unpack_experts, n_shard),
        grid=(experts,),
        out_shape=(
            shape((experts, rows, hidden), F32),
            shape((experts, rows, hidden), F32),
            shape((experts, f_loc, width), F32),
        ),
        in_specs=[
            pl.BlockSpec((1, depth, cols), lambda e: (down_at(e), 0, 0)),
            pl.BlockSpec((1, depth, cols), lambda e: (gate_up_at(e, experts), 0, 0)),
            pl.BlockSpec((1, depth, cols), lambda e: (gate_up_at(e, experts) + 1, 0, 0)),
        ],
        out_specs=(
            pl.BlockSpec((1, rows, hidden), by),
            pl.BlockSpec((1, rows, hidden), by),
            pl.BlockSpec((1, f_loc, width), by),
        ),
        compiler_params=params,
        name="unpack_experts",
    )(total, total, total)
    return gate, up, down


def unpack_rest(total, first, n_shard):
    depth, cols = total.shape[1:]
    width, half = 2 * depth, n_shard // 2
    rows = width // n_shard

    def unit(i):
        step = half // 2
        return pl.BlockSpec((1, 2 * rows, cols), lambda j: (first + 2 * i + j // step, j % step, 0))

    return pl.pallas_call(
        unpack_attention,
        grid=(half,),
        out_shape=(jax.ShapeDtypeStruct((rows, width), F32),) * 4,
        in_specs=[unit(i) for i in range(4)],
        out_specs=(pl.BlockSpec((rows, 2 * cols), lambda j: (0, j)),) * 4,
        name="unpack_attention",
    )(*([total] * 4))


def shards(
    tokens, segments, routes, slot_ids, attn_gain, w_query, w_key, w_value, w_out,
    query_gain, key_gain, ffn_gain, router, w_gate, w_up, w_down, cotangent,
):
    n_shard = lax.axis_size("shard")
    me = lax.axis_index("shard")
    seq, width = tokens.shape
    experts, rows, hidden_f = w_gate.shape
    f_loc = w_down.shape[1]
    cols = width // n_shard
    group = n_shard * seq
    n_rep = lax.axis_size("rep")
    hd = HEAD_DIM // n_shard

    row = jnp.arange(16)[:, None]

    def wide(g):
        return jnp.pad(g, (0, rows - g.shape[0]))[None]

    small = jnp.pad(router.T, ((2, 14 - experts), (0, 0)))
    for i, g in (
        (0, attn_gain), (1, ffn_gain), (experts + 2, query_gain), (experts + 3, key_gain)
    ):
        small = jnp.where(row == i, wide(g), small)
    cosine, sine = rope_tables(seq, HEAD_DIM)
    cos2, sin2 = (cosine[:, 0], sine[:, 0])
    table = jnp.stack(
        [jnp.concatenate([cos2, cos2], axis=1), jnp.concatenate([-sin2, sin2], axis=1)]
    )
    (
        x1_all, x2_all, dy_all, gate_all, gu, qkv, w_out_b, qkvr, q, k, a, seg_all, h1, pr, small,
        hit, gains,
    ) = forward_call(
        tokens, small, segments.reshape(1, seq), routes, cotangent, w_query, w_key, w_value, w_out, table,
        w_gate, w_up, n_rep, n_shard, HEAD_EXPERTS,
    )
    part, into1, into2, total, gh, da, dh1, pay, w_down_b = experts_call(
        x2_all.reshape(group, width), dy_all.reshape(group, width), gate_all.reshape(group, -1),
        gu, w_down, w_gate, w_up, h1, pr, hit, small, n_rep, n_shard,
    )
    part, _, _, total, grad_tokens, output, sums = attention_call(
        da, x1_all, a, qkv, w_out_b, qkvr, q, k, seg_all, table,
        gains, gh, w_down_b, tokens, pay, h1, dh1,
        small, part, into1, into2, total,
        n_rep, n_shard, HEAD_UNITS if n_rep == 4 else 0,
    )
    summed = total if n_rep == 4 else lax.psum(part, "rep")
    gw_gate, gw_up, gw_down = unpack(summed, experts, n_shard)
    gw_out, gw_value, gw_key, gw_query = unpack_rest(summed, 3 * experts, n_shard)
    small = sums
    gg_query = lax.dynamic_slice(small[experts + 2, :HEAD_DIM], (me * hd,), (hd,))
    gg_key = lax.dynamic_slice(small[experts + 3, :HEAD_DIM], (me * hd,), (hd,))
    return (
        output,
        grad_tokens,
        small[0],
        gw_query,
        gw_key,
        gw_value,
        gw_out,
        gg_query,
        gg_key,
        small[1],
        small[2 : experts + 2].T,
        gw_gate,
        gw_up,
        gw_down,
    )


def solution(mesh):
    both = P(("rep", "shard"), None)
    row = P("shard", None)
    vec = P("shard")
    exp = P(None, "shard", None)
    return jax.shard_map(
        shards,
        mesh=mesh,
        in_specs=(
            both, P(("rep", "shard")), both, both, vec, row, row, row, row,
            vec, vec, vec, row, exp, exp, exp, both,
        ),
        out_specs=(both, both, vec, row, row, row, row, vec, vec, vec, row, exp, exp, exp),
        check_vma=False,
    )
```

```python
from functools import partial

import jax
import jax.numpy as jnp
from jax import lax
from jax.experimental import pallas as pl
from jax.experimental.pallas import tpu as pltpu
from jax.sharding import PartitionSpec as P

HEAD_DIM = 128
HEAD_UNITS = 20
HEAD_EXPERTS = 1
SENT_AHEAD = 3
CROSSED = 2
WINDOW = 2
LAG = 1
PUMPS = (3, 1, 1, 1, 1, 1, 1, 1, 1, 2, 2, 1, 1)

epsilon = 1e-06
rope_base = 50000.0
BF = jnp.bfloat16
F32 = jnp.float32


def inverse_rms(value):
    return lax.rsqrt(jnp.mean(value * value, axis=-1, keepdims=True) + epsilon)


def rope_tables(seq_len, head_width):
    half_dim = head_width // 2
    position = jnp.arange(seq_len, dtype=jnp.float32)
    frequency = rope_base ** (-jnp.arange(half_dim, dtype=jnp.float32) * 2.0 / head_width)
    angles = position[:, None] * frequency[None, :]
    return (jnp.cos(angles)[:, None, :], jnp.sin(angles)[:, None, :])


def rotate(value, cosine, sine_table, direction):
    half_dim = value.shape[-1] // 2
    first_half = value[..., :half_dim]
    second_half = value[..., half_dim:]
    return jnp.concatenate(
        [
            first_half * cosine - direction * second_half * sine_table,
            second_half * cosine + direction * first_half * sine_table,
        ],
        axis=-1,
    )


def head_back(grad_rot, value_hat, inverse, scale_gain, cosine, sine_table):
    grad_scaled = rotate(grad_rot, cosine, sine_table, -1.0)
    grad_gain = jnp.sum(grad_scaled * value_hat, axis=(0, 1, 2))
    grad_hat = grad_scaled * scale_gain
    grad_value = inverse * (
        grad_hat - value_hat * jnp.mean(grad_hat * value_hat, axis=-1, keepdims=True)
    )
    return (grad_value.astype(BF), grad_gain)


def dot(a, b, dims):
    return lax.dot_general(a, b, (dims, ((), ())), preferred_element_type=F32)


MESH = pl.DeviceIdType.MESH


def peer(bits):
    return (lax.axis_index("rep"), lax.axis_index("shard") ^ bits)


def along(rank):
    return (rank, lax.axis_index("shard"))


def meet(n_rep, n_shard):
    barrier = pltpu.get_barrier_semaphore()
    for bits in range(1, n_shard):
        pl.semaphore_signal(barrier, inc=1, device_id=peer(bits), device_id_type=MESH)
    rep, shard = lax.axis_index("rep"), lax.axis_index("shard")
    for bits in range(1, n_rep):
        pl.semaphore_signal(barrier, inc=1, device_id=(rep ^ bits, shard), device_id_type=MESH)
    pl.semaphore_wait(barrier, n_shard + n_rep - 2)


def remote(src, dst, send, recv, to):
    return pltpu.make_async_remote_copy(
        src_ref=src, dst_ref=dst, send_sem=send, recv_sem=recv, device_id=to, device_id_type=MESH
    )


def down_at(e):
    return jnp.maximum(3 * e - 2, 0)


def gate_up_at(e, experts):
    return 3 * e + jnp.where(e == experts - 1, 1, 2)


class Line:
    def __init__(self, part, into1, into2, total, bufs, sems, base=0, landed=0, crossed=0, window=2, lag=2):
        self.part, self.into1, self.into2, self.total = part, into1, into2, total
        self.pbuf, self.ibuf, self.sbuf, self.tbuf = bufs
        (self.s1, self.r1, self.s2, self.r2, self.s3, self.r3, self.ld, self.st) = sems
        self.ring = self.sbuf.shape[0]
        self.base = base
        self.fresh = base + landed
        self.crossed = base + crossed
        self.lag = lag
        self.window = window
        rank = lax.axis_index("rep")
        self.middle = (rank == 1) | (rank == 2)
        self.end = (rank == 0) | (rank == 3)
        self.next = along(rank ^ 1)
        self.across = along(rank ^ 3)

    def first(self, u):
        i = u - self.base
        return remote(self.part.at[u], self.into1.at[u], self.s1.at[i], self.r1.at[i], self.next)

    def second(self, u):
        i = u - self.base
        slot = lax.rem(i, self.ring)
        return remote(
            self.sbuf.at[slot], self.into2.at[u], self.s2.at[i], self.r2.at[i], self.across
        )

    def third(self, u):
        i = u - self.base
        slot = lax.rem(i, 2)
        return remote(self.tbuf.at[slot], self.total.at[u], self.s3.at[i], self.r3.at[i], self.next)

    def keep(self, u):
        i = u - self.base
        slot = lax.rem(i, 2)
        return pltpu.make_async_copy(self.tbuf.at[slot], self.total.at[u], self.st.at[slot])

    def launch(self, u):
        @pl.when(self.end)
        def _():
            self.first(u).start()

    def add(self, dst, x, y):
        tile = 128

        def body(i, c):
            r = pl.ds(pl.multiple_of(i * tile, tile), tile)
            dst[r, :] = (x[r, :].astype(F32) + y[r, :].astype(F32)).astype(BF)
            return c

        lax.fori_loop(0, dst.shape[0] // tile, body, 0)

    def add_first(self, u):
        i = u - self.base

        @pl.when(self.middle & (u >= self.crossed))
        def _():
            own = pltpu.make_async_copy(self.part.at[u], self.pbuf, self.ld.at[0])
            own.start()

            @pl.when(u >= self.fresh)
            def _():
                self.first(u).wait_recv()

            got = pltpu.make_async_copy(self.into1.at[u], self.ibuf, self.ld.at[1])
            got.start()
            own.wait()
            got.wait()
            self.add(self.sbuf.at[lax.rem(i, self.ring)], self.pbuf, self.ibuf)
            self.second(u).start()

    def kept(self, u):
        slot = lax.rem(u - self.base, self.ring)
        return pltpu.make_async_copy(
            self.sbuf.at[slot], self.part.at[u], self.st.at[2 + lax.rem(u, 2)]
        )

    def add_second(self, u):
        i = u - self.base

        @pl.when(self.middle)
        def _():
            slot = lax.rem(i, self.ring)
            again = pltpu.make_async_copy(self.part.at[u], self.sbuf.at[slot], self.ld.at[0])

            @pl.when(u >= self.crossed)
            def _():
                self.second(u).wait_recv()

            @pl.when(u < self.crossed)
            def _():
                again.start()

            got = pltpu.make_async_copy(self.into2.at[u], self.ibuf, self.ld.at[1])
            got.start()

            @pl.when(i >= 2)
            def _():
                self.third(u - 2).wait_send()
                self.keep(u - 2).wait()

            @pl.when(u < self.crossed)
            def _():
                again.wait()

            got.wait()
            self.add(self.tbuf.at[lax.rem(i, 2)], self.sbuf.at[slot], self.ibuf)

            @pl.when(u >= self.crossed)
            def _():
                self.second(u).wait_send()

            self.third(u).start()
            self.keep(u).start()

    def step(self, u, limit):
        narrow = limit - 2 - self.window if self.window > 2 else 0

        @pl.when(self.end & (u >= self.fresh))
        def _():
            self.first(u).wait_send()

            @pl.when((u >= narrow + self.window - 2) & (u + 2 < limit))
            def _():
                self.first(u + 2).start()

            @pl.when(u < narrow)
            def _():
                self.first(u + self.window).start()

        self.add_first(u)

        @pl.when(u >= self.crossed + self.lag)
        def _():
            self.add_second(u - self.lag)

    def steps(self, low, high, limit):
        def body(u, c):
            self.step(u, limit)
            return c

        lax.fori_loop(low, high, body, 0)

    def finish(self, last, ahead=0, cross=0):
        for i in range(self.lag):
            self.add_second(last - self.lag + i)
            if i < cross:
                self.add_first(last + i)

                @pl.when(self.middle)
                def _():
                    self.kept(last + i).start()

        for u in range(last, last + ahead):
            @pl.when(self.end)
            def _():
                self.first(u).wait_send()
                if u + 2 < last + ahead:
                    self.first(u + 2).start()

            @pl.when(self.middle)
            def _():
                if u >= last + cross:
                    self.first(u).wait_recv()

        @pl.when(self.middle)
        def _():
            for u in range(last, last + cross):
                self.second(u).wait()
                self.kept(u).wait()

        @pl.when(self.middle)
        def _():
            for u in range(last - 2, last):
                self.third(u).wait_send()
                self.keep(u).wait()

        @pl.when(self.end)
        def _():
            def body(u, c):
                self.third(u).wait_recv()
                return c

            lax.fori_loop(self.base, last, body, 0)


def line_scratch(slots):
    dma = pltpu.SemaphoreType.DMA
    return [dma((slots,)) for _ in range(6)] + [dma((2,)), dma((4,))]


def scatter_blocks(block, width, step, stage, in1, in2, acc, out, sems):
    s1, r1, s2, r2, so = sems
    pairs, seq = stage.shape[0], stage.shape[1]

    def cols(j):
        return pl.ds(pl.multiple_of(j * step, step), step)

    def pair(j):
        return remote(
            stage.at[:, :, cols(j)], in1.at[:, :, cols(j)], s1.at[j], r1.at[j], peer(1)
        )

    def odd(j, c):
        stage[:, :, cols(j)] = block(1, j).reshape(pairs, seq, step).astype(BF)
        pair(j).start()
        return c

    n = width // step
    lax.fori_loop(0, n, odd, 0)

    def sent(j, c):
        pair(j).wait_send()
        return c

    lax.fori_loop(0, n, sent, 0)

    def even(j, c):
        value = block(0, j).reshape(pairs, seq, step)
        pair(j).wait_recv()
        value = value + in1[:, :, cols(j)].astype(F32)
        acc[:, cols(j)] = value[0]
        stage[:, :, cols(j)] = value.astype(BF)
        return c

    lax.fori_loop(0, n, even, 0)
    far = [
        remote(stage.at[i], in2.at[i - 1], s2.at[i], r2.at[i], peer(2 * i)) for i in range(1, pairs)
    ]

    def send():
        for copy in far:
            copy.start()

    def finish():
        for copy in far:
            copy.wait()
        for i in range(pairs - 1):
            acc[...] = acc[...] + in2[i].astype(F32)
        if out is not None:
            copy = pltpu.make_async_copy(acc, out, so)
            copy.start()
            copy.wait()

    return send, finish


class Columns:
    def __init__(self, gate_hbm, up_hbm, place, fbuf, stage, sems, first, last):
        self.gate, self.up, self.place = gate_hbm, up_hbm, place
        self.fbuf, self.stage = fbuf, stage
        self.ld, self.send, self.recv = sems
        self.first, self.last = first, last
        self.me = lax.axis_index("shard")
        self.n = stage.shape[1]

    def loads(self, e):
        slot = lax.rem(e, 2)
        return (
            pltpu.make_async_copy(self.gate.at[e], self.fbuf.at[slot, 0], self.ld.at[slot, 0]),
            pltpu.make_async_copy(self.up.at[e], self.fbuf.at[slot, 1], self.ld.at[slot, 1]),
        )

    def load(self, e):
        for copy in self.loads(e):
            copy.start()

    def copy_to(self, e, owner):
        away = owner ^ self.me
        slot = lax.rem(e, 2)
        return remote(
            self.stage.at[slot, owner], self.place(e, self.me), self.send.at[slot, away],
            self.recv.at[e, away], peer(away),
        )

    def sent(self, e):
        for b in range(1, self.n):
            self.copy_to(e, self.me ^ b).wait_send()

    def prepare(self, e, keep):
        for copy in self.loads(e):
            copy.wait()

        @pl.when(e >= self.first + 2)
        def _():
            self.sent(e - 2)

        slot = lax.rem(e, 2)
        size = self.fbuf.shape[3] // self.n
        for owner in range(self.n):
            c = slice(owner * size, (owner + 1) * size)
            block = jnp.concatenate([self.fbuf[slot, i, :, c] for i in range(2)], axis=1)
            self.stage[slot, owner] = block.astype(BF)

            @pl.when(owner != self.me)
            def _():
                self.copy_to(e, owner).start()

        keep(e, slot)

        @pl.when(e + 2 < self.last)
        def _():
            self.load(e + 2)

    def arrived(self, e):
        for b in range(1, self.n):
            self.copy_to(e, self.me ^ b).wait_recv()


def spread_sends(src, land, send, recv, n_shard):
    def copy(i):
        rows = src if i == 1 or i % 2 == 0 else land.at[i - 1]
        return remote(rows, land.at[i], send.at[i], recv.at[i], peer(i if i % 2 == 0 else 1))

    return copy


def expert_kernel(
    n_rep, n_shard, experts, f_loc, head_units, ahead,
    x2_hbm, dy_hbm, gate_hbm, w_hbm, wd_hbm, wg_hbm, wu_hbm, h1_hbm, pr_hbm, hit_hbm, small_hbm,
    part, into1, into2, total, gh_out, da_out, dh1_out, pay_out, wd_out,
    x2, x2t, dy, gate, w, wd, gh, dgu, dg, dstage, gstage, stage, in1, in2, acc, dgin,
    fbuf, cstage, wdf, h1, pr, hit, small, da, pay, pbuf, ibuf, sbuf, tbuf,
    ld_sem, w_sem, h_sem, c_ld, c_send, c_recv, d_sem, l_sem, a_send, a_recv, g_send, g_recv, rs_j, rr_j, rs_b, rr_b, o_sem,
    z1, y1, z2, y2, z3, y3, zl, zs,
):
    me = lax.axis_index("shard")
    tokens, width = x2.shape
    seq = tokens // n_shard
    rows = width // n_shard
    cols = 2 * f_loc
    half = n_shard // 2
    loads = [
        pltpu.make_async_copy(gate_hbm, gate, ld_sem.at[0]),
        pltpu.make_async_copy(x2_hbm, x2, ld_sem.at[1]),
        pltpu.make_async_copy(dy_hbm, dy, ld_sem.at[2]),
    ]
    late = ((h1_hbm, h1), (pr_hbm, pr), (hit_hbm, hit), (small_hbm, small))
    late = [pltpu.make_async_copy(x, y, ld_sem.at[3 + i]) for i, (x, y) in enumerate(late)]

    def ecols(e, size):
        return pl.ds(pl.multiple_of(e * size, size), size)

    head = w_hbm.shape[2] // cols

    def load_head(e):
        c = pl.ds(e * cols, cols)
        return pltpu.make_async_copy(w_hbm.at[:, :, c], w.at[:, :, c], w_sem.at[0, e])

    def load_down(e):
        slot = lax.rem(e, 2)
        return pltpu.make_async_copy(wd_hbm.at[e], wdf.at[slot], w_sem.at[1, slot])

    columns = Columns(
        wg_hbm, wu_hbm, lambda e, src: w.at[src, :, ecols(e, cols)], fbuf, cstage,
        (c_ld, c_send, c_recv), head, experts,
    )

    def keep(e, slot):
        w[me, :, ecols(e, cols)] = cstage[slot, me]

    load_down(0).start()
    for e in range(head):
        load_head(e).start()
    for copy in loads:
        copy.start()
    columns.load(head)
    columns.load(head + 1)
    load_down(1).start()
    meet(n_rep, n_shard)
    columns.prepare(head, keep)
    dg[...] = jnp.zeros_like(dg)
    for copy in loads:
        copy.wait()

    for e in range(head):
        load_head(e).wait()
    line = Line(
        part, into1, into2, total, (pbuf, ibuf, sbuf, tbuf), (z1, y1, z2, y2, z3, y3, zl, zs)
    )

    def place(ref, e, owner):
        start = pl.multiple_of(lax.rem(owner, half) * rows, rows)
        return ref.at[gate_up_at(e, experts) + owner // half, pl.ds(start, rows), :]

    def send_block(e, b):
        return remote(
            gstage.at[lax.rem(e, 2), b], place(part, e, me), a_send.at[lax.rem(e, 2), b],
            a_recv.at[e, b], peer(b),
        )

    def own_block(e):
        return pltpu.make_async_copy(
            gstage.at[lax.rem(e, 2), 0], place(part, e, me), l_sem.at[lax.rem(e, 2)]
        )

    def down_unit(e):
        return pltpu.make_async_copy(
            dstage.at[lax.rem(e, 2)], part.at[down_at(e)], d_sem.at[lax.rem(e, 2)]
        )

    def gh_copy(e):
        return pltpu.make_async_copy(gh.at[lax.rem(e, 2)], gh_out.at[e], h_sem.at[lax.rem(e, 2)])

    tile = 2 * seq

    def expert(e, carry):
        load_down(e).wait()
        slot = lax.rem(e, 2)
        wd[e] = wdf[slot].astype(BF)

        @pl.when(e + 2 < experts)
        def _():
            load_down(e + 2).start()

        @pl.when(e >= 2)
        def _():
            gh_copy(e - 2).wait()

        @pl.when(e >= head)
        def _():
            columns.arrived(e)

        def tokens_tile(i, c):
            r = pl.ds(pl.multiple_of(i * tile, tile), tile)
            pre = jnp.dot(
                x2[r, :],
                w[:, :, ecols(e, cols)].reshape(width, cols),
                preferred_element_type=F32,
            )
            g_pre, u_pre = (pre[:, :f_loc], pre[:, f_loc:])
            z = dot(dy[r, :], wd[e], ((1,), (1,)))
            lane = lax.broadcasted_iota(jnp.int32, (tile, gate.shape[1]), 1)
            own = lane == e
            gt = jnp.sum(jnp.where(own, gate[r, :], 0.0), axis=1, keepdims=True)
            sig = jax.nn.sigmoid(g_pre)
            act = g_pre * sig
            hh = act * u_pre
            dsum = jnp.sum(hh.astype(BF).astype(F32) * z, axis=1, keepdims=True)
            dg[r, :] = dg[r, :] + jnp.where(own, dsum, 0.0)
            gh[slot, r, :] = (gt * hh).astype(BF)
            dh = gt * z
            d_gate = (dh * u_pre * sig * (1.0 + g_pre * (1.0 - sig))).astype(BF)
            d_up = (dh * act).astype(BF)
            dgu[e, i] = jnp.concatenate([d_gate, d_up], axis=1).reshape(2, seq, cols)
            return c

        lax.fori_loop(0, tokens // tile, tokens_tile, 0)

        if head_units:
            @pl.when(e >= 2)
            def _():
                line.step(2 * e - 3, head_units + ahead)

        @pl.when((e >= 1) & (e + 1 < experts))
        def _():
            columns.prepare(e + 1, keep)

        gh_copy(e).start()
        ght = gh[slot].T

        def down_block(j, c):
            r = pl.ds(pl.multiple_of(j * f_loc, f_loc), f_loc)
            dstage[slot, r, :] = jnp.dot(
                ght, dy[:, ecols(j, cols)], preferred_element_type=F32
            ).astype(BF)
            return c

        lax.fori_loop(0, width // cols, down_block, 0)
        down_unit(e).start()
        down_unit(e).wait()

        if head_units:
            @pl.when(e < 2)
            def _():
                line.launch(e)

        @pl.when(e == 0)
        def _():
            def turn(i, c):
                for j in range(n_shard):
                    x2t[j * rows : (j + 1) * rows, ecols(i, seq)] = x2[
                        ecols(i, seq), j * rows : (j + 1) * rows
                    ].T
                return c

            lax.fori_loop(0, n_shard, turn, 0)

        @pl.when(e >= 2)
        def _():
            for b in range(1, n_shard):
                send_block(e - 2, b).wait_send()

        def grad_block(b, c):
            owner = me ^ b
            r = pl.ds(pl.multiple_of(owner * rows, rows), rows)
            value = jnp.dot(
                x2t[r, :], dgu[e].reshape(tokens, cols), preferred_element_type=F32
            ).astype(BF)
            gstage[slot, b] = value

            @pl.when(b > 0)
            def _():
                send_block(e, b).start()

            return c

        lax.fori_loop(0, n_shard, grad_block, 0)
        own_block(e).start()

        def ready(x):
            for b in range(1, n_shard):
                send_block(x, b).wait_recv()
            own_block(x).wait()

        @pl.when(e >= 1)
        def _():
            ready(e - 1)

        @pl.when(e == experts - 1)
        def _():
            ready(e)

        if head_units:
            @pl.when(e >= 1)
            def _():
                line.step(2 * e - 2, head_units + ahead)

        return carry

    lax.fori_loop(0, experts, expert, 0)
    for e in (experts - 2, experts - 1):
        columns.sent(e)
        for b in range(1, n_shard):
            send_block(e, b).wait_send()

    wd_copy = pltpu.make_async_copy(wd, wd_out, ld_sem.at[0])
    wd_copy.start()

    def gate_copy(b):
        return remote(
            dg.at[pl.ds(b * seq, seq), :], dgin.at[b - 1], g_send.at[b], g_recv.at[b], peer(b)
        )

    for b in range(1, n_shard):
        gate_copy(b).start()

    def dx2_block(parity, j):
        total_block = None
        for e in range(experts):
            lhs = dgu[e, :, parity].reshape(half * seq, cols)
            term = dot(lhs, w[j, :, e * cols : (e + 1) * cols], ((1,), (1,)))
            total_block = term if total_block is None else total_block + term
        return total_block

    for copy in late:
        copy.start()
    send, finish = scatter_blocks(
        dx2_block, width, rows, stage, in1, in2, acc, None, (rs_j, rr_j, rs_b, rr_b, None)
    )
    send()
    if head_units:
        line.steps(2 * experts - 3, head_units - 1, head_units + ahead)
    for b in range(1, n_shard):
        gate_copy(b).wait()
        dg[pl.ds(0, seq), :] = dg[pl.ds(0, seq), :] + dgin[b - 1]
    finish()
    for copy in late:
        copy.wait()

    probs = pr[...]
    dpr = dg[pl.ds(0, seq), :] * hit[...]
    dz = probs * (dpr - jnp.sum(probs * dpr, axis=-1, keepdims=True))
    low = dz.astype(BF)
    taps = pltpu.roll(low.astype(F32), 2, 1)[:, :16].astype(BF)
    pay[...] = jnp.zeros_like(pay)
    pay[2 : experts + 2, :] = dot(low.T, x2[pl.ds(0, seq), :], ((1,), (0,)))[:experts]
    gain = small[1:2, :].astype(BF).astype(F32)
    inverse = lax.rsqrt(jnp.mean(h1[...] * h1[...], axis=-1, keepdims=True) + epsilon)
    n2 = h1[...] * inverse
    dx2 = acc[...] + dot(taps, small[...].astype(BF), ((1,), (0,)))
    pay[1:2, :] = jnp.sum(dx2 * n2, axis=0, keepdims=True)
    e2 = dx2 * gain
    dh1 = dy[pl.ds(0, seq), :].astype(F32) + inverse * (
        e2 - n2 * jnp.mean(e2 * n2, axis=-1, keepdims=True)
    )
    acc[...] = dh1
    da[...] = dh1.astype(BF)
    outs = ((acc, dh1_out), (da, da_out), (pay, pay_out))
    outs = [pltpu.make_async_copy(x, y, ld_sem.at[3 + i]) for i, (x, y) in enumerate(outs)]
    for copy in outs:
        copy.start()
    for copy in outs:
        copy.wait()
    wd_copy.wait()
    for e in (experts - 2, experts - 1):
        gh_copy(e).wait()
    if head_units:
        line.step(head_units - 1, head_units + ahead)
        line.finish(head_units, ahead, CROSSED)


def experts_call(
    x2, dy, gate, w, wd, w_gate, w_up, h1, pr, hit, small, n_rep, n_shard
):
    tokens, width = x2.shape
    experts, f_loc = wd.shape[:2]
    seq, rows, cols, half = tokens // n_shard, width // n_shard, 2 * f_loc, n_shard // 2
    head_units = HEAD_UNITS if n_rep == 4 else 0
    units = 3 * experts + 8
    ahead = SENT_AHEAD if head_units else 0
    slots = max(head_units, 1) + ahead
    unit = (width // 2, cols)
    dma = pltpu.SemaphoreType.DMA
    anyspec = pl.BlockSpec(memory_space=pl.ANY)
    shape = jax.ShapeDtypeStruct
    return pl.pallas_call(
        partial(expert_kernel, n_rep, n_shard, experts, f_loc, head_units, ahead),
        out_shape=(
            shape((units,) + unit, BF),
            shape((units if head_units else 1,) + unit, BF),
            shape((units if head_units else 1,) + unit, BF),
            shape((units if head_units else 1,) + unit, BF),
            shape((experts, tokens, f_loc), BF),
            shape((seq, width), BF),
            shape((seq, width), F32),
            shape((16, width), F32),
            shape(wd.shape, BF),
        ),
        in_specs=[anyspec] * 11,
        out_specs=(anyspec,) * 9,
        scratch_shapes=[
            pltpu.VMEM((tokens, width), BF),
            pltpu.VMEM((width, tokens), BF),
            pltpu.VMEM((tokens, width), BF),
            pltpu.VMEM(gate.shape, F32),
            pltpu.VMEM((n_shard, rows, experts * cols), BF),
            pltpu.VMEM(wd.shape, BF),
            pltpu.VMEM((2, tokens, f_loc), BF),
            pltpu.VMEM((experts, half, 2, seq, cols), BF),
            pltpu.VMEM(gate.shape, F32),
            pltpu.VMEM((2,) + unit, BF),
            pltpu.VMEM((2, n_shard, rows, cols), BF),
            pltpu.VMEM((half, seq, width), BF),
            pltpu.VMEM((half, seq, width), BF),
            pltpu.VMEM((half - 1, seq, width), BF),
            pltpu.VMEM((seq, width), F32),
            pltpu.VMEM((n_shard - 1, seq, gate.shape[1]), F32),
            pltpu.VMEM((2, 2) + w_gate.shape[1:], F32),
            pltpu.VMEM((2, n_shard, rows, cols), BF),
            pltpu.VMEM((2,) + wd.shape[1:], F32),
            pltpu.VMEM(h1.shape, F32),
            pltpu.VMEM(pr.shape, F32),
            pltpu.VMEM(hit.shape, F32),
            pltpu.VMEM(small.shape, F32),
            pltpu.VMEM((seq, width), BF),
            pltpu.VMEM((16, width), F32),
            pltpu.VMEM(unit if head_units else (8, cols), BF),
            pltpu.VMEM(unit if head_units else (8, cols), BF),
            pltpu.VMEM((4 if head_units else 1,) + unit, BF),
            pltpu.VMEM((2 if head_units else 1,) + unit, BF),
            dma((7,)),
            dma((2, experts)),
            dma((2,)),
            dma((2, 2)),
            dma((2, n_shard)),
            dma((experts, n_shard)),
            dma((2,)),
            dma((2,)),
            dma((2, n_shard)),
            dma((experts, n_shard)),
            dma((n_shard,)),
            dma((n_shard,)),
            dma((n_shard,)),
            dma((n_shard,)),
            dma((half,)),
            dma((half,)),
            dma,
        ]
        + line_scratch(slots),
        compiler_params=pltpu.CompilerParams(
            collective_id=1, has_side_effects=True, vmem_limit_bytes=67000000
        ),
        name="experts",
    )(x2, dy, gate, w, wd, w_gate, w_up, h1, pr, hit, small)


def attention_kernel(
    n_rep, n_shard, experts, f_loc, head_units, ahead,
    da_hbm, x1_hbm, a_hbm, wqkv_hbm, wo_hbm, qkvr_hbm, q_hbm, k_hbm, seg_hbm, table_hbm, gain_hbm,
    gh_hbm, wd_hbm, tok_hbm, pay_hbm, h1_hbm, dh1_hbm, small_hbm, part_in, into1_in, into2_in, total_in,
    part, into1, into2, total, gtok_out, out_out, pay_out,
    da, x1, a, wqkv, wo, qkvr, q, k, seg, table, gain, gh, wd, tok, pay, h1, dh1, small,
    do, dqkv, ggain, payin, payrep, dstage, gstage, stage, in1, in2, acc,
    pbuf, ibuf, sbuf, tbuf,
    ld_sem, f_send, f_recv, d_sem, l_sem, a_send, a_recv,
    rs_j, rr_j, rs_b, rr_b, ts_j, tr_j, ts_b, tr_b, p_send, p_recv, q_send, q_recv, o_sem,
    z1, y1, z2, y2, z3, y3, zl, zs,
):
    me = lax.axis_index("shard")
    half, seq, width = stage.shape
    tokens = n_shard * seq
    rows = width // n_shard
    cols = rows
    heads = cols // HEAD_DIM
    scale = HEAD_DIM ** (-0.5)
    first_unit = 3 * experts
    pairs = (
        (x1_hbm, x1), (a_hbm, a), (wo_hbm, wo), (qkvr_hbm, qkvr), (q_hbm, q), (k_hbm, k),
        (seg_hbm, seg), (table_hbm, table), (gain_hbm, gain), (wqkv_hbm, wqkv), (gh_hbm, gh),
        (wd_hbm, wd), (tok_hbm, tok), (pay_hbm, pay),
        (h1_hbm, h1), (dh1_hbm, dh1), (small_hbm, small),
    )
    loads = [pltpu.make_async_copy(x, y, ld_sem.at[i]) for i, (x, y) in enumerate(pairs)]
    mine = pltpu.make_async_copy(da_hbm, da.at[0], ld_sem.at[len(pairs)])
    mine.start()
    for copy in (*loads[10:12], *loads[:10], *loads[12:]):
        copy.start()
    meet(n_rep, n_shard)
    line = Line(
        part, into1, into2, total, (pbuf, ibuf, sbuf, tbuf), (z1, y1, z2, y2, z3, y3, zl, zs),
        head_units, ahead, CROSSED, WINDOW, LAG,
    )
    last_unit = first_unit + 8

    place_of = [head_units + sum(PUMPS[:i]) for i in range(len(PUMPS) + 1)]

    def pump(i):
        if head_units and PUMPS[i]:
            line.steps(place_of[i], place_of[i + 1], last_unit)

    if head_units:
        for u in range(WINDOW):
            line.launch(head_units + ahead + u)

    def block_cols(j, size):
        return pl.ds(pl.multiple_of(j * size, size), size)

    def cross_over():
        if head_units:
            for u in range(head_units, head_units + CROSSED):
                line.add_second(u)

    spread = spread_sends(da_hbm, da, f_send, f_recv, n_shard)
    for i in list(range(2, n_shard, 2)) + [1]:
        spread(i).start()
    cross_over()
    pump(0)
    for copy in loads[10:12]:
        copy.wait()

    def out_part(parity, j):
        total_block = None
        for e in range(experts):
            lhs = gh[e, :, parity].reshape(half * seq, f_loc)
            term = dot(lhs, wd[e, :, block_cols(j, cols)], ((1,), (0,)))
            total_block = term if total_block is None else total_block + term
        return total_block

    send_out, finish_out = scatter_blocks(
        out_part, width, rows, stage, in1.at[1], in2.at[1], acc.at[1], None,
        (ts_j, tr_j, ts_b, tr_b, None),
    )
    send_out()
    pump(1)
    for i in range(2, n_shard, 2):
        spread(i).wait_recv()
        spread(i + 1).start()
    for i in range(1, n_shard, 2):
        spread(i).wait_recv()
    for i in range(1, n_shard):
        spread(i).wait_send()
    mine.wait()
    for copy in loads[:9]:
        copy.wait()
    pump(2)

    at = a[...].T

    def out_block(j, c):
        r = block_cols(lax.rem(j, half), cols)
        value = jnp.dot(
            at, da[:, :, block_cols(j, cols)].reshape(tokens, cols), preferred_element_type=F32
        )
        dstage[j // half, r, :] = value.astype(BF)
        return c

    lax.fori_loop(0, n_shard, out_block, 0)
    outs = [
        pltpu.make_async_copy(dstage.at[i], part.at[first_unit + i], d_sem.at[i]) for i in range(2)
    ]
    for copy in outs:
        copy.start()

    def do_block(i, c):
        r = block_cols(i, 2 * seq)
        lhs = da[pl.ds(2 * i, 2)].reshape(2 * seq, width)
        do[r, :] = dot(lhs, wo[...], ((1,), (1,))).astype(BF)
        return c

    lax.fori_loop(0, half, do_block, 0)
    for copy in outs:
        copy.wait()
    pump(3)
    finish_out()

    cosine, sine = (table[0], table[1])

    def head_grad(grad, x, gain_row):
        inverse = lax.rsqrt(jnp.mean(x * x, axis=-1, keepdims=True) + epsilon)
        x_hat = x * inverse
        back = grad * cosine - pltpu.roll(grad, HEAD_DIM // 2, 1) * sine
        scaled = back * gain_row
        value = inverse * (scaled - x_hat * jnp.mean(scaled * x_hat, axis=-1, keepdims=True))
        return (value.astype(BF), jnp.sum(back * x_hat, axis=0, keepdims=True))

    ggain[...] = jnp.zeros_like(ggain)

    def sequence(b, carry):
        r = block_cols(b, seq)
        row = jnp.broadcast_to(seg[b].astype(F32), (seq, seq))
        same = row == row.T
        for i in range(heads):
            c = slice(i * HEAD_DIM, (i + 1) * HEAD_DIM)
            qr, kr, v = (qkvr[n, r, c] for n in range(3))
            d = do[r, c]
            s = jnp.where(same, dot(qr, kr, ((1,), (1,))) * scale, -1000000000.0)
            e = jnp.exp(s - jnp.max(s, axis=-1, keepdims=True))
            p = e / jnp.sum(e, axis=-1, keepdims=True)
            dv = dot(p.astype(BF).T, d, ((1,), (0,)))
            dp = dot(d, v, ((1,), (1,)))
            ds = (p * (dp - jnp.sum(p * dp, axis=-1, keepdims=True))).astype(BF)
            dqr = dot(ds, kr, ((1,), (0,))) * scale
            dkr = dot(ds.T, qr, ((1,), (0,))) * scale
            dq, gq = head_grad(dqr, q[r, c], gain[0:1, :])
            dk, gk = head_grad(dkr, k[r, c], gain[1:2, :])
            dqkv[0, r, c] = dq
            dqkv[1, r, c] = dk
            dqkv[2, r, c] = dv.astype(BF)
            ggain[0:1, :] = ggain[0:1, :] + gq
            ggain[1:2, :] = ggain[1:2, :] + gk
        return carry

    lax.fori_loop(0, half, sequence, 0)
    pump(4)
    lax.fori_loop(half, n_shard, sequence, 0)
    pump(5)
    for copy in (loads[9], *loads[12:]):
        copy.wait()

    def place(n, owner):
        start = pl.multiple_of(lax.rem(owner, half) * rows, rows)
        unit = first_unit + 2 + 2 * (2 - n) + owner // half
        return part.at[unit, pl.ds(start, rows), :]

    def send_block(n, b):
        return remote(gstage.at[n, b], place(n, me), a_send.at[n, b], a_recv.at[n, b], peer(b))

    def own_block(n):
        return pltpu.make_async_copy(gstage.at[n, 0], place(n, me), l_sem.at[n])

    def weight_grad(i, carry):
        n = 2 - i
        grad_t = dqkv[n].T

        def block(b, c):
            owner = me ^ b
            value = jnp.dot(
                grad_t,
                x1[:, :, block_cols(owner, rows)].reshape(tokens, rows),
                preferred_element_type=F32,
            )
            gstage[n, b] = value.T.astype(BF)

            @pl.when(b > 0)
            def _():
                send_block(n, b).start()

            return c

        lax.fori_loop(0, n_shard, block, 0)
        own_block(n).start()
        return carry

    lax.fori_loop(0, 3, weight_grad, 0)
    pump(6)

    def grad_ready(n):
        for b in range(1, n_shard):
            send_block(n, b).wait()
        own_block(n).wait()

    def dx1_block(parity, j):
        total_block = None
        for n in range(3):
            lhs = dqkv[n].reshape(half, 2, seq, cols)[:, parity].reshape(half * seq, cols)
            term = dot(lhs, wqkv[block_cols(j, rows), n * cols : (n + 1) * cols], ((1,), (1,)))
            total_block = term if total_block is None else total_block + term
        return total_block

    send_dx1, finish_dx1 = scatter_blocks(
        dx1_block, width, rows, stage, in1.at[0], in2.at[0], acc.at[0], None,
        (rs_j, rr_j, rs_b, rr_b, None),
    )
    pump(7)
    for n in (2, 1, 0):
        grad_ready(n)
    send_dx1()
    pump(8)
    pump(9)
    finish_dx1()
    pump(10)

    rank = lax.axis_index("rep")
    h = tok[...].astype(F32)
    r1 = lax.rsqrt(jnp.mean(h * h, axis=-1, keepdims=True) + epsilon)
    n1 = h * r1
    dx1 = acc[0]
    pay[0:1, :] = jnp.sum(dx1 * n1, axis=0, keepdims=True)
    e1 = dx1 * small[0:1, :].astype(BF).astype(F32)
    dh1[...] = dh1[...] + r1 * (e1 - n1 * jnp.mean(e1 * n1, axis=-1, keepdims=True))
    tok[...] = (h1[...] + acc[1]).astype(BF)
    done = ((dh1, gtok_out), (tok, out_out))
    done = [pltpu.make_async_copy(x, y, o_sem.at[i]) for i, (x, y) in enumerate(done)]
    for copy in done:
        copy.start()
    for i in range(width // HEAD_DIM):
        pay[experts + 2 : experts + 4, i * HEAD_DIM : (i + 1) * HEAD_DIM] = ggain[0:2, :]

    def owner_copy(b):
        return remote(
            pay.at[:, block_cols(me ^ b, cols)], payin.at[b], p_send.at[b], p_recv.at[b], peer(b)
        )

    for b in range(1, n_shard):
        owner_copy(b).start()
    payin[0] = pay[:, block_cols(me, cols)]
    pump(11)
    for b in range(1, n_shard):
        owner_copy(b).wait()
        payin[0] = payin[0] + payin[b]

    def rep_copy(b):
        return remote(
            payin.at[0], payrep.at[rank], q_send.at[b], q_recv.at[b], along(rank ^ b)
        )

    for b in range(1, n_rep):
        rep_copy(b).start()
    payrep[rank] = payin[0]
    pump(12)
    for b in range(1, n_rep):
        rep_copy(b).wait()
    summed = payrep[0]
    for i in range(1, n_rep):
        summed = summed + payrep[i]
    payin[1] = summed
    copy = pltpu.make_async_copy(payin.at[1], pay_out, o_sem.at[2])
    copy.start()
    copy.wait()
    for copy in done:
        copy.wait()
    if head_units:
        line.steps(place_of[-1], last_unit, last_unit)
        line.finish(last_unit)


def attention_call(
    da, x1, a, wqkv, wo, qkvr, q, k, seg, table, gain, gh, wd, tok, pay, h1, dh1, small, part, into1,
    into2, total, n_rep, n_shard, head_units,
):
    seq, width = da.shape
    tokens, cols = a.shape
    experts, f_loc = wd.shape[:2]
    half = n_shard // 2
    units = part.shape[0]
    slots = units - head_units if head_units else 1
    unit = part.shape[1:]
    gh = gh.reshape(experts, half, 2, seq, f_loc)
    dma = pltpu.SemaphoreType.DMA
    anyspec = pl.BlockSpec(memory_space=pl.ANY)
    shape = jax.ShapeDtypeStruct
    whole = (x1, a, wqkv, wo, qkvr, q, k, seg, table, gain, gh, wd, tok, pay, h1, dh1, small)
    return pl.pallas_call(
        partial(
            attention_kernel, n_rep, n_shard, experts, f_loc, head_units,
            SENT_AHEAD if head_units else 0,
        ),
        out_shape=(
            shape(part.shape, BF),
            shape(into1.shape, BF),
            shape(into2.shape, BF),
            shape(total.shape, BF),
            shape((seq, width), F32),
            shape((seq, width), BF),
            shape((pay.shape[0], width // n_shard), F32),
        ),
        in_specs=[anyspec] * 22,
        out_specs=(anyspec,) * 7,
        input_output_aliases={18: 0, 19: 1, 20: 2, 21: 3},
        scratch_shapes=[pltpu.VMEM((n_shard, seq, width), BF)]
        + [pltpu.VMEM(x.shape, x.dtype) for x in whole]
        + [
            pltpu.VMEM((tokens, cols), BF),
            pltpu.VMEM((3, tokens, cols), BF),
            pltpu.VMEM((8, HEAD_DIM), F32),
            pltpu.VMEM((n_shard, pay.shape[0], cols), F32),
            pltpu.VMEM((n_rep, pay.shape[0], cols), F32),
            pltpu.VMEM((2,) + unit, BF),
            pltpu.VMEM((3, n_shard, cols, cols), BF),
            pltpu.VMEM((half, seq, width), BF),
            pltpu.VMEM((2, half, seq, width), BF),
            pltpu.VMEM((2, half - 1, seq, width), BF),
            pltpu.VMEM((2, seq, width), F32),
            pltpu.VMEM(unit, BF),
            pltpu.VMEM(unit, BF),
            pltpu.VMEM((4 if head_units else 1,) + unit, BF),
            pltpu.VMEM((2 if head_units else 1,) + unit, BF),
            dma((18,)),
            dma((n_shard,)),
            dma((n_shard,)),
            dma((2,)),
            dma((3,)),
            dma((3, n_shard)),
            dma((3, n_shard)),
            dma((n_shard,)),
            dma((n_shard,)),
            dma((half,)),
            dma((half,)),
            dma((n_shard,)),
            dma((n_shard,)),
            dma((half,)),
            dma((half,)),
            dma((n_shard,)),
            dma((n_shard,)),
            dma((n_rep,)),
            dma((n_rep,)),
            dma((3,)),
        ]
        + line_scratch(slots),
        compiler_params=pltpu.CompilerParams(
            collective_id=2, has_side_effects=True, vmem_limit_bytes=67000000
        ),
        name="attention",
    )(da, *whole, part, into1, into2, total)


def forward_kernel(
    n_rep, n_shard, experts, head,
    tok_hbm, small_hbm, seg_hbm, route_hbm, dy_hbm, wq_hbm, wk_hbm, wv_hbm, wo_hbm, table_hbm,
    wg_hbm, wu_hbm,
    x1_out, x2_out, dy_out, gate_out, w_out, wqkv_out, wo_out, qkvr_out, q_out, k_out, a_out,
    seg_out, h1_out, pr_out, small_out, hit_out, gain_out,
    tok, small, seg, hit, gain, route, wf, wof, table, x1, wqkv, wst, wo, qkvr, q, k, a, x2, gate, pr,
    stage, in1, in2, acc, fbuf, cstage,
    ld_sem, t_send, t_recv, s_send, s_recv, e_send, e_recv, w_send, w_recv, d_send, d_recv,
    x_send, x_recv, g_send, g_recv, c_ld, c_send, c_recv, o_sem, rs_j, rr_j, rs_b, rr_b,
):
    me = lax.axis_index("shard")
    half, seq, width = stage.shape
    rows = width // n_shard
    cols = rows
    tokens = n_shard * seq
    heads = cols // HEAD_DIM
    scale = HEAD_DIM ** (-0.5)
    cut = w_out.shape[2] // head

    def block_cols(j, size):
        return pl.ds(pl.multiple_of(j * size, size), size)

    pairs = (
        (tok_hbm, tok.at[0]), (small_hbm, small.at[:, block_cols(me, rows)]),
        (wq_hbm, wf.at[0]), (wk_hbm, wf.at[1]), (wv_hbm, wf.at[2]), (wo_hbm, wof),
        (seg_hbm, seg.at[0]), (route_hbm, route), (table_hbm, table),
    )
    loads = [pltpu.make_async_copy(x, y, ld_sem.at[i]) for i, (x, y) in enumerate(pairs)]
    for copy in loads:
        copy.start()
    columns = Columns(
        wg_hbm, wu_hbm, lambda e, src: w_out.at[src, :, block_cols(e, cut)], fbuf, cstage,
        (c_ld, c_send, c_recv), 0, head,
    )
    for e in range(min(head, 2)):
        columns.load(e)
    dy_own = pltpu.make_async_copy(dy_hbm, dy_out.at[0], ld_sem.at[len(pairs)])
    dy_own.start()
    meet(n_rep, n_shard)

    def small_copy(b):
        return remote(
            small_hbm, small.at[:, block_cols(me, rows)], s_send.at[b], s_recv.at[b], peer(b)
        )

    def seg_copy(b):
        return remote(seg_hbm, seg.at[b], e_send.at[b], e_recv.at[b], peer(b))

    for b in range(1, n_shard):
        small_copy(b).start()
        seg_copy(b).start()
    spread = spread_sends(tok_hbm, tok, t_send, t_recv, n_shard)
    for i in list(range(2, n_shard, 2)) + [1]:
        spread(i).start()

    def w_copy(owner):
        away = owner ^ me
        return remote(
            wst.at[owner], wqkv.at[block_cols(me, rows), :], w_send.at[away], w_recv.at[away],
            peer(away),
        )

    for copy in loads[2:5]:
        copy.wait()

    def cast_block(owner, c):
        wst[owner] = jnp.concatenate(
            [wf[i, :, block_cols(owner, cols)] for i in range(3)], axis=1
        ).astype(BF)

        @pl.when(owner != me)
        def _():
            w_copy(owner).start()

        return c

    lax.fori_loop(0, n_shard, cast_block, 0)
    wqkv[block_cols(me, rows), :] = wst[me]
    for copy in (loads[0], loads[1], *loads[5:]):
        copy.wait()
    wo[...] = wof[...].astype(BF)
    for b in range(1, n_shard):
        small_copy(b).wait()
        seg_copy(b).wait()
    gain_attn = small[0:1, :].astype(BF).astype(F32)
    lane = lax.broadcasted_iota(jnp.int32, hit.shape, 1)
    named = jnp.zeros(hit.shape, F32)
    for j in range(route.shape[1]):
        named = named + (lane == route[:, j : j + 1]).astype(F32)
    hit[...] = named

    def norm_first(i):
        h = tok[i].astype(F32)
        n1 = h * lax.rsqrt(jnp.mean(h * h, axis=-1, keepdims=True) + epsilon)
        x1[i] = (n1 * gain_attn).astype(BF)

    norm_first(0)
    spread(1).wait_recv()
    norm_first(1)
    for i in range(2, n_shard, 2):
        spread(i).wait_recv()
        spread(i + 1).start()
        norm_first(i)
    for i in range(3, n_shard, 2):
        spread(i).wait_recv()
        norm_first(i)
    for b in range(1, n_shard):
        w_copy(me ^ b).wait_recv()

    spread_dy = spread_sends(dy_hbm, dy_out, d_send, d_recv, n_shard)
    for i in list(range(2, n_shard, 2)) + [1]:
        spread_dy(i).start()

    keeps = []

    def keep(e, slot):
        copy = pltpu.make_async_copy(
            cstage.at[slot, me], w_out.at[me, :, block_cols(e, cut)], o_sem.at[14 + e]
        )
        copy.start()
        keeps.append(copy)

    for e in range(head):
        columns.prepare(e, keep)

    def spread_gain(row):
        hd = HEAD_DIM // n_shard
        total = small[row : row + 1, :HEAD_DIM]
        for j in range(1, n_shard):
            part = small[row : row + 1, j * rows : j * rows + HEAD_DIM]
            total = total + pltpu.roll(part, j * hd, 1)
        return total.astype(BF).astype(F32)

    gain_q = spread_gain(experts + 2)
    gain_k = spread_gain(experts + 3)
    gain[...] = jnp.concatenate([gain_q, gain_k, jnp.zeros((6, HEAD_DIM), F32)], axis=0)
    cosine, sine = (table[0], table[1])

    def turned(x, gain):
        hat = x * lax.rsqrt(jnp.mean(x * x, axis=-1, keepdims=True) + epsilon) * gain
        return (hat * cosine + pltpu.roll(hat, HEAD_DIM // 2, 1) * sine).astype(BF)

    def two_sequences(i, carry):
        y = jnp.dot(
            x1[pl.ds(2 * i, 2)].reshape(2 * seq, width), wqkv[...], preferred_element_type=F32
        )
        r2 = block_cols(i, 2 * seq)
        q[r2, :] = y[:, :cols]
        k[r2, :] = y[:, cols : 2 * cols]
        qkvr[2, r2, :] = y[:, 2 * cols :].astype(BF)
        for j in range(2):
            r = block_cols(2 * i + j, seq)
            row = jnp.broadcast_to(seg[2 * i + j].astype(F32), (seq, seq))
            same = row == row.T
            for n in range(heads):
                c = slice(n * HEAD_DIM, (n + 1) * HEAD_DIM)
                qr = turned(q[r, c], gain_q)
                kr = turned(k[r, c], gain_k)
                qkvr[0, r, c] = qr
                qkvr[1, r, c] = kr
                s = jnp.where(same, dot(qr, kr, ((1,), (1,))) * scale, -1000000000.0)
                e = jnp.exp(s - jnp.max(s, axis=-1, keepdims=True))
                p = e / jnp.sum(e, axis=-1, keepdims=True)
                a[r, c] = dot(p.astype(BF), qkvr[2, r, c], ((1,), (0,))).astype(BF)
        return carry

    lax.fori_loop(0, half, two_sequences, 0)
    stores = [
        (q, q_out), (k, k_out), (qkvr, qkvr_out), (a, a_out), (x1, x1_out), (wqkv, wqkv_out),
        (wo, wo_out), (seg, seg_out), (small, small_out), (hit, hit_out),
        (gain, gain_out),
    ]
    stores = [pltpu.make_async_copy(x, y, o_sem.at[i]) for i, (x, y) in enumerate(stores)]

    def out_block(parity, j):
        lhs = a[...].reshape(half, 2, seq, cols)[:, parity].reshape(half * seq, cols)
        return dot(lhs, wo[:, block_cols(j, rows)], ((1,), (0,)))

    send, finish = scatter_blocks(
        out_block, width, rows, stage, in1, in2, acc, None, (rs_j, rr_j, rs_b, rr_b, None)
    )
    send()
    for i in range(2, n_shard, 2):
        spread_dy(i).wait_recv()
        spread_dy(i + 1).start()
    finish()
    h1 = tok[0].astype(F32) + acc[...]
    acc[...] = h1
    n2 = h1 * lax.rsqrt(jnp.mean(h1 * h1, axis=-1, keepdims=True) + epsilon)
    x2[...] = (n2 * small[1:2, :].astype(BF).astype(F32)).astype(BF)
    spread_x2 = spread_sends(x2, x2_out, x_send, x_recv, n_shard)
    for i in list(range(2, n_shard, 2)) + [1]:
        spread_x2(i).start()
    own = pltpu.make_async_copy(x2, x2_out.at[0], o_sem.at[11])
    own.start()
    lane = lax.broadcasted_iota(jnp.int32, (seq, 16), 1)
    z = dot(x2[...], small[...].astype(BF), ((1,), (1,)))
    valid = (lane >= 2) & (lane < experts + 2)
    z = jnp.where(valid, z, -1e30)
    e = jnp.exp(z - jnp.max(z, axis=-1, keepdims=True))
    probs = e / jnp.sum(e, axis=-1, keepdims=True)
    probs = jnp.concatenate([probs, jnp.zeros((seq, gate.shape[1] - 16), F32)], axis=1)
    probs = pltpu.roll(probs, gate.shape[1] - 2, 1)
    pr[...] = probs
    gate[...] = probs * hit[...]

    def gate_copy(b):
        return remote(gate, gate_out.at[b], g_send.at[b], g_recv.at[b], peer(b))

    for b in range(1, n_shard):
        gate_copy(b).start()
    more = [(gate, gate_out.at[0]), (pr, pr_out)]
    more = [pltpu.make_async_copy(x, y, o_sem.at[12 + i]) for i, (x, y) in enumerate(more)]
    last = pltpu.make_async_copy(acc, h1_out, ld_sem.at[0])
    for copy in (*stores, *more, last):
        copy.start()
    for i in range(2, n_shard, 2):
        spread_x2(i).wait_recv()
        spread_x2(i + 1).start()
    for i in range(1, n_shard, 2):
        spread_x2(i).wait_recv()
        spread_dy(i).wait_recv()
    for b in range(1, n_shard):
        gate_copy(b).wait()
        spread(b).wait_send()
        spread_dy(b).wait_send()
        spread_x2(b).wait_send()
        w_copy(me ^ b).wait_send()
    for e in range(head):
        columns.arrived(e)
        columns.sent(e)
    dy_own.wait()
    for copy in (own, *stores, *more, last, *keeps):
        copy.wait()


def forward_call(
    tok, small, seg, route, dy, wq, wk, wv, wo, table, w_gate, w_up, n_rep, n_shard, head
):
    seq, width = tok.shape
    experts = w_gate.shape[0]
    rows, half, tokens = width // n_shard, n_shard // 2, n_shard * seq
    cols = rows
    dma = pltpu.SemaphoreType.DMA
    anyspec = pl.BlockSpec(memory_space=pl.ANY)
    shape = jax.ShapeDtypeStruct
    group = (n_shard, seq, width)
    lanes = (seq, 128)
    return pl.pallas_call(
        partial(forward_kernel, n_rep, n_shard, experts, head),
        out_shape=(
            shape(group, BF),
            shape(group, BF),
            shape(group, BF),
            shape((n_shard,) + lanes, F32),
            shape((n_shard, rows, head * cols), BF),
            shape((width, 3 * cols), BF),
            shape((rows, width), BF),
            shape((3, tokens, cols), BF),
            shape((tokens, cols), F32),
            shape((tokens, cols), F32),
            shape((tokens, cols), BF),
            shape((n_shard,) + seg.shape, seg.dtype),
            shape((seq, width), F32),
            shape(lanes, F32),
            shape((16, width), F32),
            shape(lanes, F32),
            shape((8, HEAD_DIM), F32),
        ),
        in_specs=[anyspec] * 12,
        out_specs=(anyspec,) * 17,
        scratch_shapes=[
            pltpu.VMEM(group, BF),
            pltpu.VMEM((16, width), F32),
            pltpu.VMEM((n_shard,) + seg.shape, seg.dtype),
            pltpu.VMEM(lanes, F32),
            pltpu.VMEM((8, HEAD_DIM), F32),
            pltpu.VMEM(route.shape, route.dtype),
            pltpu.VMEM((3, rows, width), F32),
            pltpu.VMEM((rows, width), F32),
            pltpu.VMEM(table.shape, F32),
            pltpu.VMEM(group, BF),
            pltpu.VMEM((width, 3 * cols), BF),
            pltpu.VMEM((n_shard, rows, 3 * cols), BF),
            pltpu.VMEM((rows, width), BF),
            pltpu.VMEM((3, tokens, cols), BF),
            pltpu.VMEM((tokens, cols), F32),
            pltpu.VMEM((tokens, cols), F32),
            pltpu.VMEM((tokens, cols), BF),
            pltpu.VMEM((seq, width), BF),
            pltpu.VMEM(lanes, F32),
            pltpu.VMEM(lanes, F32),
            pltpu.VMEM((half, seq, width), BF),
            pltpu.VMEM((half, seq, width), BF),
            pltpu.VMEM((half - 1, seq, width), BF),
            pltpu.VMEM((seq, width), F32),
            pltpu.VMEM((2, 2) + w_gate.shape[1:], F32),
            pltpu.VMEM((2, n_shard, rows, cols), BF),
            dma((10,)),
        ]
        + [dma((n_shard,)) for _ in range(14)]
        + [
            dma((2, 2)),
            dma((2, n_shard)),
            dma((head, n_shard)),
            dma((14 + head,)),
            dma((n_shard,)),
            dma((n_shard,)),
            dma((half,)),
            dma((half,)),
        ],
        compiler_params=pltpu.CompilerParams(
            collective_id=3, has_side_effects=True, vmem_limit_bytes=67000000
        ),
        name="forward",
    )(tok, small, seg, route, dy, wq, wk, wv, wo, table, w_gate, w_up)


def unpack_kernel(n_shard, d, ga, gb, w0, w1, w2, w3, gate, up, down, o0, o1, o2, o3):
    rows, hidden = gate.shape[1:]
    f_loc = hidden // n_shard
    cols = 2 * f_loc
    half = n_shard // 2
    x = (ga, gb)
    for j in range(n_shard):
        r = slice((j % half) * rows, (j % half + 1) * rows)
        gate[0, :, j * f_loc : (j + 1) * f_loc] = x[j // half][0, r, :f_loc].astype(F32)
        up[0, :, j * f_loc : (j + 1) * f_loc] = x[j // half][0, r, f_loc:].astype(F32)
    for j in range(down.shape[2] // cols):
        down[0, :, j * cols : (j + 1) * cols] = d[0, j * f_loc : (j + 1) * f_loc, :].astype(F32)

    @pl.when(pl.program_id(0) < half)
    def _():
        for w, out in ((w0, o0), (w1, o1), (w2, o2), (w3, o3)):
            for j in range(2):
                out[:, j * cols : (j + 1) * cols] = w[0, j * rows : (j + 1) * rows, :].astype(F32)


def unpack(total, experts, n_shard):
    depth, cols = total.shape[1:]
    width, f_loc, half = 2 * depth, cols // 2, n_shard // 2
    rows = width // n_shard
    hidden = n_shard * f_loc
    step = half // 2
    first = 3 * experts
    shape = jax.ShapeDtypeStruct
    one = lambda e: jnp.minimum(e, experts - 1)
    two = lambda e: jnp.minimum(e, half - 1)
    by = lambda e: (one(e), 0, 0)

    def unit(i):
        return pl.BlockSpec(
            (1, 2 * rows, cols),
            lambda e: (first + 2 * i + two(e) // step, lax.rem(two(e), step), 0),
        )

    return pl.pallas_call(
        partial(unpack_kernel, n_shard),
        grid=(max(experts, half),),
        out_shape=(
            shape((experts, rows, hidden), F32),
            shape((experts, rows, hidden), F32),
            shape((experts, f_loc, width), F32),
        )
        + (shape((rows, width), F32),) * 4,
        in_specs=[
            pl.BlockSpec((1, depth, cols), lambda e: (down_at(one(e)), 0, 0)),
            pl.BlockSpec((1, depth, cols), lambda e: (gate_up_at(one(e), experts), 0, 0)),
            pl.BlockSpec((1, depth, cols), lambda e: (gate_up_at(one(e), experts) + 1, 0, 0)),
        ]
        + [unit(i) for i in range(4)],
        out_specs=(
            pl.BlockSpec((1, rows, hidden), by),
            pl.BlockSpec((1, rows, hidden), by),
            pl.BlockSpec((1, f_loc, width), by),
        )
        + (pl.BlockSpec((rows, 2 * cols), lambda e: (0, two(e))),) * 4,
        compiler_params=pltpu.CompilerParams(vmem_limit_bytes=48 << 20),
        name="unpack",
    )(*([total] * 7))


def shards(
    tokens, segments, routes, slot_ids, attn_gain, w_query, w_key, w_value, w_out,
    query_gain, key_gain, ffn_gain, router, w_gate, w_up, w_down, cotangent,
):
    n_shard = lax.axis_size("shard")
    me = lax.axis_index("shard")
    seq, width = tokens.shape
    experts, rows, hidden_f = w_gate.shape
    f_loc = w_down.shape[1]
    cols = width // n_shard
    group = n_shard * seq
    n_rep = lax.axis_size("rep")
    hd = HEAD_DIM // n_shard

    row = jnp.arange(16)[:, None]

    def wide(g):
        return jnp.pad(g, (0, rows - g.shape[0]))[None]

    small = jnp.pad(router.T, ((2, 14 - experts), (0, 0)))
    for i, g in (
        (0, attn_gain), (1, ffn_gain), (experts + 2, query_gain), (experts + 3, key_gain)
    ):
        small = jnp.where(row == i, wide(g), small)
    cosine, sine = rope_tables(seq, HEAD_DIM)
    cos2, sin2 = (cosine[:, 0], sine[:, 0])
    table = jnp.stack(
        [jnp.concatenate([cos2, cos2], axis=1), jnp.concatenate([-sin2, sin2], axis=1)]
    )
    (
        x1_all, x2_all, dy_all, gate_all, gu, qkv, w_out_b, qkvr, q, k, a, seg_all, h1, pr, small,
        hit, gains,
    ) = forward_call(
        tokens, small, segments.reshape(1, seq), routes, cotangent, w_query, w_key, w_value, w_out, table,
        w_gate, w_up, n_rep, n_shard, HEAD_EXPERTS,
    )
    part, into1, into2, total, gh, da, dh1, pay, w_down_b = experts_call(
        x2_all.reshape(group, width), dy_all.reshape(group, width), gate_all.reshape(group, -1),
        gu, w_down, w_gate, w_up, h1, pr, hit, small, n_rep, n_shard,
    )
    part, _, _, total, grad_tokens, output, sums = attention_call(
        da, x1_all, a, qkv, w_out_b, qkvr, q, k, seg_all, table,
        gains, gh, w_down_b, tokens, pay, h1, dh1,
        small, part, into1, into2, total,
        n_rep, n_shard, HEAD_UNITS if n_rep == 4 else 0,
    )
    summed = total if n_rep == 4 else lax.psum(part, "rep")
    gw_gate, gw_up, gw_down, gw_out, gw_value, gw_key, gw_query = unpack(
        summed, experts, n_shard
    )
    small = sums
    gg_query = lax.dynamic_slice(small[experts + 2, :HEAD_DIM], (me * hd,), (hd,))
    gg_key = lax.dynamic_slice(small[experts + 3, :HEAD_DIM], (me * hd,), (hd,))
    return (
        output,
        grad_tokens,
        small[0],
        gw_query,
        gw_key,
        gw_value,
        gw_out,
        gg_query,
        gg_key,
        small[1],
        small[2 : experts + 2].T,
        gw_gate,
        gw_up,
        gw_down,
    )


def solution(mesh):
    both = P(("rep", "shard"), None)
    row = P("shard", None)
    vec = P("shard")
    exp = P(None, "shard", None)
    return jax.shard_map(
        shards,
        mesh=mesh,
        in_specs=(
            both, P(("rep", "shard")), both, both, vec, row, row, row, row,
            vec, vec, vec, row, exp, exp, exp, both,
        ),
        out_specs=(both, both, vec, row, row, row, row, vec, vec, vec, row, exp, exp, exp),
        check_vma=False,
    )
```
